256 devices in a mesh: dom: 64 (over z, y, core), st: 4 (over x).
Axes of the slice: x: 4, y: 4, z: 8, core: 2. Of those that a mesh axis runs over, the one named last changes fastest.
Arguments:
- orbitals: float32 [64, 512, 32, 128], P('st', 'dom'), may hold values from -6 to 6
- levels: float32 [64], P('st'), may hold values from -2 to -0.5
- potential: float32 [512, 32, 128], P('dom'), may hold values from 0 to 2
- perturbation: float32 [512, 32, 128], P('dom'), may hold values from -3 to 3
- projector: float32 [526336], P('dom'), may hold values from -1.5 to 1.5
- point_cell: int32 [526336], P('dom'), may hold values from 0 to 32767, as said below
- point_atom: int32 [526336], P('dom'), may hold values from -1 to 1023, as said below
- kb_energy: float32 [1024], replicated, may hold values from 1 to 4
Outputs:
- response: float32 [64, 512, 32, 128], P('st', 'dom')
- density: float32 [512, 32, 128], P('dom', 'st')
The draws below stay inside these ranges and needn't reach their ends.
Inputs may be any that keep to these rules, and one draw needn't show every extreme that they name: `point_cell`: within the domain's block of 8 x 32 x 128 cells in row-major order; 0 in unused slots. `point_atom`: -1 marks an unused slot, and a domain's unused slots come after its used ones; atom a has its centre in domain a // 16, and its slots lie in that domain or in the two beside it; no two used slots of a domain share both cell and atom.
All inputs are finite; a program needn't handle non-finite values.
Results may differ from the reference program's by a relative error of at most 0.0001.
Values sent between devices are 32-bit elements; how exact they have to be, the bound alone decides.
A program may use at most 128 MiB of HBM per device.

```python
import math
import jax
import jax.numpy as jnp
import numpy as np
from jax import lax

SX = 8
NY = 32
NZ = 128
STATES = 64
ATOM_DEV = 16
RADIUS = 4
SPHERE = 257
ITERS = 4
NX = 512
ATOMS = 1024
PTS_DEV = 8224
N_DOM = 64


def sphere_table():
    offsets = []
    for first in range(-RADIUS, RADIUS + 1):
        for second in range(-RADIUS, RADIUS + 1):
            for third in range(-RADIUS, RADIUS + 1):
                if first * first + second * second + third * third <= RADIUS * RADIUS:
                    offsets.append((first, second, third))
    return np.array(offsets, dtype=np.int32)


def point_lists(key):
    base = jax.random.fold_in(key, 11)
    key_first, key_second, key_third = jax.random.split(base, 3)
    owner = jnp.arange(ATOMS, dtype=jnp.int32) // ATOM_DEV
    centre_first = owner * SX + jax.random.randint(key_first, (ATOMS,), 0, SX)
    centre_second = jax.random.randint(key_second, (ATOMS,), 0, NY)
    centre_third = jax.random.randint(key_third, (ATOMS,), 0, NZ)
    table = jnp.asarray(sphere_table())
    grid_first = centre_first[:, None] + table[None, :, 0]
    grid_second = centre_second[:, None] + table[None, :, 1]
    grid_third = centre_third[:, None] + table[None, :, 2]
    inside = (grid_first >= 0) & (grid_first < NX) & (grid_second >= 0) & (grid_second < NY) & (grid_third >= 0) & (grid_third < NZ)
    domain = jnp.floor_divide(grid_first, SX)
    cell = (grid_first - domain * SX) * (NY * NZ) + grid_second * NZ + grid_third
    atom = jnp.broadcast_to(jnp.arange(ATOMS, dtype=jnp.int32)[:, None], grid_first.shape)

    def padded(values, filler):
        return jnp.pad(values.astype(jnp.int32), ((ATOM_DEV, ATOM_DEV), (0, 0)), constant_values=filler)
    cells_pad = padded(cell, 0)
    atoms_pad = padded(atom, -1)
    domain_pad = padded(domain, -2)
    inside_pad = padded(inside.astype(jnp.int32), 0)

    def one_domain(index):

        def taken(values):
            return lax.dynamic_slice(values, (index * ATOM_DEV, jnp.int32(0)), (3 * ATOM_DEV, SPHERE)).reshape(-1)
        live = (taken(inside_pad) == 1) & (taken(domain_pad) == index)
        order = jnp.argsort(jnp.where(live, 0, 1).astype(jnp.int32), stable=True)[:PTS_DEV]
        kept = live[order]
        return (jnp.where(kept, taken(cells_pad)[order], 0), jnp.where(kept, taken(atoms_pad)[order], -1))
    cells_all, atoms_all = jax.vmap(one_domain)(jnp.arange(N_DOM, dtype=jnp.int32))
    return (cells_all.reshape(-1).astype(jnp.int32), atoms_all.reshape(-1).astype(jnp.int32))


def draw_point_cell(key, part):
    return point_lists(key)[0]


def draw_point_atom(key, part):
    return point_lists(key)[1]


def draw_perturbation(key, part):
    base = jax.random.fold_in(key, 23)
    ramp = jnp.arange(NX, dtype=jnp.float32) / max(NX - 1, 1)
    envelope = 0.25 * (1.0 + 2.0 * ramp)
    values = jnp.clip(jax.random.normal(base, (NX, NY, NZ), jnp.float32), -4.0, 4.0) * envelope[:, None, None]
    return values.astype(jnp.float32)


def block_scale(key, dims, pieces, low, largest):
    factor_of = 1.0
    for dim, parts in pieces:
        draws = jax.random.uniform(jax.random.fold_in(jax.random.fold_in(key, 6), dim), (parts,), jnp.float32, low / len(pieces), largest / len(pieces))
        factor_of = factor_of * jnp.repeat(jnp.exp(draws), dims[dim] // parts).reshape((-1,) + (1,) * (len(dims) - 1 - dim))
    return factor_of


def scatter_about(rng, extent, width, reach, cuts=(), held_as=jnp.bfloat16):
    factor_of = block_scale(rng, extent, cuts, -0.22, 0.18) if cuts else 1.0
    values = jax.random.normal(rng, extent, jnp.float32) * width * factor_of
    return jnp.minimum(jnp.maximum(values, -reach), reach).astype(held_as)


def setup_inputs(seed: int = 0) -> dict:
    key_list = jax.random.split(jax.random.key(seed), 9)
    orbitals = scatter_about(key_list[0], (STATES, NX, NY, NZ), 1.0, 6.0, ((0, 4), (1, 64)), jnp.float32)
    levels = jnp.clip(-2.0 + 1.5 * jax.random.uniform(key_list[1], (STATES,), jnp.float32) ** block_scale(key_list[1], (STATES,), ((0, 4),), -0.2, 0.2), -2.0, -0.5)
    potential = jnp.clip(2.0 * jax.random.uniform(key_list[2], (NX, NY, NZ), jnp.float32) ** block_scale(key_list[2], (NX, NY, NZ), ((0, 64),), -0.2, 0.2), 0.0, 2.0)
    perturbation = draw_perturbation(jax.random.fold_in(key_list[8], 71), 0)
    projector = scatter_about(key_list[4], (N_DOM * PTS_DEV,), 0.25, 1.5, ((0, 64),), jnp.float32)
    point_cell = draw_point_cell(jax.random.fold_in(key_list[8], 71), 0)
    point_atom = draw_point_atom(jax.random.fold_in(key_list[8], 71), 0)
    kb_energy = jnp.clip(jnp.exp(jax.random.uniform(key_list[7], (ATOMS,), jnp.float32, math.log(1.0), math.log(4.0))), 1.0, 4.0)
    return {"orbitals": orbitals, "levels": levels, "potential": potential, "perturbation": perturbation, "projector": projector, "point_cell": point_cell, "point_atom": point_atom, "kb_energy": kb_energy}


STENCIL = (-5369.0 / 1800.0, 12.0 / 7.0, -15.0 / 56.0, 10.0 / 189.0, -1.0 / 112.0, 2.0 / 1925.0, -1.0 / 16632.0)


def laplace(field):
    first, second, third = field.shape
    padded = jnp.pad(field, 6)
    result = 3.0 * STENCIL[0] * field
    for shift in range(1, 7):
        lower = 6 - shift
        upper = 6 + shift
        beside_all = (padded[upper:upper + first, 6:6 + second, 6:6 + third]
                  + padded[lower:lower + first, 6:6 + second, 6:6 + third]
                  + padded[6:6 + first, upper:upper + second, 6:6 + third]
                  + padded[6:6 + first, lower:lower + second, 6:6 + third]
                  + padded[6:6 + first, 6:6 + second, upper:upper + third]
                  + padded[6:6 + first, 6:6 + second, lower:lower + third])
        result = result + STENCIL[shift] * beside_all
    return result


def reference(orbitals, levels, potential, perturbation, projector, point_cell, point_atom, kb_energy):
    cells = SX * NY * NZ
    domains = jnp.arange(N_DOM * PTS_DEV, dtype=jnp.int32) // PTS_DEV
    places = (domains * cells + point_cell).astype(jnp.int32)
    segment = jnp.where(point_atom >= 0, point_atom, ATOMS).astype(jnp.int32)
    energies = jnp.concatenate([kb_energy, jnp.zeros((1,), kb_energy.dtype)])

    def operate(field, level):
        flat = field.reshape(-1)
        picked = flat[places] * projector
        totals = jax.ops.segment_sum(picked, segment, num_segments=ATOMS + 1)
        spread = (totals * energies)[segment] * projector
        projected = jnp.zeros_like(flat).at[places].add(spread).reshape(field.shape)
        return -0.5 * laplace(field) + (potential - level) * field + projected

    def solve(item):
        wave, level = item
        right = -perturbation * wave
        solution = jnp.zeros_like(right)
        residual = right
        direction = right
        norm_now = jnp.sum(residual * residual)
        for turn in range(ITERS):
            image = operate(direction, level)
            alpha = norm_now / jnp.sum(direction * image)
            solution = solution + alpha * direction
            residual = residual - alpha * image
            norm_next = jnp.sum(residual * residual)
            direction = residual + (norm_next / norm_now) * direction
            norm_now = norm_next
        return solution

    answer = lax.map(solve, (orbitals, levels))
    density = 4.0 * jnp.sum(orbitals * answer, axis=0)
    return answer, density
```

```python
import numpy as np
import jax
import jax.numpy as jnp
from jax import lax
from jax.experimental import pallas as pl
from jax.experimental.pallas import tpu as pltpu
from jax.sharding import PartitionSpec as P

ATOM_DEV = 16
SLOTS = 3 * ATOM_DEV
SX, NY, NZ = 8, 32, 128
HALO = 6
EXT = SX + 2 * HALO
NYP = NY + 2 * HALO
N_DOM = 64
PLANE = 8
DEPTH = 8
C = (
    -5369.0 / 1800.0,
    12.0 / 7.0,
    -15.0 / 56.0,
    10.0 / 189.0,
    -1.0 / 112.0,
    2.0 / 1925.0,
    -1.0 / 16632.0,
)
F32 = jnp.float32
BF16 = jnp.bfloat16
UNROLL = 8


def depth_matrix():
    lag = np.abs(np.arange(NZ)[:, None] - np.arange(NZ)[None, :])
    band = np.zeros((NZ, NZ), np.float32)
    for k in range(1, 7):
        band[lag == k] = -0.5 * C[k]
    high = band.astype(jnp.bfloat16)
    low = (band - high.astype(np.float32)).astype(jnp.bfloat16)
    half = np.concatenate([high, low], axis=1)
    return np.concatenate([half, half], axis=0)


def both_parts(value, axis):
    high = value.astype(BF16).astype(F32)
    return jnp.concatenate([high, value - high], axis=axis).astype(BF16)


def table_kernel(cell, atom, value, table, dense):
    first = (lax.axis_index("dom") - 1) * ATOM_DEV
    slots = cell.shape[0]

    def clear(i, _):
        dense[pl.ds(pl.multiple_of(i * 64, 64), 64), :] = jnp.zeros((64, NZ), F32)
        return 0

    lax.fori_loop(0, dense.shape[0] // 64, clear, 0)

    def halve(_, ends):
        low, high = ends
        mid = (low + high) // 2
        used = atom[jnp.minimum(mid, slots - 1)] >= 0
        go = low < high
        return (
            jnp.where(go & used, mid + 1, low),
            jnp.where(go & jnp.logical_not(used), mid, high),
        )

    used, _ = lax.fori_loop(0, 15, halve, (jnp.int32(0), jnp.int32(slots)))
    lanes = lax.broadcasted_iota(jnp.int32, (1, NZ), 1)

    def put(i, _):
        for u in range(UNROLL):
            s = i * UNROLL + u
            c = cell[s]
            a = atom[s] - first
            live = s < used
            row = jnp.where(live, (c >> 7) * SLOTS + a, 0)
            lane = jnp.where(live, c & 127, -1)
            pltpu.store(
                dense.at[pl.ds(row, 1), :],
                jnp.full((1, NZ), value[s], F32),
                mask=lanes == lane,
            )
        return 0

    lax.fori_loop(0, (used + UNROLL - 1) // UNROLL, put, 0)

    def split(i, _):
        table[i] = both_parts(dense[pl.ds(pl.multiple_of(i * SLOTS, SLOTS), SLOTS), :], 0)
        return 0

    lax.fori_loop(0, SX * NY, split, 0)


def build_table(projector, point_cell, point_atom):
    smem = pl.BlockSpec(memory_space=pltpu.SMEM)
    return pl.pallas_call(
        table_kernel,
        out_shape=jax.ShapeDtypeStruct((SX * NY, 2 * SLOTS, NZ), BF16),
        in_specs=[smem, smem, smem],
        out_specs=pl.BlockSpec(memory_space=pltpu.VMEM),
        scratch_shapes=[pltpu.VMEM((SX * NY * SLOTS, NZ), F32)],
        compiler_params=pltpu.CompilerParams(vmem_limit_bytes=40 * 2**20),
        cost_estimate=pl.CostEstimate(flops=0, bytes_accessed=40 * 2**20, transcendentals=0),
        name="projector_table",
    )(point_cell, point_atom, projector)


def solve_kernel(
    own_in, low_in, high_in, table_in, pot_in, lev, energy, tz,
    x_out,
    r, s, w, hb, hb2, hist, table, potb, st1, st2, pj, msg, pmsg, scal, tot, lhs,
    sem_in, h_send, h_recv, a_send, a_recv, b_send, b_recv, p_send, p_recv,
):
    d = lax.axis_index("dom")
    zi = d // PLANE
    ji = d % PLANE
    inner = pl.ds(HALO, NY)

    loads = []
    for g in range(2):
        loads += [
            pltpu.make_async_copy(own_in.at[:, g], r.at[g, pl.ds(HALO, SX), inner], sem_in.at[4 * g]),
            pltpu.make_async_copy(low_in.at[:, g], r.at[g, pl.ds(0, HALO), inner], sem_in.at[4 * g + 1]),
            pltpu.make_async_copy(high_in.at[:, g], r.at[g, pl.ds(HALO + SX, HALO), inner], sem_in.at[4 * g + 2]),
            pltpu.make_async_copy(own_in.at[:, g], hist.at[0, g], sem_in.at[4 * g + 3]),
        ]
    loads.append(pltpu.make_async_copy(table_in, table, sem_in.at[8]))
    for c in loads:
        c.start()

    zero = jnp.zeros((HALO, 8, NZ), F32)

    def clear(i, _):
        for g in range(2):
            r[g, i, pl.ds(0, HALO)] = zero
            r[g, i, pl.ds(HALO + NY, HALO)] = zero
        return 0

    lax.fori_loop(0, EXT, clear, 0)

    def clear_halo(base):
        plane = jnp.zeros((NY, 8, NZ), F32)

        def one(i, _):
            for k in range(2):
                for g in range(2):
                    hb[k, g, base + i] = plane
            for g in range(2):
                hb2[g, i] = plane
            return 0

        lax.fori_loop(0, HALO, one, 0)

    @pl.when(d == 0)
    def _():
        clear_halo(0)

    @pl.when(d == N_DOM - 1)
    def _():
        clear_halo(HALO)

    for k in range(4):
        for g in range(2):
            pj[k, g] = jnp.zeros((4, 8, NZ), F32)

    near = ((-2, d >= 2), (-1, d >= 1), (1, d < N_DOM - 1), (2, d < N_DOM - 2))

    def in_plane(i):
        return zi * PLANE + (ji + i) % PLANE

    def in_column(i):
        return ((zi + i) % DEPTH) * PLANE + ji

    barrier = pltpu.get_barrier_semaphore()
    count = jnp.int32(PLANE - 1 + DEPTH - 1)
    for i in range(1, PLANE):
        pl.semaphore_signal(barrier, inc=1, device_id={"dom": in_plane(i)})
    for i in range(1, DEPTH):
        pl.semaphore_signal(barrier, inc=1, device_id={"dom": in_column(i)})
    for step, there in near:
        count = count + there.astype(jnp.int32)

        @pl.when(there)
        def _(step=step):
            pl.semaphore_signal(barrier, inc=1, device_id={"dom": d + step})

    lanes = lax.broadcasted_iota(jnp.int32, (8, NZ), 1)

    def spread(i, _):
        rows = pot_in[pl.ds(pl.multiple_of(i * 8, 8), 8), :]
        for j in range(8):
            potb[i * 8 + j] = jnp.broadcast_to(rows[j : j + 1, :], (8, NZ))
        return 0

    lax.fori_loop(0, SX * NY // 8, spread, 0)
    pl.semaphore_wait(barrier, count)

    def project(blocks, row, acc):
        left = jnp.concatenate([both_parts(b, 0) for b in blocks], axis=1)
        right = jnp.concatenate([table[row + j] for j in range(len(blocks))], axis=1)
        return acc + lax.dot_general(
            left, right, (((1,), (1,)), ((), ())), preferred_element_type=F32
        )

    def near_copy(k, g, n):
        step = near[n][0]
        return pltpu.make_async_remote_copy(
            src_ref=pmsg.at[k, g],
            dst_ref=pj.at[k, g, 3 - n],
            send_sem=p_send.at[g, n],
            recv_sem=p_recv.at[k % 2, g, 3 - n],
            device_id={"dom": d + step},
        )

    def near_arrival(k, g, n):
        return pltpu.make_async_remote_copy(
            src_ref=pmsg.at[k, g],
            dst_ref=pj.at[k, g, n],
            send_sem=p_send.at[g, n],
            recv_sem=p_recv.at[k % 2, g, n],
            device_id={"dom": d + near[n][0]},
        )

    def send_projections(k, g, acc):
        part = acc[:8, :SLOTS] + acc[8:, :SLOTS] + acc[:8, SLOTS:] + acc[8:, SLOTS:]
        pmsg[k, g] = jnp.concatenate([part, jnp.zeros((8, NZ - SLOTS), F32)], axis=1)
        for n in range(4):

            @pl.when(near[n][1])
            def _(n=n):
                near_copy(k, g, n).start()

    def gathered_projections(k, g):
        for n in range(4):

            @pl.when(near[n][1])
            def _(n=n):
                near_arrival(k, g, n).wait_recv()
                near_copy(k, g, n).wait_send()

        total = pmsg[k, g]
        shifts = ((2 * ATOM_DEV, 0, 16), (ATOM_DEV, 0, 32), (-ATOM_DEV, 16, 48), (-2 * ATOM_DEV, 32, 48))
        for n, (back, low, high) in enumerate(shifts):
            moved = pltpu.roll(pj[k, g, n], (-back) % NZ, 1)
            total = total + jnp.where((lanes >= low) & (lanes < high), moved, 0.0)
        return total

    def plane_copy(k, g, i):
        return pltpu.make_async_remote_copy(
            src_ref=msg.at[k, g, 0],
            dst_ref=st1.at[k, g, ji],
            send_sem=a_send.at[g, i],
            recv_sem=a_recv.at[k % 2, g, i],
            device_id={"dom": in_plane(i)},
        )

    def plane_arrival(k, g, i):
        return pltpu.make_async_remote_copy(
            src_ref=msg.at[k, g, 0],
            dst_ref=st1.at[k, g, (ji + PLANE - i) % PLANE],
            send_sem=a_send.at[g, i],
            recv_sem=a_recv.at[k % 2, g, i],
            device_id={"dom": in_plane(i)},
        )

    def column_copy(k, g, i):
        return pltpu.make_async_remote_copy(
            src_ref=msg.at[k, g, 1],
            dst_ref=st2.at[k, g, zi],
            send_sem=b_send.at[g, i],
            recv_sem=b_recv.at[k % 2, g, i],
            device_id={"dom": in_column(i)},
        )

    def column_arrival(k, g, i):
        return pltpu.make_async_remote_copy(
            src_ref=msg.at[k, g, 1],
            dst_ref=st2.at[k, g, (zi + DEPTH - i) % DEPTH],
            send_sem=b_send.at[g, i],
            recv_sem=b_recv.at[k % 2, g, i],
            device_id={"dom": in_column(i)},
        )

    def send_sums(k, g, rr, rw):
        tile = jnp.where(
            lanes < 64, jnp.sum(rr, axis=1, keepdims=True), jnp.sum(rw, axis=1, keepdims=True)
        )
        msg[k, g, 0] = tile
        st1[k, g, ji] = tile
        for i in range(1, PLANE):
            plane_copy(k, g, i).start()

    def forward_sums(k, g):
        for i in range(1, PLANE):
            plane_arrival(k, g, i).wait_recv()
            plane_copy(k, g, i).wait_send()
        tile = st1[k, g, 0]
        for i in range(1, PLANE):
            tile = tile + st1[k, g, i]
        msg[k, g, 1] = tile
        st2[k, g, zi] = tile
        for i in range(1, DEPTH):
            column_copy(k, g, i).start()

    def take_sums(k, g):
        for i in range(1, DEPTH):
            column_arrival(k, g, i).wait_recv()
            column_copy(k, g, i).wait_send()
        tile = st2[k, g, 0]
        for i in range(1, DEPTH):
            tile = tile + st2[k, g, i]
        rr = jnp.broadcast_to(tile[:, 0:1], (8, NZ))
        rw = jnp.broadcast_to(tile[:, 64:65], (8, NZ))
        scal[g, 8 + k] = rr
        if k == 0:
            alpha, beta = rr / rw, jnp.zeros_like(rr)
        else:
            beta = rr / scal[g, 7 + k]
            alpha = rr / (rw - beta * rr / scal[g, k - 1])
        scal[g, k] = alpha
        scal[g, 4 + k] = beta
        return alpha, beta

    def up_copy(k, g):
        dst = hb.at[k, g, pl.ds(0, HALO)] if k < 2 else hb2.at[g]
        return pltpu.make_async_remote_copy(
            src_ref=w.at[k % 2, g, pl.ds(SX - HALO, HALO)],
            dst_ref=dst,
            send_sem=h_send.at[k, g, 0],
            recv_sem=h_recv.at[k, g, 0],
            device_id={"dom": d + 1},
        )

    def down_copy(k, g):
        dst = hb.at[k, g, pl.ds(HALO, HALO)] if k < 2 else hb2.at[g]
        return pltpu.make_async_remote_copy(
            src_ref=w.at[k % 2, g, pl.ds(0, HALO)],
            dst_ref=dst,
            send_sem=h_send.at[k, g, 1],
            recv_sem=h_recv.at[k, g, 1],
            device_id={"dom": d - 1},
        )

    def goes_up(k, g):
        return (d < N_DOM - 1) if k < 2 else ((d < N_DOM - 1) & (g == 0))

    def goes_down(k, g):
        return (d > 0) if k < 2 else ((d > 0) & (g == 1))

    def comes_up(k, g):
        return (d > 0) if k < 2 else ((d > 0) & (g == 0))

    def comes_down(k, g):
        return (d < N_DOM - 1) if k < 2 else ((d < N_DOM - 1) & (g == 1))

    def send_halo(k, g):
        @pl.when(goes_up(k, g))
        def _():
            up_copy(k, g).start()

        @pl.when(goes_down(k, g))
        def _():
            down_copy(k, g).start()

    def take_halo(k, g):
        @pl.when(comes_up(k, g))
        def _():
            up_copy(k, g).wait_recv()

        @pl.when(comes_down(k, g))
        def _():
            down_copy(k, g).wait_recv()

    def halo_sent(k, g):
        @pl.when(goes_up(k, g))
        def _():
            up_copy(k, g).wait_send()

        @pl.when(goes_down(k, g))
        def _():
            down_copy(k, g).wait_send()

    def stencil(g, x, y0, level):
        line = r[g, x + HALO, pl.ds(y0, 20)]
        f = line[HALO : HALO + 8]
        acc = (potb[pl.ds(x * NY + y0, 8)] + level[None]) * f
        for k in range(1, 7):
            pair = (
                line[HALO + k : HALO + k + 8]
                + line[HALO - k : HALO - k + 8]
                + r[g, x + HALO + k, pl.ds(y0 + HALO, 8)]
                + r[g, x + HALO - k, pl.ds(y0 + HALO, 8)]
            )
            acc = acc + (-0.5 * C[k]) * pair
        deep = jnp.dot(both_parts(f.reshape(64, NZ), 1), tz[...], preferred_element_type=F32)
        return f, acc + (deep[:, :NZ] + deep[:, NZ:]).reshape(8, 8, NZ)

    def tree(parts):
        parts = [parts[j] for j in range(8)]
        while len(parts) > 1:
            parts = [a + b for a, b in zip(parts[::2], parts[1::2])]
        return parts[0]

    none = jnp.zeros((8, NZ), F32)

    def level_of(g):
        return jnp.broadcast_to(lev[g], (8, NZ))

    def main(k, g):
        level = level_of(g)
        coeff = tot[g, 0] * energy[...]
        coeff = jnp.where(lanes < SLOTS, coeff, pltpu.roll(coeff, SLOTS, 1))
        lhs[...] = both_parts(coeff, 0)

        def body(i, carry):
            rr, rw, acc = carry
            x = i // 4
            y0 = pl.multiple_of((i % 4) * 8, 8)
            row = x * NY + y0
            f, image = stencil(g, x, y0, level)
            left = lhs[:, : 2 * SLOTS]
            blocks = []
            for j in range(8):
                v = jnp.dot(left, table[row + j], preferred_element_type=F32)
                blocks.append(image[j] + (v[:8] + v[8:]))
            for j in range(8):
                w[k % 2, g, x, y0 + j] = blocks[j]
            rr = rr + tree(f * f)
            rw = rw + tree([f[j] * blocks[j] for j in range(8)])
            return rr, rw, project(blocks, row, acc)

        rr, rw, acc = lax.fori_loop(
            0, SX * NY // 8, body, (none, none, jnp.zeros((16, 2 * SLOTS), F32))
        )
        send_sums(k, g, rr, rw)
        send_projections(k + 1, g, acc)
        send_halo(k, g)

    def last(g):
        level = level_of(g)

        def body(i, carry):
            rr, rw = carry
            x = i // 4
            y0 = pl.multiple_of((i % 4) * 8, 8)
            f, image = stencil(g, x, y0, level)
            return rr + tree(f * f), rw + tree(f * image)

        rr, rw = lax.fori_loop(0, SX * NY // 8, body, (none, none))
        own = (lanes >= ATOM_DEV) & (lanes < 2 * ATOM_DEV)
        t = tot[g, 0]
        rw = rw + jnp.where(own, t * t * energy[...], 0.0)
        send_sums(3, g, rr, rw)

    def update(k, g):
        alpha, beta = take_sums(k - 1, g)
        t = gathered_projections(k, g)
        if k > 1:
            t = t + beta * tot[g, 1]
        tot[g, 1] = t
        tot[g, 0] = tot[g, 0] - alpha * t
        a, b = alpha[None], beta[None]

        def own(i, _):
            x = i // 4
            y0 = pl.multiple_of((i % 4) * 8, 8)
            step = w[(k - 1) % 2, g, x, pl.ds(y0, 8)]
            if k > 1:
                step = step + b * s[g, x + HALO, pl.ds(y0, 8)]
            if k < 3:
                s[g, x + HALO, pl.ds(y0, 8)] = step
            new = r[g, x + HALO, pl.ds(y0 + HALO, 8)] - a * step
            r[g, x + HALO, pl.ds(y0 + HALO, 8)] = new
            if k < 3:
                hist[k, g, x, pl.ds(y0, 8)] = new
            return 0

        lax.fori_loop(0, SX * 4, own, 0)
        take_halo(k - 1, g)

        if k < 3:

            def side(i, _):
                x = i // 4
                y0 = pl.multiple_of((i % 4) * 8, 8)
                to = jnp.where(x < HALO, x, x + SX)
                step = hb[k - 1, g, x, pl.ds(y0, 8)]
                if k > 1:
                    step = step + b * s[g, to, pl.ds(y0, 8)]
                s[g, to, pl.ds(y0, 8)] = step
                r[g, to, pl.ds(y0 + HALO, 8)] = r[g, to, pl.ds(y0 + HALO, 8)] - a * step
                return 0

            lax.fori_loop(0, 2 * HALO * 4, side, 0)
        else:
            base = jnp.where(g == 0, 0, HALO + SX)
            other = HALO + SX - base

            def one_side(i, _):
                x = i // 4
                y0 = pl.multiple_of((i % 4) * 8, 8)
                step = hb2[g, x, pl.ds(y0, 8)] + b * s[g, base + x, pl.ds(y0, 8)]
                new = r[g, base + x, pl.ds(y0 + HALO, 8)] - a * step
                r[g, base + x, pl.ds(y0 + HALO, 8)] = new + new
                r[g, other + x, pl.ds(y0 + HALO, 8)] = jnp.zeros((8, 8, NZ), F32)
                return 0

            lax.fori_loop(0, HALO * 4, one_side, 0)

    loads[-1].wait()
    for g in range(2):
        for c in loads[4 * g : 4 * g + 4]:
            c.wait()

    def each(body):
        def run(g, _):
            body(g)
            return 0

        lax.fori_loop(0, 2, run, 0)

    def begin(g):
        def body(i, acc):
            x = i // 4
            y0 = pl.multiple_of((i % 4) * 8, 8)
            f = r[g, x + HALO, pl.ds(y0 + HALO, 8)]
            return project([f[j] for j in range(8)], x * NY + y0, acc)

        acc = lax.fori_loop(0, SX * NY // 8, body, jnp.zeros((16, 2 * SLOTS), F32))
        send_projections(0, g, acc)

    each(begin)

    def first(g):
        tot[g, 0] = gathered_projections(0, g)
        main(0, g)

    each(first)
    each(lambda g: forward_sums(0, g))

    for k in (1, 2):

        def turn(g, k=k):
            update(k, g)
            main(k, g)

        each(turn)
        each(lambda g, k=k: forward_sums(k, g))
        each(lambda g, k=k: halo_sent(k - 1, g))

    def closing(g):
        update(3, g)
        last(g)

    each(closing)
    each(lambda g: forward_sums(3, g))
    each(lambda g: halo_sent(2, g))

    def finish(g):
        a3, b3 = take_sums(3, g)
        g3 = a3
        g2 = scal[g, 2] + b3 * g3
        g1 = scal[g, 1] + scal[g, 6] * g2
        g0 = scal[g, 0] + scal[g, 5] * g1

        def body(i, _):
            x = i // 4
            y0 = pl.multiple_of((i % 4) * 8, 8)
            x_out[x, g, pl.ds(y0, 8)] = (
                g0[None] * hist[0, g, x, pl.ds(y0, 8)]
                + g1[None] * hist[1, g, x, pl.ds(y0, 8)]
                + g2[None] * hist[2, g, x, pl.ds(y0, 8)]
                + g3[None] * r[g, x + HALO, pl.ds(y0 + HALO, 8)]
            )
            return 0

        lax.fori_loop(0, SX * 4, body, 0)

    each(finish)


def solve(own, low, high, table, pot, lev, energy, tz):
    vmem = pl.BlockSpec(memory_space=pltpu.VMEM)
    anywhere = pl.BlockSpec(memory_space=pl.ANY)
    dma = pltpu.SemaphoreType.DMA
    return pl.pallas_call(
        solve_kernel,
        out_shape=jax.ShapeDtypeStruct((SX, 2, NY, 8, NZ), F32),
        in_specs=[anywhere] * 4 + [vmem] * 4,
        out_specs=vmem,
        scratch_shapes=[
            pltpu.VMEM((2, EXT, NYP, 8, NZ), F32),
            pltpu.VMEM((2, EXT, NY, 8, NZ), F32),
            pltpu.VMEM((2, 2, SX, NY, 8, NZ), F32),
            pltpu.VMEM((2, 2, 2 * HALO, NY, 8, NZ), F32),
            pltpu.VMEM((2, HALO, NY, 8, NZ), F32),
            pltpu.VMEM((3, 2, SX, NY, 8, NZ), F32),
            pltpu.VMEM((SX * NY, 2 * SLOTS, NZ), BF16),
            pltpu.VMEM((SX * NY, 8, NZ), F32),
            pltpu.VMEM((4, 2, PLANE, 8, NZ), F32),
            pltpu.VMEM((4, 2, DEPTH, 8, NZ), F32),
            pltpu.VMEM((4, 2, 4, 8, NZ), F32),
            pltpu.VMEM((4, 2, 2, 8, NZ), F32),
            pltpu.VMEM((4, 2, 8, NZ), F32),
            pltpu.VMEM((2, 12, 8, NZ), F32),
            pltpu.VMEM((2, 2, 8, NZ), F32),
            pltpu.VMEM((16, NZ), BF16),
            dma((9,)),
            dma((3, 2, 2)),
            dma((3, 2, 2)),
            dma((2, PLANE)),
            dma((2, 2, PLANE)),
            dma((2, DEPTH)),
            dma((2, 2, DEPTH)),
            dma((2, 4)),
            dma((2, 2, 4)),
        ],
        compiler_params=pltpu.CompilerParams(
            collective_id=0, has_side_effects=True, vmem_limit_bytes=60 * 2**20
        ),
        name="bicg_solve",
    )(own, low, high, table, pot, lev, energy, tz)


def cut_along(shard, dim, count):
    lengths = shard.shape
    tiles = shard.reshape(*lengths[:dim], count, lengths[dim] // count, *lengths[dim + 1 :])
    return jnp.moveaxis(tiles, dim, 0)


def summed_on_arrival(shard, axis, dim):
    count = lax.axis_size(axis)
    tiles = lax.all_to_all(cut_along(shard, dim, count), axis, 0, 0, tiled=True)
    return jnp.sum(tiles, axis=0)


def shards(orbitals, levels, potential, perturbation, projector, point_cell, point_atom, kb_energy):
    index = lax.axis_index("dom")
    up = [(i, i + 1) for i in range(N_DOM - 1)]
    down = [(i + 1, i) for i in range(N_DOM - 1)]
    right = -perturbation[None] * orbitals
    own = right.reshape(2, 8, SX, NY, NZ).transpose(2, 0, 3, 1, 4)
    low = lax.ppermute(own[SX - HALO :], "dom", up)
    high = lax.ppermute(own[:HALO], "dom", down)
    table = build_table(projector, point_cell, point_atom)
    energy = lax.dynamic_slice_in_dim(
        jnp.pad(kb_energy, (ATOM_DEV, ATOM_DEV)), index * ATOM_DEV, SLOTS
    )
    energy = jnp.pad(energy, (0, NZ - SLOTS))[None]
    lev = (-1.5 * C[0]) - levels.reshape(2, 8, 1)
    tz = jnp.asarray(depth_matrix())
    turned = solve(own, low, high, table, potential.reshape(SX * NY, NZ), lev, energy, tz)
    response = turned.transpose(1, 3, 0, 2, 4).reshape(orbitals.shape)
    density = summed_on_arrival(4.0 * jnp.sum(orbitals * response, axis=0), "st", 1)
    return response, density


def solution(mesh):
    in_specs = (
        P("st", "dom", None, None),
        P("st"),
        P("dom", None, None),
        P("dom", None, None),
        P("dom"),
        P("dom"),
        P("dom"),
        P(),
    )
    out_specs = (P("st", "dom", None, None), P("dom", "st", None))
    return jax.shard_map(shards, mesh=mesh, in_specs=in_specs, out_specs=out_specs, check_vma=False)
```

```python
import numpy as np
import jax
import jax.numpy as jnp
from jax import lax
from jax.experimental import pallas as pl
from jax.experimental.pallas import tpu as pltpu
from jax.sharding import PartitionSpec as P

ATOM_DEV = 16
SLOTS = 3 * ATOM_DEV
SX, NY, NZ = 8, 32, 128
HALO = 6
EXT = SX + 2 * HALO
NYP = NY + 2 * HALO
N_DOM = 64
PLANE = 8
DEPTH = 8
C = (
    -5369.0 / 1800.0,
    12.0 / 7.0,
    -15.0 / 56.0,
    10.0 / 189.0,
    -1.0 / 112.0,
    2.0 / 1925.0,
    -1.0 / 16632.0,
)
F32 = jnp.float32
BF16 = jnp.bfloat16
UNROLL = 8
VMEM_MIB = 36
ROWS = 32
UNUSED = SX * NY * SLOTS * NZ
SWAP = False


def depth_matrix():
    lag = np.abs(np.arange(NZ)[:, None] - np.arange(NZ)[None, :])
    band = np.zeros((NZ, NZ), np.float32)
    for k in range(1, 7):
        band[lag == k] = -0.5 * C[k]
    high = band.astype(jnp.bfloat16)
    low = (band - high.astype(np.float32)).astype(jnp.bfloat16)
    half = np.concatenate([high, low], axis=1)
    return np.concatenate([half, half], axis=0)


def both_parts(value, axis):
    high = value.astype(BF16).astype(F32)
    return jnp.concatenate([high, value - high], axis=axis).astype(BF16)


def table_kernel(place, value, table, dense):
    slots = place.shape[0]

    def clear(i, _):
        dense[pl.ds(pl.multiple_of(i * 64, 64), 64), :] = jnp.zeros((64, NZ), F32)
        return 0

    lax.fori_loop(0, SX * NY * SLOTS // 64, clear, 0)

    def halve(_, ends):
        low, high = ends
        mid = (low + high) // 2
        used = place[jnp.minimum(mid, slots - 1)] < UNUSED
        go = low < high
        return (
            jnp.where(go & used, mid + 1, low),
            jnp.where(go & jnp.logical_not(used), mid, high),
        )

    used, _ = lax.fori_loop(0, 15, halve, (jnp.int32(0), jnp.int32(slots)))
    lanes = lax.broadcasted_iota(jnp.int32, (1, NZ), 1)

    def put(i, _):
        for u in range(UNROLL):
            where = place[i * UNROLL + u]
            pltpu.store(
                dense.at[pl.ds(where >> 7, 1), :],
                jnp.full((1, NZ), value[i * UNROLL + u], F32),
                mask=lanes == (where & 127),
            )
        return 0

    lax.fori_loop(0, (used + UNROLL - 1) // UNROLL, put, 0)

    def split(i, _):
        for j in range(4):
            row = i * 4 + j
            part = dense[pl.ds(pl.multiple_of(row * SLOTS, SLOTS), SLOTS), :]
            table[row] = both_parts(part, 0)
        return 0

    lax.fori_loop(0, SX * NY // 4, split, 0)


def build_table(projector, place):
    smem = pl.BlockSpec(memory_space=pltpu.SMEM)
    return pl.pallas_call(
        table_kernel,
        out_shape=jax.ShapeDtypeStruct((SX * NY, 2 * SLOTS, NZ), BF16),
        in_specs=[smem, smem],
        out_specs=pl.BlockSpec(memory_space=pltpu.VMEM),
        scratch_shapes=[pltpu.VMEM((SX * NY * SLOTS + 8, NZ), F32)],
        compiler_params=pltpu.CompilerParams(vmem_limit_bytes=10 * 2**20),
        cost_estimate=pl.CostEstimate(flops=0, bytes_accessed=40 * 2**20, transcendentals=0),
        name="projector_table",
    )(place, projector)


def solve_kernel(
    own_in, low_in, high_in, table, orb, pot_in, lev, energy, tz,
    x_out, dens_out,
    r, s, w, hb, hb2, hist, potb, st1, st2, pj, msg, pmsg, scal, tot, lhs, dens, parts,
    sem_in, h_send, h_recv, a_send, a_recv, b_send, b_recv, p_send, p_recv, d_send, d_recv,
):
    d = lax.axis_index("dom")
    zi = d // PLANE
    ji = d % PLANE
    inner = pl.ds(HALO, NY)

    loads = []
    for g in range(2):
        loads += [
            pltpu.make_async_copy(own_in.at[:, g], r.at[g, pl.ds(HALO, SX), inner], sem_in.at[g, 0]),
            pltpu.make_async_copy(low_in.at[:, g], r.at[g, pl.ds(0, HALO), inner], sem_in.at[g, 1]),
            pltpu.make_async_copy(high_in.at[:, g], r.at[g, pl.ds(HALO + SX, HALO), inner], sem_in.at[g, 2]),
        ]
    for c in loads:
        c.start()

    zero = jnp.zeros((HALO, 8, NZ), F32)

    def clear(i, _):
        for g in range(2):
            r[g, i, pl.ds(0, HALO)] = zero
            r[g, i, pl.ds(HALO + NY, HALO)] = zero
        return 0

    lax.fori_loop(0, EXT, clear, 0)

    def clear_halo(base):
        plane = jnp.zeros((NY, 8, NZ), F32)

        def one(i, _):
            for k in range(2):
                for g in range(2):
                    hb[k, g, base + i] = plane
            for g in range(2):
                hb2[g, i] = plane
            return 0

        lax.fori_loop(0, HALO, one, 0)

    @pl.when(d == 0)
    def _():
        clear_halo(0)

    @pl.when(d == N_DOM - 1)
    def _():
        clear_halo(HALO)

    for k in range(4):
        for g in range(2):
            pj[k, g] = jnp.zeros((4, 8, NZ), F32)

    near = ((-2, d >= 2), (-1, d >= 1), (1, d < N_DOM - 1), (2, d < N_DOM - 2))

    def in_plane(i):
        return zi * PLANE + (ji + i) % PLANE

    def in_column(i):
        return ((zi + i) % DEPTH) * PLANE + ji

    me = lax.axis_index("st")
    blocks_st = lax.axis_size("st")

    def other_block(i):
        return (me + i) % blocks_st

    barrier = pltpu.get_barrier_semaphore()
    count = jnp.int32(PLANE - 1 + DEPTH - 1 + blocks_st - 1)
    for i in range(1, blocks_st):
        pl.semaphore_signal(barrier, inc=1, device_id={"st": other_block(i)})
    for i in range(1, PLANE):
        pl.semaphore_signal(barrier, inc=1, device_id={"dom": in_plane(i)})
    for i in range(1, DEPTH):
        pl.semaphore_signal(barrier, inc=1, device_id={"dom": in_column(i)})
    for step, there in near:
        count = count + there.astype(jnp.int32)

        @pl.when(there)
        def _(step=step):
            pl.semaphore_signal(barrier, inc=1, device_id={"dom": d + step})

    lanes = lax.broadcasted_iota(jnp.int32, (8, NZ), 1)

    def spread(i, _):
        rows = pot_in[pl.ds(pl.multiple_of(i * 8, 8), 8), :]
        for j in range(8):
            potb[i * 8 + j] = jnp.broadcast_to(rows[j : j + 1, :], (8, NZ))
        return 0

    lax.fori_loop(0, SX * NY // 8, spread, 0)
    pl.semaphore_wait(barrier, count)

    def project(blocks, row, acc):
        left = jnp.concatenate([both_parts(b, 0) for b in blocks], axis=1)
        right = jnp.concatenate([table[row + j] for j in range(len(blocks))], axis=1)
        if SWAP:
            left, right = right, left
        return acc + lax.dot_general(
            left, right, (((1,), (1,)), ((), ())), preferred_element_type=F32
        )

    def near_copy(k, g, n):
        step = near[n][0]
        return pltpu.make_async_remote_copy(
            src_ref=pmsg.at[k, g],
            dst_ref=pj.at[k, g, 3 - n],
            send_sem=p_send.at[g, n],
            recv_sem=p_recv.at[k % 2, g, 3 - n],
            device_id={"dom": d + step},
        )

    def near_arrival(k, g, n):
        return pltpu.make_async_remote_copy(
            src_ref=pmsg.at[k, g],
            dst_ref=pj.at[k, g, n],
            send_sem=p_send.at[g, n],
            recv_sem=p_recv.at[k % 2, g, n],
            device_id={"dom": d + near[n][0]},
        )

    def send_projections(k, g, acc):
        if SWAP:
            acc = acc[:SLOTS] + acc[SLOTS:]
            acc = jnp.concatenate([acc, jnp.zeros((SLOTS, NZ - 16), F32)], axis=1)
            acc = jnp.concatenate([acc, jnp.zeros((NZ - SLOTS, NZ), F32)], axis=0).T
            pmsg[k, g] = acc[:8] + acc[8:16]
        else:
            part = acc[:8, :SLOTS] + acc[8:, :SLOTS] + acc[:8, SLOTS:] + acc[8:, SLOTS:]
            pmsg[k, g] = jnp.concatenate([part, jnp.zeros((8, NZ - SLOTS), F32)], axis=1)
        for n in range(4):

            @pl.when(near[n][1])
            def _(n=n):
                near_copy(k, g, n).start()

    def gathered_projections(k, g):
        for n in range(4):

            @pl.when(near[n][1])
            def _(n=n):
                near_arrival(k, g, n).wait_recv()
                near_copy(k, g, n).wait_send()

        total = pmsg[k, g]
        shifts = ((2 * ATOM_DEV, 0, 16), (ATOM_DEV, 0, 32), (-ATOM_DEV, 16, 48), (-2 * ATOM_DEV, 32, 48))
        for n, (back, low, high) in enumerate(shifts):
            moved = pltpu.roll(pj[k, g, n], (-back) % NZ, 1)
            total = total + jnp.where((lanes >= low) & (lanes < high), moved, 0.0)
        return total

    def plane_copy(k, g, i):
        return pltpu.make_async_remote_copy(
            src_ref=msg.at[k, g, 0],
            dst_ref=st1.at[k, g, ji],
            send_sem=a_send.at[g, i],
            recv_sem=a_recv.at[k % 2, g, i],
            device_id={"dom": in_plane(i)},
        )

    def plane_arrival(k, g, i):
        return pltpu.make_async_remote_copy(
            src_ref=msg.at[k, g, 0],
            dst_ref=st1.at[k, g, (ji + PLANE - i) % PLANE],
            send_sem=a_send.at[g, i],
            recv_sem=a_recv.at[k % 2, g, i],
            device_id={"dom": in_plane(i)},
        )

    def column_copy(k, g, i):
        return pltpu.make_async_remote_copy(
            src_ref=msg.at[k, g, 1],
            dst_ref=st2.at[k, g, zi],
            send_sem=b_send.at[g, i],
            recv_sem=b_recv.at[k % 2, g, i],
            device_id={"dom": in_column(i)},
        )

    def column_arrival(k, g, i):
        return pltpu.make_async_remote_copy(
            src_ref=msg.at[k, g, 1],
            dst_ref=st2.at[k, g, (zi + DEPTH - i) % DEPTH],
            send_sem=b_send.at[g, i],
            recv_sem=b_recv.at[k % 2, g, i],
            device_id={"dom": in_column(i)},
        )

    def send_sums(k, g, rr, rw):
        tile = jnp.where(
            lanes < 64, jnp.sum(rr, axis=1, keepdims=True), jnp.sum(rw, axis=1, keepdims=True)
        )
        msg[k, g, 0] = tile
        st1[k, g, ji] = tile
        for i in range(1, PLANE):
            plane_copy(k, g, i).start()

    def forward_sums(k, g):
        for i in range(1, PLANE):
            plane_arrival(k, g, i).wait_recv()
            plane_copy(k, g, i).wait_send()
        tile = st1[k, g, 0]
        for i in range(1, PLANE):
            tile = tile + st1[k, g, i]
        msg[k, g, 1] = tile
        st2[k, g, zi] = tile
        for i in range(1, DEPTH):
            column_copy(k, g, i).start()

    def take_sums(k, g):
        for i in range(1, DEPTH):
            column_arrival(k, g, i).wait_recv()
            column_copy(k, g, i).wait_send()
        tile = st2[k, g, 0]
        for i in range(1, DEPTH):
            tile = tile + st2[k, g, i]
        rr = jnp.broadcast_to(tile[:, 0:1], (8, NZ))
        rw = jnp.broadcast_to(tile[:, 64:65], (8, NZ))
        scal[g, 8 + k] = rr
        if k == 0:
            alpha, beta = rr / rw, jnp.zeros_like(rr)
        else:
            beta = rr / scal[g, 7 + k]
            alpha = rr / (rw - beta * rr / scal[g, k - 1])
        scal[g, k] = alpha
        scal[g, 4 + k] = beta
        return alpha, beta

    def up_copy(k, g):
        dst = hb.at[k, g, pl.ds(0, HALO)] if k < 2 else hb2.at[g]
        return pltpu.make_async_remote_copy(
            src_ref=w.at[k % 2, g, pl.ds(SX - HALO, HALO)],
            dst_ref=dst,
            send_sem=h_send.at[k, g, 0],
            recv_sem=h_recv.at[k, g, 0],
            device_id={"dom": d + 1},
        )

    def down_copy(k, g):
        dst = hb.at[k, g, pl.ds(HALO, HALO)] if k < 2 else hb2.at[g]
        return pltpu.make_async_remote_copy(
            src_ref=w.at[k % 2, g, pl.ds(0, HALO)],
            dst_ref=dst,
            send_sem=h_send.at[k, g, 1],
            recv_sem=h_recv.at[k, g, 1],
            device_id={"dom": d - 1},
        )

    def goes_up(k, g):
        return (d < N_DOM - 1) if k < 2 else ((d < N_DOM - 1) & (g == 0))

    def goes_down(k, g):
        return (d > 0) if k < 2 else ((d > 0) & (g == 1))

    def comes_up(k, g):
        return (d > 0) if k < 2 else ((d > 0) & (g == 0))

    def comes_down(k, g):
        return (d < N_DOM - 1) if k < 2 else ((d < N_DOM - 1) & (g == 1))

    def send_halo(k, g):
        @pl.when(goes_up(k, g))
        def _():
            up_copy(k, g).start()

        @pl.when(goes_down(k, g))
        def _():
            down_copy(k, g).start()

    def take_halo(k, g):
        @pl.when(comes_up(k, g))
        def _():
            up_copy(k, g).wait_recv()

        @pl.when(comes_down(k, g))
        def _():
            down_copy(k, g).wait_recv()

    def halo_sent(k, g):
        @pl.when(goes_up(k, g))
        def _():
            up_copy(k, g).wait_send()

        @pl.when(goes_down(k, g))
        def _():
            down_copy(k, g).wait_send()

    def stencil(g, x, y0, level, rows):
        f = r[g, x + HALO, pl.ds(y0 + HALO, rows)]
        deep = jnp.dot(
            both_parts(f.reshape(rows * 8, NZ), 1), tz[...], preferred_element_type=F32
        )
        deep = (deep[:, :NZ] + deep[:, NZ:]).reshape(rows, 8, NZ)
        fs, images = [], []
        for part in range(0, rows, 8):
            line = r[g, x + HALO, pl.ds(y0 + part, 20)]
            f = line[HALO : HALO + 8]
            acc = deep[part : part + 8] + (potb[pl.ds(x * NY + y0 + part, 8)] + level[None]) * f
            for k in range(1, 7):
                pair = (
                    line[HALO + k : HALO + k + 8]
                    + line[HALO - k : HALO - k + 8]
                    + r[g, x + HALO + k, pl.ds(y0 + part + HALO, 8)]
                    + r[g, x + HALO - k, pl.ds(y0 + part + HALO, 8)]
                )
                acc = acc + (-0.5 * C[k]) * pair
            fs.append(f)
            images.append(acc)
        return fs, images

    def tree(parts):
        parts = [parts[j] for j in range(8)]
        while len(parts) > 1:
            parts = [a + b for a, b in zip(parts[::2], parts[1::2])]
        return parts[0]

    def place(i):
        per = NY // ROWS
        return i // per, pl.multiple_of((i % per) * ROWS, ROWS)

    none = jnp.zeros((8, NZ), F32)

    def level_of(g):
        return jnp.broadcast_to(lev[g], (8, NZ))

    def main(k, g):
        level = level_of(g)
        coeff = tot[g, 0] * energy[...]
        coeff = jnp.where(lanes < SLOTS, coeff, pltpu.roll(coeff, SLOTS, 1))
        lhs[...] = both_parts(coeff, 0)

        def body(i, carry):
            rr, rw, acc = carry
            x, y0 = place(i)
            fs, images = stencil(g, x, y0, level, ROWS)
            left = lhs[:, : 2 * SLOTS]
            for n, (f, image) in enumerate(zip(fs, images)):
                row = x * NY + y0 + n * 8
                blocks = []
                for j in range(8):
                    v = jnp.dot(left, table[row + j], preferred_element_type=F32)
                    blocks.append(image[j] + (v[:8] + v[8:]))
                for j in range(8):
                    w[k % 2, g, x, y0 + n * 8 + j] = blocks[j]
                rr = rr + tree(f * f)
                rw = rw + tree([f[j] * blocks[j] for j in range(8)])
                acc = project(blocks, row, acc)
            return rr, rw, acc

        rr, rw, acc = lax.fori_loop(
            0, SX * NY // ROWS, body, (none, none, jnp.zeros((2 * SLOTS, 16) if SWAP else (16, 2 * SLOTS), F32))
        )
        send_sums(k, g, rr, rw)
        send_projections(k + 1, g, acc)
        send_halo(k, g)

    def last(g):
        level = level_of(g)

        def body(i, carry):
            rr, rw = carry
            x, y0 = place(i)
            for f, image in zip(*stencil(g, x, y0, level, ROWS)):
                rr, rw = rr + tree(f * f), rw + tree(f * image)
            return rr, rw

        rr, rw = lax.fori_loop(0, SX * NY // ROWS, body, (none, none))
        own = (lanes >= ATOM_DEV) & (lanes < 2 * ATOM_DEV)
        t = tot[g, 0]
        rw = rw + jnp.where(own, t * t * energy[...], 0.0)
        send_sums(3, g, rr, rw)

    def update(k, g):
        alpha, beta = take_sums(k - 1, g)
        t = gathered_projections(k, g)
        if k > 1:
            t = t + beta * tot[g, 1]
        tot[g, 1] = t
        tot[g, 0] = tot[g, 0] - alpha * t
        a, b = alpha[None], beta[None]

        def own(i, _):
            x = i // 4
            y0 = pl.multiple_of((i % 4) * 8, 8)
            step = w[(k - 1) % 2, g, x, pl.ds(y0, 8)]
            if k > 1:
                step = step + b * s[g, x + HALO, pl.ds(y0, 8)]
            if k < 3:
                s[g, x + HALO, pl.ds(y0, 8)] = step
            new = r[g, x + HALO, pl.ds(y0 + HALO, 8)] - a * step
            r[g, x + HALO, pl.ds(y0 + HALO, 8)] = new
            if k < 3:
                hist[k - 1, g, x, pl.ds(y0, 8)] = new
            return 0

        lax.fori_loop(0, SX * 4, own, 0)
        take_halo(k - 1, g)

        if k < 3:

            def side(i, _):
                x = i // 4
                y0 = pl.multiple_of((i % 4) * 8, 8)
                to = jnp.where(x < HALO, x, x + SX)
                step = hb[k - 1, g, x, pl.ds(y0, 8)]
                if k > 1:
                    step = step + b * s[g, to, pl.ds(y0, 8)]
                s[g, to, pl.ds(y0, 8)] = step
                r[g, to, pl.ds(y0 + HALO, 8)] = r[g, to, pl.ds(y0 + HALO, 8)] - a * step
                return 0

            lax.fori_loop(0, 2 * HALO * 4, side, 0)
        else:
            base = jnp.where(g == 0, 0, HALO + SX)
            other = HALO + SX - base

            def one_side(i, _):
                x = i // 4
                y0 = pl.multiple_of((i % 4) * 8, 8)
                step = hb2[g, x, pl.ds(y0, 8)] + b * s[g, base + x, pl.ds(y0, 8)]
                new = r[g, base + x, pl.ds(y0 + HALO, 8)] - a * step
                r[g, base + x, pl.ds(y0 + HALO, 8)] = new + new
                r[g, other + x, pl.ds(y0 + HALO, 8)] = jnp.zeros((8, 8, NZ), F32)
                return 0

            lax.fori_loop(0, HALO * 4, one_side, 0)

    def each(body):
        def run(g, _):
            body(g)
            return 0

        lax.fori_loop(0, 2, run, 0)

    def begin(g):
        def body(i, acc):
            x = i // 4
            y0 = pl.multiple_of((i % 4) * 8, 8)
            f = own_in[x, g, pl.ds(y0, 8)]
            return project([f[j] for j in range(8)], x * NY + y0, acc)

        acc = lax.fori_loop(0, SX * NY // 8, body, jnp.zeros((2 * SLOTS, 16) if SWAP else (16, 2 * SLOTS), F32))
        send_projections(0, g, acc)

    each(begin)
    for c in loads:
        c.wait()

    def pass_on(k, g):
        forward_sums(k - 1 + g, 1 - g)

    def first(g):
        tot[g, 0] = gathered_projections(0, g)

        @pl.when(g == 1)
        def _():
            pass_on(0, g)

        main(0, g)

    each(first)

    for k in (1, 2):

        def turn(g, k=k):
            update(k, g)
            pass_on(k, g)
            main(k, g)

        each(turn)
        each(lambda g, k=k: halo_sent(k - 1, g))

    def closing(g):
        update(3, g)
        pass_on(3, g)
        last(g)

    each(closing)
    forward_sums(3, 1)
    each(lambda g: halo_sent(2, g))

    def finish(g):
        a3, b3 = take_sums(3, g)
        g3 = a3
        g2 = scal[g, 2] + b3 * g3
        g1 = scal[g, 1] + scal[g, 6] * g2
        g0 = scal[g, 0] + scal[g, 5] * g1

        def body(i, _):
            x = i // 4
            y0 = pl.multiple_of((i % 4) * 8, 8)
            value = (
                g0[None] * own_in[x, g, pl.ds(y0, 8)]
                + g1[None] * hist[0, g, x, pl.ds(y0, 8)]
                + g2[None] * hist[1, g, x, pl.ds(y0, 8)]
                + g3[None] * r[g, x + HALO, pl.ds(y0 + HALO, 8)]
            )
            x_out[x, g, pl.ds(y0, 8)] = value
            part = 4.0 * jnp.sum(value * orb[x, g, pl.ds(y0, 8)], axis=1)
            dens[x, pl.ds(y0, 8), :] = jnp.where(g == 0, part, dens[x, pl.ds(y0, 8), :] + part)
            return 0

        lax.fori_loop(0, SX * 4, body, 0)

    def clear_dens(i, _):
        dens[i] = jnp.zeros((NY, NZ), F32)
        return 0

    lax.fori_loop(0, SX, clear_dens, 0)
    each(finish)

    def rows_of(block):
        return pl.ds(pl.multiple_of(block * (NY // blocks_st), NY // blocks_st), NY // blocks_st)

    def block_copy(i, source):
        return pltpu.make_async_remote_copy(
            src_ref=dens.at[:, rows_of(other_block(i)), :],
            dst_ref=parts.at[source],
            send_sem=d_send.at[i],
            recv_sem=d_recv.at[i],
            device_id={"st": other_block(i)},
        )

    for i in range(1, blocks_st):
        block_copy(i, me).start()
    parts[me] = dens[:, rows_of(me), :]
    for i in range(1, blocks_st):
        block_copy(i, (me + blocks_st - i) % blocks_st).wait_recv()
    total = parts[0]
    for i in range(1, blocks_st):
        total = total + parts[i]
    dens_out[...] = total
    for i in range(1, blocks_st):
        block_copy(i, me).wait_send()


def solve(own, low, high, table, orb, pot, lev, energy, tz, blocks_st):
    vmem = pl.BlockSpec(memory_space=pltpu.VMEM)
    dma = pltpu.SemaphoreType.DMA
    return pl.pallas_call(
        solve_kernel,
        out_shape=(
            jax.ShapeDtypeStruct((SX, 2, NY, 8, NZ), F32),
            jax.ShapeDtypeStruct((SX, NY // blocks_st, NZ), F32),
        ),
        in_specs=[vmem] * 9,
        out_specs=(vmem, vmem),
        scratch_shapes=[
            pltpu.VMEM((2, EXT, NYP, 8, NZ), F32),
            pltpu.VMEM((2, EXT, NY, 8, NZ), F32),
            pltpu.VMEM((2, 2, SX, NY, 8, NZ), F32),
            pltpu.VMEM((2, 2, 2 * HALO, NY, 8, NZ), F32),
            pltpu.VMEM((2, HALO, NY, 8, NZ), F32),
            pltpu.VMEM((2, 2, SX, NY, 8, NZ), F32),
            pltpu.VMEM((SX * NY, 8, NZ), F32),
            pltpu.VMEM((4, 2, PLANE, 8, NZ), F32),
            pltpu.VMEM((4, 2, DEPTH, 8, NZ), F32),
            pltpu.VMEM((4, 2, 4, 8, NZ), F32),
            pltpu.VMEM((4, 2, 2, 8, NZ), F32),
            pltpu.VMEM((4, 2, 8, NZ), F32),
            pltpu.VMEM((2, 12, 8, NZ), F32),
            pltpu.VMEM((2, 2, 8, NZ), F32),
            pltpu.VMEM((16, NZ), BF16),
            pltpu.VMEM((SX, NY, NZ), F32),
            pltpu.VMEM((blocks_st, SX, NY // blocks_st, NZ), F32),
            dma((2, 3)),
            dma((3, 2, 2)),
            dma((3, 2, 2)),
            dma((2, PLANE)),
            dma((2, 2, PLANE)),
            dma((2, DEPTH)),
            dma((2, 2, DEPTH)),
            dma((2, 4)),
            dma((2, 2, 4)),
            dma((blocks_st,)),
            dma((blocks_st,)),
        ],
        compiler_params=pltpu.CompilerParams(
            collective_id=0, has_side_effects=True, vmem_limit_bytes=VMEM_MIB * 2**20
        ),
        name="bicg_solve",
    )(own, low, high, table, orb, pot, lev, energy, tz)


def shards(orbitals, levels, potential, perturbation, projector, point_cell, point_atom, kb_energy):
    index = lax.axis_index("dom")
    up = [(i, i + 1) for i in range(N_DOM - 1)]
    down = [(i + 1, i) for i in range(N_DOM - 1)]
    orb = orbitals.reshape(2, 8, SX, NY, NZ).transpose(2, 0, 3, 1, 4)
    own = -(orb * perturbation[:, None, :, None, :])
    low = lax.ppermute(own[SX - HALO :], "dom", up)
    high = lax.ppermute(own[:HALO], "dom", down)
    row = (point_cell >> 7) * SLOTS + point_atom - (index - 1) * ATOM_DEV
    place = jnp.where(point_atom >= 0, row * NZ + (point_cell & 127), UNUSED)
    table = build_table(projector, place)
    energy = lax.dynamic_slice_in_dim(
        jnp.pad(kb_energy, (ATOM_DEV, ATOM_DEV)), index * ATOM_DEV, SLOTS
    )
    energy = jnp.pad(energy, (0, NZ - SLOTS))[None]
    lev = (-1.5 * C[0]) - levels.reshape(2, 8, 1)
    tz = jnp.asarray(depth_matrix())
    turned, density = solve(
        own, low, high, table, orb, potential.reshape(SX * NY, NZ), lev, energy, tz,
        lax.axis_size("st"),
    )
    response = turned.transpose(1, 3, 0, 2, 4).reshape(orbitals.shape)
    return response, density


def solution(mesh):
    in_specs = (
        P("st", "dom", None, None),
        P("st"),
        P("dom", None, None),
        P("dom", None, None),
        P("dom"),
        P("dom"),
        P("dom"),
        P(),
    )
    out_specs = (P("st", "dom", None, None), P("dom", "st", None))
    return jax.shard_map(shards, mesh=mesh, in_specs=in_specs, out_specs=out_specs, check_vma=False)
```

```python
import numpy as np
import jax
import jax.numpy as jnp
from jax import lax
from jax.experimental import pallas as pl
from jax.experimental.pallas import tpu as pltpu
from jax.sharding import PartitionSpec as P

ATOM_DEV = 16
SLOTS = 3 * ATOM_DEV
SX, NY, NZ = 8, 32, 128
HALO = 6
EXT = SX + 2 * HALO
NYP = NY + 2 * HALO
N_DOM = 64
PLANE = 8
DEPTH = 8
C = (
    -5369.0 / 1800.0,
    12.0 / 7.0,
    -15.0 / 56.0,
    10.0 / 189.0,
    -1.0 / 112.0,
    2.0 / 1925.0,
    -1.0 / 16632.0,
)
F32 = jnp.float32
BF16 = jnp.bfloat16
UNROLL = 8
VMEM_MIB = 43
ROWS = 32
BREAK = 2
UNUSED = SX * NY * SLOTS * NZ


def depth_matrix():
    lag = np.abs(np.arange(NZ)[:, None] - np.arange(NZ)[None, :])
    band = np.zeros((NZ, NZ), np.float32)
    for k in range(1, 7):
        band[lag == k] = -0.5 * C[k]
    high = band.astype(jnp.bfloat16)
    low = (band - high.astype(np.float32)).astype(jnp.bfloat16)
    half = np.concatenate([high, low], axis=1)
    return np.concatenate([half, half], axis=0)


def both_parts(value, axis):
    high = value.astype(BF16).astype(F32)
    return jnp.concatenate([high, value - high], axis=axis).astype(BF16)


def table_kernel(place, value, table, dense):
    slots = place.shape[0]

    def clear(i, _):
        dense[pl.ds(pl.multiple_of(i * 64, 64), 64), :] = jnp.zeros((64, NZ), F32)
        return 0

    lax.fori_loop(0, SX * NY * SLOTS // 64, clear, 0)

    def halve(_, ends):
        low, high = ends
        mid = (low + high) // 2
        used = place[jnp.minimum(mid, slots - 1)] < UNUSED
        go = low < high
        return (
            jnp.where(go & used, mid + 1, low),
            jnp.where(go & jnp.logical_not(used), mid, high),
        )

    used, _ = lax.fori_loop(0, 15, halve, (jnp.int32(0), jnp.int32(slots)))
    lanes = lax.broadcasted_iota(jnp.int32, (1, NZ), 1)

    def put(i, _):
        for u in range(UNROLL):
            where = place[i * UNROLL + u]
            pltpu.store(
                dense.at[pl.ds(where >> 7, 1), :],
                jnp.full((1, NZ), value[i * UNROLL + u], F32),
                mask=lanes == (where & 127),
            )
        return 0

    lax.fori_loop(0, (used + UNROLL - 1) // UNROLL, put, 0)

    def split(i, _):
        for j in range(4):
            row = i * 4 + j
            part = dense[pl.ds(pl.multiple_of(row * SLOTS, SLOTS), SLOTS), :]
            table[row] = both_parts(part, 0)
        return 0

    lax.fori_loop(0, SX * NY // 4, split, 0)


def build_table(projector, place):
    smem = pl.BlockSpec(memory_space=pltpu.SMEM)
    return pl.pallas_call(
        table_kernel,
        out_shape=jax.ShapeDtypeStruct((SX * NY, 2 * SLOTS, NZ), BF16),
        in_specs=[smem, smem],
        out_specs=pl.BlockSpec(memory_space=pltpu.VMEM),
        scratch_shapes=[pltpu.VMEM((SX * NY * SLOTS + 8, NZ), F32)],
        compiler_params=pltpu.CompilerParams(vmem_limit_bytes=10 * 2**20),
        cost_estimate=pl.CostEstimate(flops=0, bytes_accessed=40 * 2**20, transcendentals=0),
        name="projector_table",
    )(place, projector)


def solve_kernel(
    table, orb, pot_in, pert_in, lev, energy, tz,
    x_out, dens_out,
    own_in, turned, r, s, w, hb, hb2, hist, potb, st1, st2, pj, msg, pmsg, scal, tot, lhs, dens, parts,
    h_send, h_recv, a_send, a_recv, b_send, b_recv, p_send, p_recv, d_send, d_recv,
):
    d = lax.axis_index("dom")
    zi = d // PLANE
    ji = d % PLANE
    inner = pl.ds(HALO, NY)

    zero = jnp.zeros((HALO, 8, NZ), F32)

    def clear(i, _):
        for g in range(2):
            r[g, i, pl.ds(0, HALO)] = zero
            r[g, i, pl.ds(HALO + NY, HALO)] = zero
        return 0

    lax.fori_loop(0, EXT, clear, 0)

    def start(i, _):
        x = i // 4
        y0 = pl.multiple_of((i % 4) * 8, 8)
        rows = pert_in[pl.ds(pl.multiple_of(i * 8, 8), 8), :]
        for j in range(8):
            row = jnp.broadcast_to(rows[j : j + 1, :], (8, NZ))
            for g in range(2):
                value = -row * orb[x, g, y0 + j]
                own_in[x, g, y0 + j] = value
                r[g, x + HALO, y0 + HALO + j] = value
        return 0

    lax.fori_loop(0, SX * NY // 8, start, 0)

    def clear_halo(base):
        plane = jnp.zeros((NY, 8, NZ), F32)
        far = jnp.where(base == 0, 0, SX + HALO)

        def one(i, _):
            for k in range(2):
                for g in range(2):
                    hb[k, g, base + i] = plane
            for g in range(2):
                hb2[g, i] = plane
                r[g, far + i, inner] = plane
            return 0

        lax.fori_loop(0, HALO, one, 0)

    @pl.when(d == 0)
    def _():
        clear_halo(0)

    @pl.when(d == N_DOM - 1)
    def _():
        clear_halo(HALO)

    for k in range(4):
        for g in range(2):
            pj[k, g] = jnp.zeros((4, 8, NZ), F32)

    near = ((-2, d >= 2), (-1, d >= 1), (1, d < N_DOM - 1), (2, d < N_DOM - 2))

    def in_plane(i):
        return zi * PLANE + (ji + i) % PLANE

    def in_column(i):
        return ((zi + i) % DEPTH) * PLANE + ji

    me = lax.axis_index("st")
    blocks_st = lax.axis_size("st")

    def other_block(i):
        return (me + i) % blocks_st

    barrier = pltpu.get_barrier_semaphore()
    count = jnp.int32(PLANE - 1 + DEPTH - 1 + blocks_st - 1)
    for i in range(1, blocks_st):
        pl.semaphore_signal(barrier, inc=1, device_id={"st": other_block(i)})
    for i in range(1, PLANE):
        pl.semaphore_signal(barrier, inc=1, device_id={"dom": in_plane(i)})
    for i in range(1, DEPTH):
        pl.semaphore_signal(barrier, inc=1, device_id={"dom": in_column(i)})
    for step, there in near:
        count = count + there.astype(jnp.int32)

        @pl.when(there)
        def _(step=step):
            pl.semaphore_signal(barrier, inc=1, device_id={"dom": d + step})

    lanes = lax.broadcasted_iota(jnp.int32, (8, NZ), 1)

    pl.semaphore_wait(barrier, count)

    def project(blocks, row, acc):
        left = jnp.concatenate([both_parts(b, 0) for b in blocks], axis=1)
        right = turned[pl.ds(pl.multiple_of(row * NZ, 8 * NZ), 8 * NZ), :]
        return acc + jnp.dot(left, right, preferred_element_type=F32)

    def near_copy(k, g, n):
        step = near[n][0]
        return pltpu.make_async_remote_copy(
            src_ref=pmsg.at[k, g],
            dst_ref=pj.at[k, g, 3 - n],
            send_sem=p_send.at[g, n],
            recv_sem=p_recv.at[k % 2, g, 3 - n],
            device_id={"dom": d + step},
        )

    def near_arrival(k, g, n):
        return pltpu.make_async_remote_copy(
            src_ref=pmsg.at[k, g],
            dst_ref=pj.at[k, g, n],
            send_sem=p_send.at[g, n],
            recv_sem=p_recv.at[k % 2, g, n],
            device_id={"dom": d + near[n][0]},
        )

    def send_projections(k, g, acc):
        part = acc[:8, :SLOTS] + acc[8:, :SLOTS] + acc[:8, SLOTS:] + acc[8:, SLOTS:]
        pmsg[k, g] = jnp.concatenate([part, jnp.zeros((8, NZ - SLOTS), F32)], axis=1)
        for n in range(4):

            @pl.when(near[n][1])
            def _(n=n):
                near_copy(k, g, n).start()

    def gathered_projections(k, g):
        for n in range(4):

            @pl.when(near[n][1])
            def _(n=n):
                near_arrival(k, g, n).wait_recv()
                near_copy(k, g, n).wait_send()

        total = pmsg[k, g]
        shifts = ((2 * ATOM_DEV, 0, 16), (ATOM_DEV, 0, 32), (-ATOM_DEV, 16, 48), (-2 * ATOM_DEV, 32, 48))
        for n, (back, low, high) in enumerate(shifts):
            moved = pltpu.roll(pj[k, g, n], (-back) % NZ, 1)
            total = total + jnp.where((lanes >= low) & (lanes < high), moved, 0.0)
        return total

    def plane_copy(k, g, i):
        return pltpu.make_async_remote_copy(
            src_ref=msg.at[k, g, 0],
            dst_ref=st1.at[k, g, ji],
            send_sem=a_send.at[g, i],
            recv_sem=a_recv.at[k % 2, g, i],
            device_id={"dom": in_plane(i)},
        )

    def plane_arrival(k, g, i):
        return pltpu.make_async_remote_copy(
            src_ref=msg.at[k, g, 0],
            dst_ref=st1.at[k, g, (ji + PLANE - i) % PLANE],
            send_sem=a_send.at[g, i],
            recv_sem=a_recv.at[k % 2, g, i],
            device_id={"dom": in_plane(i)},
        )

    def column_copy(k, g, i):
        return pltpu.make_async_remote_copy(
            src_ref=msg.at[k, g, 1],
            dst_ref=st2.at[k, g, zi],
            send_sem=b_send.at[g, i],
            recv_sem=b_recv.at[k % 2, g, i],
            device_id={"dom": in_column(i)},
        )

    def column_arrival(k, g, i):
        return pltpu.make_async_remote_copy(
            src_ref=msg.at[k, g, 1],
            dst_ref=st2.at[k, g, (zi + DEPTH - i) % DEPTH],
            send_sem=b_send.at[g, i],
            recv_sem=b_recv.at[k % 2, g, i],
            device_id={"dom": in_column(i)},
        )

    def send_sums(k, g, rr, rw):
        tile = jnp.where(
            lanes < 64, jnp.sum(rr, axis=1, keepdims=True), jnp.sum(rw, axis=1, keepdims=True)
        )
        msg[k, g, 0] = tile
        st1[k, g, ji] = tile
        for i in range(1, PLANE):
            plane_copy(k, g, i).start()

    def forward_sums(k, g):
        for i in range(1, PLANE):
            plane_arrival(k, g, i).wait_recv()
            plane_copy(k, g, i).wait_send()
        tile = st1[k, g, 0]
        for i in range(1, PLANE):
            tile = tile + st1[k, g, i]
        msg[k, g, 1] = tile
        st2[k, g, zi] = tile
        for i in range(1, DEPTH):
            column_copy(k, g, i).start()

    def take_sums(k, g):
        for i in range(1, DEPTH):
            column_arrival(k, g, i).wait_recv()
            column_copy(k, g, i).wait_send()
        tile = st2[k, g, 0]
        for i in range(1, DEPTH):
            tile = tile + st2[k, g, i]
        rr = jnp.broadcast_to(tile[:, 0:1], (8, NZ))
        rw = jnp.broadcast_to(tile[:, 64:65], (8, NZ))
        scal[g, 8 + k] = rr
        if k == 0:
            alpha, beta = rr / rw, jnp.zeros_like(rr)
        else:
            beta = rr / scal[g, 7 + k]
            alpha = rr / (rw - beta * rr / scal[g, k - 1])
        scal[g, k] = alpha
        scal[g, 4 + k] = beta
        return alpha, beta

    def up_copy(k, g):
        dst = hb.at[k, g, pl.ds(0, HALO)] if k < 2 else hb2.at[g]
        return pltpu.make_async_remote_copy(
            src_ref=w.at[k % 2, g, pl.ds(SX - HALO, HALO)],
            dst_ref=dst,
            send_sem=h_send.at[k, g, 0],
            recv_sem=h_recv.at[k, g, 0],
            device_id={"dom": d + 1},
        )

    def down_copy(k, g):
        dst = hb.at[k, g, pl.ds(HALO, HALO)] if k < 2 else hb2.at[g]
        return pltpu.make_async_remote_copy(
            src_ref=w.at[k % 2, g, pl.ds(0, HALO)],
            dst_ref=dst,
            send_sem=h_send.at[k, g, 1],
            recv_sem=h_recv.at[k, g, 1],
            device_id={"dom": d - 1},
        )

    def goes_up(k, g):
        return (d < N_DOM - 1) if k < 2 else ((d < N_DOM - 1) & (g == 0))

    def goes_down(k, g):
        return (d > 0) if k < 2 else ((d > 0) & (g == 1))

    def comes_up(k, g):
        return (d > 0) if k < 2 else ((d > 0) & (g == 0))

    def comes_down(k, g):
        return (d < N_DOM - 1) if k < 2 else ((d < N_DOM - 1) & (g == 1))

    def send_halo(k, g):
        @pl.when(goes_up(k, g))
        def _():
            up_copy(k, g).start()

        @pl.when(goes_down(k, g))
        def _():
            down_copy(k, g).start()

    def take_halo(k, g):
        @pl.when(comes_up(k, g))
        def _():
            up_copy(k, g).wait_recv()

        @pl.when(comes_down(k, g))
        def _():
            down_copy(k, g).wait_recv()

    def halo_sent(k, g):
        @pl.when(goes_up(k, g))
        def _():
            up_copy(k, g).wait_send()

        @pl.when(goes_down(k, g))
        def _():
            down_copy(k, g).wait_send()

    def first_up(g):
        return pltpu.make_async_remote_copy(
            src_ref=own_in.at[pl.ds(SX - HALO, HALO), g],
            dst_ref=r.at[g, pl.ds(0, HALO), inner],
            send_sem=h_send.at[3, g, 0],
            recv_sem=h_recv.at[3, g, 0],
            device_id={"dom": d + 1},
        )

    def first_down(g):
        return pltpu.make_async_remote_copy(
            src_ref=own_in.at[pl.ds(0, HALO), g],
            dst_ref=r.at[g, pl.ds(SX + HALO, HALO), inner],
            send_sem=h_send.at[3, g, 1],
            recv_sem=h_recv.at[3, g, 1],
            device_id={"dom": d - 1},
        )

    def send_first(g):
        @pl.when(d < N_DOM - 1)
        def _():
            first_up(g).start()

        @pl.when(d > 0)
        def _():
            first_down(g).start()

    def take_first(g):
        @pl.when(d > 0)
        def _():
            first_up(g).wait_recv()

        @pl.when(d < N_DOM - 1)
        def _():
            first_down(g).wait_recv()

    def first_sent(g):
        @pl.when(d < N_DOM - 1)
        def _():
            first_up(g).wait_send()

        @pl.when(d > 0)
        def _():
            first_down(g).wait_send()

    def stencil(g, x, y0, level, rows):
        f = r[g, x + HALO, pl.ds(y0 + HALO, rows)]
        deep = jnp.dot(
            both_parts(f.reshape(rows * 8, NZ), 1), tz[...], preferred_element_type=F32
        )
        deep = (deep[:, :NZ] + deep[:, NZ:]).reshape(rows, 8, NZ)
        fs, images = [], []
        for part in range(0, rows, 8):
            line = r[g, x + HALO, pl.ds(y0 + part, 20)]
            f = line[HALO : HALO + 8]
            acc = deep[part : part + 8] + (potb[pl.ds(x * NY + y0 + part, 8)] + level[None]) * f
            for k in range(1, 7):
                pair = (
                    line[HALO + k : HALO + k + 8]
                    + line[HALO - k : HALO - k + 8]
                    + r[g, x + HALO + k, pl.ds(y0 + part + HALO, 8)]
                    + r[g, x + HALO - k, pl.ds(y0 + part + HALO, 8)]
                )
                acc = acc + (-0.5 * C[k]) * pair
            fs.append(f)
            images.append(acc)
        return fs, images

    def tree(parts):
        parts = [parts[j] for j in range(8)]
        while len(parts) > 1:
            parts = [a + b for a, b in zip(parts[::2], parts[1::2])]
        return parts[0]

    def place(i):
        per = NY // ROWS
        return i // per, pl.multiple_of((i % per) * ROWS, ROWS)

    none = jnp.zeros((8, NZ), F32)

    def level_of(g):
        return jnp.broadcast_to(lev[g], (8, NZ))

    def main(k, g, between):
        level = level_of(g)
        coeff = tot[g, 0] * energy[...]
        coeff = jnp.where(lanes < SLOTS, coeff, pltpu.roll(coeff, SLOTS, 1))
        lhs[...] = both_parts(coeff, 0)

        def body(i, carry):
            rr, rw, acc = carry
            pl.when(i == BREAK)(between)
            x, y0 = place(i)
            fs, images = stencil(g, x, y0, level, ROWS)
            left = lhs[:, : 2 * SLOTS]
            for n, (f, image) in enumerate(zip(fs, images)):
                row = x * NY + y0 + n * 8
                blocks = []
                for j in range(8):
                    v = jnp.dot(left, table[row + j], preferred_element_type=F32)
                    blocks.append(image[j] + (v[:8] + v[8:]))
                for j in range(8):
                    w[k % 2, g, x, y0 + n * 8 + j] = blocks[j]
                rr = rr + tree(f * f)
                rw = rw + tree([f[j] * blocks[j] for j in range(8)])
                acc = project(blocks, row, acc)
            return rr, rw, acc

        rr, rw, acc = lax.fori_loop(
            0, SX * NY // ROWS, body, (none, none, jnp.zeros((16, 2 * SLOTS), F32))
        )
        send_sums(k, g, rr, rw)
        send_projections(k + 1, g, acc)
        send_halo(k, g)

    def last(g):
        level = level_of(g)

        def body(i, carry):
            rr, rw = carry
            x, y0 = place(i)
            for f, image in zip(*stencil(g, x, y0, level, ROWS)):
                rr, rw = rr + tree(f * f), rw + tree(f * image)
            return rr, rw

        rr, rw = lax.fori_loop(0, SX * NY // ROWS, body, (none, none))
        own = (lanes >= ATOM_DEV) & (lanes < 2 * ATOM_DEV)
        t = tot[g, 0]
        rw = rw + jnp.where(own, t * t * energy[...], 0.0)
        send_sums(3, g, rr, rw)

    def update(k, g):
        alpha, beta = take_sums(k - 1, g)
        t = gathered_projections(k, g)
        if k > 1:
            t = t + beta * tot[g, 1]
        tot[g, 1] = t
        tot[g, 0] = tot[g, 0] - alpha * t
        a, b = alpha[None], beta[None]

        def own(i, _):
            x = i // 4
            y0 = pl.multiple_of((i % 4) * 8, 8)
            step = w[(k - 1) % 2, g, x, pl.ds(y0, 8)]
            if k > 1:
                step = step + b * s[g, x + HALO, pl.ds(y0, 8)]
            if k < 3:
                s[g, x + HALO, pl.ds(y0, 8)] = step
            new = r[g, x + HALO, pl.ds(y0 + HALO, 8)] - a * step
            r[g, x + HALO, pl.ds(y0 + HALO, 8)] = new
            if k < 3:
                hist[k - 1, g, x, pl.ds(y0, 8)] = new
            return 0

        lax.fori_loop(0, SX * 4, own, 0)
        take_halo(k - 1, g)

        if k < 3:

            def side(i, _):
                x = i // 4
                y0 = pl.multiple_of((i % 4) * 8, 8)
                to = jnp.where(x < HALO, x, x + SX)
                step = hb[k - 1, g, x, pl.ds(y0, 8)]
                if k > 1:
                    step = step + b * s[g, to, pl.ds(y0, 8)]
                s[g, to, pl.ds(y0, 8)] = step
                r[g, to, pl.ds(y0 + HALO, 8)] = r[g, to, pl.ds(y0 + HALO, 8)] - a * step
                return 0

            lax.fori_loop(0, 2 * HALO * 4, side, 0)
        else:
            base = jnp.where(g == 0, 0, HALO + SX)
            other = HALO + SX - base

            def one_side(i, _):
                x = i // 4
                y0 = pl.multiple_of((i % 4) * 8, 8)
                step = hb2[g, x, pl.ds(y0, 8)] + b * s[g, base + x, pl.ds(y0, 8)]
                new = r[g, base + x, pl.ds(y0 + HALO, 8)] - a * step
                r[g, base + x, pl.ds(y0 + HALO, 8)] = new + new
                r[g, other + x, pl.ds(y0 + HALO, 8)] = jnp.zeros((8, 8, NZ), F32)
                return 0

            lax.fori_loop(0, HALO * 4, one_side, 0)

    def each(body):
        def run(g, _):
            body(g)
            return 0

        lax.fori_loop(0, 2, run, 0)

    def begin(i, acc):
        x = i // 4
        y0 = pl.multiple_of((i % 4) * 8, 8)
        row = pl.multiple_of(i * 8, 8)
        left = []
        for j in range(8):
            left.append(
                jnp.concatenate([both_parts(own_in[x, g, y0 + j], 0) for g in range(2)], axis=0)
            )
        right = []
        for j in range(8):
            right.append(table[row + j].astype(F32).T.astype(BF16))
            turned[pl.ds(pl.multiple_of((row + j) * NZ, NZ), NZ), :] = right[-1]
        return acc + jnp.dot(
            jnp.concatenate(left, axis=1),
            jnp.concatenate(right, axis=0),
            preferred_element_type=F32,
        )

    send_first(0)
    acc = lax.fori_loop(0, SX * NY // 8, begin, jnp.zeros((32, 2 * SLOTS), F32))
    send_projections(0, 0, acc[:16])
    send_projections(0, 1, acc[16:])
    send_first(1)

    def spread(i, _):
        rows = pot_in[pl.ds(pl.multiple_of(i * 8, 8), 8), :]
        for j in range(8):
            potb[i * 8 + j] = jnp.broadcast_to(rows[j : j + 1, :], (8, NZ))
        return 0

    lax.fori_loop(0, SX * NY // 8, spread, 0)

    def pass_on(k, g):
        forward_sums(k - 1 + g, 1 - g)

    def first(g):
        take_first(g)
        tot[g, 0] = gathered_projections(0, g)

        def between():
            @pl.when(g == 1)
            def _():
                pass_on(0, g)

        main(0, g, between)

    each(first)

    for k in (1, 2):

        def turn(g, k=k):
            update(k, g)
            main(k, g, lambda: pass_on(k, g))

        each(turn)
        each(lambda g, k=k: halo_sent(k - 1, g))

    each(first_sent)

    def closing(g):
        update(3, g)
        pass_on(3, g)
        last(g)

    each(closing)
    forward_sums(3, 1)
    each(lambda g: halo_sent(2, g))

    def finish(g):
        a3, b3 = take_sums(3, g)
        g3 = a3
        g2 = scal[g, 2] + b3 * g3
        g1 = scal[g, 1] + scal[g, 6] * g2
        g0 = scal[g, 0] + scal[g, 5] * g1

        def body(i, _):
            x = i // 4
            y0 = pl.multiple_of((i % 4) * 8, 8)
            value = (
                g0[None] * own_in[x, g, pl.ds(y0, 8)]
                + g1[None] * hist[0, g, x, pl.ds(y0, 8)]
                + g2[None] * hist[1, g, x, pl.ds(y0, 8)]
                + g3[None] * r[g, x + HALO, pl.ds(y0 + HALO, 8)]
            )
            x_out[x, g, pl.ds(y0, 8)] = value
            part = 4.0 * jnp.sum(value * orb[x, g, pl.ds(y0, 8)], axis=1)
            dens[x, pl.ds(y0, 8), :] = jnp.where(g == 0, part, dens[x, pl.ds(y0, 8), :] + part)
            return 0

        lax.fori_loop(0, SX * 4, body, 0)

    def clear_dens(i, _):
        dens[i] = jnp.zeros((NY, NZ), F32)
        return 0

    lax.fori_loop(0, SX, clear_dens, 0)
    each(finish)

    def rows_of(block):
        return pl.ds(pl.multiple_of(block * (NY // blocks_st), NY // blocks_st), NY // blocks_st)

    def block_copy(i, source):
        return pltpu.make_async_remote_copy(
            src_ref=dens.at[:, rows_of(other_block(i)), :],
            dst_ref=parts.at[source],
            send_sem=d_send.at[i],
            recv_sem=d_recv.at[i],
            device_id={"st": other_block(i)},
        )

    for i in range(1, blocks_st):
        block_copy(i, me).start()
    parts[me] = dens[:, rows_of(me), :]
    for i in range(1, blocks_st):
        block_copy(i, (me + blocks_st - i) % blocks_st).wait_recv()
    total = parts[0]
    for i in range(1, blocks_st):
        total = total + parts[i]
    dens_out[...] = total
    for i in range(1, blocks_st):
        block_copy(i, me).wait_send()


def solve(table, orb, pot, pert, lev, energy, tz, blocks_st):
    vmem = pl.BlockSpec(memory_space=pltpu.VMEM)
    dma = pltpu.SemaphoreType.DMA
    return pl.pallas_call(
        solve_kernel,
        out_shape=(
            jax.ShapeDtypeStruct((SX, 2, NY, 8, NZ), F32),
            jax.ShapeDtypeStruct((SX, NY // blocks_st, NZ), F32),
        ),
        in_specs=[vmem] * 7,
        out_specs=(vmem, vmem),
        scratch_shapes=[
            pltpu.VMEM((SX, 2, NY, 8, NZ), F32),
            pltpu.VMEM((SX * NY * NZ, 2 * SLOTS), BF16),
            pltpu.VMEM((2, EXT, NYP, 8, NZ), F32),
            pltpu.VMEM((2, EXT, NY, 8, NZ), F32),
            pltpu.VMEM((2, 2, SX, NY, 8, NZ), F32),
            pltpu.VMEM((2, 2, 2 * HALO, NY, 8, NZ), F32),
            pltpu.VMEM((2, HALO, NY, 8, NZ), F32),
            pltpu.VMEM((2, 2, SX, NY, 8, NZ), F32),
            pltpu.VMEM((SX * NY, 8, NZ), F32),
            pltpu.VMEM((4, 2, PLANE, 8, NZ), F32),
            pltpu.VMEM((4, 2, DEPTH, 8, NZ), F32),
            pltpu.VMEM((4, 2, 4, 8, NZ), F32),
            pltpu.VMEM((4, 2, 2, 8, NZ), F32),
            pltpu.VMEM((4, 2, 8, NZ), F32),
            pltpu.VMEM((2, 12, 8, NZ), F32),
            pltpu.VMEM((2, 2, 8, NZ), F32),
            pltpu.VMEM((16, NZ), BF16),
            pltpu.VMEM((SX, NY, NZ), F32),
            pltpu.VMEM((blocks_st, SX, NY // blocks_st, NZ), F32),
            dma((4, 2, 2)),
            dma((4, 2, 2)),
            dma((2, PLANE)),
            dma((2, 2, PLANE)),
            dma((2, DEPTH)),
            dma((2, 2, DEPTH)),
            dma((2, 4)),
            dma((2, 2, 4)),
            dma((blocks_st,)),
            dma((blocks_st,)),
        ],
        compiler_params=pltpu.CompilerParams(
            collective_id=0, has_side_effects=True, vmem_limit_bytes=VMEM_MIB * 2**20
        ),
        name="bicg_solve",
    )(table, orb, pot, pert, lev, energy, tz)


def shards(orbitals, levels, potential, perturbation, projector, point_cell, point_atom, kb_energy):
    index = lax.axis_index("dom")
    orb = orbitals.reshape(2, 8, SX, NY, NZ).transpose(2, 0, 3, 1, 4)
    row = (point_cell >> 7) * SLOTS + point_atom - (index - 1) * ATOM_DEV
    place = jnp.where(point_atom >= 0, row * NZ + (point_cell & 127), UNUSED)
    table = build_table(projector, place)
    energy = lax.dynamic_slice_in_dim(
        jnp.pad(kb_energy, (ATOM_DEV, ATOM_DEV)), index * ATOM_DEV, SLOTS
    )
    energy = jnp.pad(energy, (0, NZ - SLOTS))[None]
    lev = (-1.5 * C[0]) - levels.reshape(2, 8, 1)
    tz = jnp.asarray(depth_matrix())
    turned, density = solve(
        table, orb, potential.reshape(SX * NY, NZ), perturbation.reshape(SX * NY, NZ), lev, energy, tz,
        lax.axis_size("st"),
    )
    response = turned.transpose(1, 3, 0, 2, 4).reshape(orbitals.shape)
    return response, density


def solution(mesh):
    in_specs = (
        P("st", "dom", None, None),
        P("st"),
        P("dom", None, None),
        P("dom", None, None),
        P("dom"),
        P("dom"),
        P("dom"),
        P(),
    )
    out_specs = (P("st", "dom", None, None), P("dom", "st", None))
    return jax.shard_map(shards, mesh=mesh, in_specs=in_specs, out_specs=out_specs, check_vma=False)
```

```python
import numpy as np
import jax
import jax.numpy as jnp
from jax import lax
from jax.experimental import pallas as pl
from jax.experimental.pallas import tpu as pltpu
from jax.sharding import PartitionSpec as P

ATOM_DEV = 16
SLOTS = 3 * ATOM_DEV
SX, NY, NZ = 8, 32, 128
HALO = 6
EXT = SX + 2 * HALO
NYP = NY + 2 * HALO
N_DOM = 64
PLANE = 8
DEPTH = 8
C = (
    -5369.0 / 1800.0,
    12.0 / 7.0,
    -15.0 / 56.0,
    10.0 / 189.0,
    -1.0 / 112.0,
    2.0 / 1925.0,
    -1.0 / 16632.0,
)
F32 = jnp.float32
BF16 = jnp.bfloat16
UNROLL = 8
VMEM_MIB = 43
ROWS = 32
BREAK = 2
UNUSED = SX * NY * SLOTS * NZ


def depth_matrix():
    lag = np.abs(np.arange(NZ)[:, None] - np.arange(NZ)[None, :])
    band = np.zeros((NZ, NZ), np.float32)
    for k in range(1, 7):
        band[lag == k] = -0.5 * C[k]
    high = band.astype(jnp.bfloat16)
    low = (band - high.astype(np.float32)).astype(jnp.bfloat16)
    half = np.concatenate([high, low], axis=1)
    return np.concatenate([half, half], axis=0)


def both_parts(value, axis):
    high = value.astype(BF16).astype(F32)
    return jnp.concatenate([high, value - high], axis=axis).astype(BF16)


def table_kernel(place, value, table, dense):
    slots = place.shape[0]

    def clear(i, _):
        dense[pl.ds(pl.multiple_of(i * 64, 64), 64), :] = jnp.zeros((64, NZ), F32)
        return 0

    lax.fori_loop(0, SX * NY * SLOTS // 64, clear, 0)

    def halve(_, ends):
        low, high = ends
        mid = (low + high) // 2
        used = place[jnp.minimum(mid, slots - 1)] < UNUSED
        go = low < high
        return (
            jnp.where(go & used, mid + 1, low),
            jnp.where(go & jnp.logical_not(used), mid, high),
        )

    used, _ = lax.fori_loop(0, 15, halve, (jnp.int32(0), jnp.int32(slots)))
    lanes = lax.broadcasted_iota(jnp.int32, (1, NZ), 1)

    def put(i, _):
        for u in range(UNROLL):
            where = place[i * UNROLL + u]
            pltpu.store(
                dense.at[pl.ds(where >> 7, 1), :],
                jnp.full((1, NZ), value[i * UNROLL + u], F32),
                mask=lanes == (jnp.full((1, NZ), where, jnp.int32) & 127),
            )
        return 0

    lax.fori_loop(0, (used + UNROLL - 1) // UNROLL, put, 0)

    def split(i, _):
        for j in range(4):
            row = i * 4 + j
            part = dense[pl.ds(pl.multiple_of(row * SLOTS, SLOTS), SLOTS), :]
            table[row] = both_parts(part, 0)
        return 0

    lax.fori_loop(0, SX * NY // 4, split, 0)


def build_table(projector, place):
    smem = pl.BlockSpec(memory_space=pltpu.SMEM)
    return pl.pallas_call(
        table_kernel,
        out_shape=jax.ShapeDtypeStruct((SX * NY, 2 * SLOTS, NZ), BF16),
        in_specs=[smem, smem],
        out_specs=pl.BlockSpec(memory_space=pltpu.VMEM),
        scratch_shapes=[pltpu.VMEM((SX * NY * SLOTS + 8, NZ), F32)],
        compiler_params=pltpu.CompilerParams(vmem_limit_bytes=10 * 2**20),
        cost_estimate=pl.CostEstimate(flops=0, bytes_accessed=40 * 2**20, transcendentals=0),
        name="projector_table",
    )(place, projector)


def solve_kernel(
    table, orb, pot_in, pert_in, lev, kb, tz,
    x_out, dens_out,
    energy, own_in, turned, r, s, w, hb, hb2, hist, potb, st1, st2, pj, msg, pmsg, scal, tot, lhs, dens, parts,
    h_send, h_recv, a_send, a_recv, b_send, b_recv, p_send, p_recv, d_send, d_recv,
):
    d = lax.axis_index("dom")
    zi = d // PLANE
    ji = d % PLANE
    inner = pl.ds(HALO, NY)

    zero = jnp.zeros((HALO, 8, NZ), F32)

    def clear(i, _):
        for g in range(2):
            r[g, i, pl.ds(0, HALO)] = zero
            r[g, i, pl.ds(HALO + NY, HALO)] = zero
        return 0

    lax.fori_loop(0, EXT, clear, 0)

    def start(i, _):
        x = i // 4
        y0 = pl.multiple_of((i % 4) * 8, 8)
        rows = pert_in[pl.ds(pl.multiple_of(i * 8, 8), 8), :]
        for j in range(8):
            row = jnp.broadcast_to(rows[j : j + 1, :], (8, NZ))
            for g in range(2):
                value = -row * orb[x, g, y0 + j]
                own_in[x, g, y0 + j] = value
                r[g, x + HALO, y0 + HALO + j] = value
        return 0

    lax.fori_loop(0, SX * NY // 8, start, 0)

    def clear_halo(base):
        plane = jnp.zeros((NY, 8, NZ), F32)
        far = jnp.where(base == 0, 0, SX + HALO)

        def one(i, _):
            for k in range(2):
                for g in range(2):
                    hb[k, g, base + i] = plane
            for g in range(2):
                hb2[g, i] = plane
                r[g, far + i, inner] = plane
            return 0

        lax.fori_loop(0, HALO, one, 0)

    @pl.when(d == 0)
    def _():
        clear_halo(0)

    @pl.when(d == N_DOM - 1)
    def _():
        clear_halo(HALO)

    for k in range(4):
        for g in range(2):
            pj[k, g] = jnp.zeros((4, 8, NZ), F32)

    near = ((-2, d >= 2), (-1, d >= 1), (1, d < N_DOM - 1), (2, d < N_DOM - 2))

    first_at, second_at = zi, ji

    def in_first(i):
        return ((zi + i) % DEPTH) * PLANE + ji

    def in_second(i):
        return zi * PLANE + (ji + i) % PLANE

    me = lax.axis_index("st")
    blocks_st = lax.axis_size("st")

    def other_block(i):
        return (me + i) % blocks_st

    barrier = pltpu.get_barrier_semaphore()
    count = jnp.int32(PLANE - 1 + DEPTH - 1 + blocks_st - 1)
    for i in range(1, blocks_st):
        pl.semaphore_signal(barrier, inc=1, device_id={"st": other_block(i)})
    for i in range(1, PLANE):
        pl.semaphore_signal(barrier, inc=1, device_id={"dom": in_first(i)})
    for i in range(1, DEPTH):
        pl.semaphore_signal(barrier, inc=1, device_id={"dom": in_second(i)})
    for step, there in near:
        count = count + there.astype(jnp.int32)

        @pl.when(there)
        def _(step=step):
            pl.semaphore_signal(barrier, inc=1, device_id={"dom": d + step})

    lanes = lax.broadcasted_iota(jnp.int32, (8, NZ), 1)
    line = jnp.zeros((1, NZ), F32)
    for j in range(SLOTS):
        atom = jnp.clip((d - 1) * ATOM_DEV + j, 0, kb.shape[0] - 1)
        line = jnp.where(lanes[:1] == j, kb[atom], line)
    energy[...] = line

    pl.semaphore_wait(barrier, count)

    def project(blocks, row, acc):
        left = jnp.concatenate([both_parts(b, 0) for b in blocks], axis=1)
        right = turned[pl.ds(pl.multiple_of(row * NZ, 8 * NZ), 8 * NZ), :]
        return acc + jnp.dot(left, right, preferred_element_type=F32)

    def near_copy(k, g, n):
        step = near[n][0]
        return pltpu.make_async_remote_copy(
            src_ref=pmsg.at[k, g],
            dst_ref=pj.at[k, g, 3 - n],
            send_sem=p_send.at[g, n],
            recv_sem=p_recv.at[k % 2, g, 3 - n],
            device_id={"dom": d + step},
        )

    def near_arrival(k, g, n):
        return pltpu.make_async_remote_copy(
            src_ref=pmsg.at[k, g],
            dst_ref=pj.at[k, g, n],
            send_sem=p_send.at[g, n],
            recv_sem=p_recv.at[k % 2, g, n],
            device_id={"dom": d + near[n][0]},
        )

    def send_projections(k, g, acc):
        part = acc[:8, :SLOTS] + acc[8:, :SLOTS] + acc[:8, SLOTS:] + acc[8:, SLOTS:]
        pmsg[k, g] = jnp.concatenate([part, jnp.zeros((8, NZ - SLOTS), F32)], axis=1)
        for n in range(4):

            @pl.when(near[n][1])
            def _(n=n):
                near_copy(k, g, n).start()

    def gathered_projections(k, g):
        for n in range(4):

            @pl.when(near[n][1])
            def _(n=n):
                near_arrival(k, g, n).wait_recv()
                near_copy(k, g, n).wait_send()

        total = pmsg[k, g]
        shifts = ((2 * ATOM_DEV, 0, 16), (ATOM_DEV, 0, 32), (-ATOM_DEV, 16, 48), (-2 * ATOM_DEV, 32, 48))
        for n, (back, low, high) in enumerate(shifts):
            moved = pltpu.roll(pj[k, g, n], (-back) % NZ, 1)
            total = total + jnp.where((lanes >= low) & (lanes < high), moved, 0.0)
        return total

    def first_copy(k, g, i):
        return pltpu.make_async_remote_copy(
            src_ref=msg.at[k, g, 0],
            dst_ref=st1.at[k, g, first_at],
            send_sem=a_send.at[g, i],
            recv_sem=a_recv.at[k % 2, g, i],
            device_id={"dom": in_first(i)},
        )

    def first_arrival(k, g, i):
        return pltpu.make_async_remote_copy(
            src_ref=msg.at[k, g, 0],
            dst_ref=st1.at[k, g, (first_at + PLANE - i) % PLANE],
            send_sem=a_send.at[g, i],
            recv_sem=a_recv.at[k % 2, g, i],
            device_id={"dom": in_first(i)},
        )

    def second_copy(k, g, i):
        return pltpu.make_async_remote_copy(
            src_ref=msg.at[k, g, 1],
            dst_ref=st2.at[k, g, second_at],
            send_sem=b_send.at[g, i],
            recv_sem=b_recv.at[k % 2, g, i],
            device_id={"dom": in_second(i)},
        )

    def second_arrival(k, g, i):
        return pltpu.make_async_remote_copy(
            src_ref=msg.at[k, g, 1],
            dst_ref=st2.at[k, g, (second_at + DEPTH - i) % DEPTH],
            send_sem=b_send.at[g, i],
            recv_sem=b_recv.at[k % 2, g, i],
            device_id={"dom": in_second(i)},
        )

    def send_sums(k, g, rr, rw):
        tile = jnp.where(
            lanes < 64, jnp.sum(rr, axis=1, keepdims=True), jnp.sum(rw, axis=1, keepdims=True)
        )
        msg[k, g, 0] = tile
        st1[k, g, first_at] = tile
        for i in range(1, PLANE):
            first_copy(k, g, i).start()

    def forward_sums(k, g):
        for i in range(1, PLANE):
            first_arrival(k, g, i).wait_recv()
            first_copy(k, g, i).wait_send()
        tile = st1[k, g, 0]
        for i in range(1, PLANE):
            tile = tile + st1[k, g, i]
        msg[k, g, 1] = tile
        st2[k, g, second_at] = tile
        for i in range(1, DEPTH):
            second_copy(k, g, i).start()

    def take_sums(k, g):
        for i in range(1, DEPTH):
            second_arrival(k, g, i).wait_recv()
            second_copy(k, g, i).wait_send()
        tile = st2[k, g, 0]
        for i in range(1, DEPTH):
            tile = tile + st2[k, g, i]
        rr = jnp.broadcast_to(tile[:, 0:1], (8, NZ))
        rw = jnp.broadcast_to(tile[:, 64:65], (8, NZ))
        scal[g, 8 + k] = rr
        if k == 0:
            alpha, beta = rr / rw, jnp.zeros_like(rr)
        else:
            beta = rr / scal[g, 7 + k]
            alpha = rr / (rw - beta * rr / scal[g, k - 1])
        scal[g, k] = alpha
        scal[g, 4 + k] = beta
        return alpha, beta

    def up_copy(k, g):
        dst = hb.at[k, g, pl.ds(0, HALO)] if k < 2 else hb2.at[g]
        return pltpu.make_async_remote_copy(
            src_ref=w.at[k % 2, g, pl.ds(SX - HALO, HALO)],
            dst_ref=dst,
            send_sem=h_send.at[k, g, 0],
            recv_sem=h_recv.at[k, g, 0],
            device_id={"dom": d + 1},
        )

    def down_copy(k, g):
        dst = hb.at[k, g, pl.ds(HALO, HALO)] if k < 2 else hb2.at[g]
        return pltpu.make_async_remote_copy(
            src_ref=w.at[k % 2, g, pl.ds(0, HALO)],
            dst_ref=dst,
            send_sem=h_send.at[k, g, 1],
            recv_sem=h_recv.at[k, g, 1],
            device_id={"dom": d - 1},
        )

    def goes_up(k, g):
        return (d < N_DOM - 1) if k < 2 else ((d < N_DOM - 1) & (g == 0))

    def goes_down(k, g):
        return (d > 0) if k < 2 else ((d > 0) & (g == 1))

    def comes_up(k, g):
        return (d > 0) if k < 2 else ((d > 0) & (g == 0))

    def comes_down(k, g):
        return (d < N_DOM - 1) if k < 2 else ((d < N_DOM - 1) & (g == 1))

    def send_halo(k, g):
        @pl.when(goes_up(k, g))
        def _():
            up_copy(k, g).start()

        @pl.when(goes_down(k, g))
        def _():
            down_copy(k, g).start()

    def take_halo(k, g):
        @pl.when(comes_up(k, g))
        def _():
            up_copy(k, g).wait_recv()

        @pl.when(comes_down(k, g))
        def _():
            down_copy(k, g).wait_recv()

    def halo_sent(k, g):
        @pl.when(goes_up(k, g))
        def _():
            up_copy(k, g).wait_send()

        @pl.when(goes_down(k, g))
        def _():
            down_copy(k, g).wait_send()

    def first_up(g):
        return pltpu.make_async_remote_copy(
            src_ref=own_in.at[pl.ds(SX - HALO, HALO), g],
            dst_ref=r.at[g, pl.ds(0, HALO), inner],
            send_sem=h_send.at[3, g, 0],
            recv_sem=h_recv.at[3, g, 0],
            device_id={"dom": d + 1},
        )

    def first_down(g):
        return pltpu.make_async_remote_copy(
            src_ref=own_in.at[pl.ds(0, HALO), g],
            dst_ref=r.at[g, pl.ds(SX + HALO, HALO), inner],
            send_sem=h_send.at[3, g, 1],
            recv_sem=h_recv.at[3, g, 1],
            device_id={"dom": d - 1},
        )

    def send_first(g):
        @pl.when(d < N_DOM - 1)
        def _():
            first_up(g).start()

        @pl.when(d > 0)
        def _():
            first_down(g).start()

    def take_first(g):
        @pl.when(d > 0)
        def _():
            first_up(g).wait_recv()

        @pl.when(d < N_DOM - 1)
        def _():
            first_down(g).wait_recv()

    def first_sent(g):
        @pl.when(d < N_DOM - 1)
        def _():
            first_up(g).wait_send()

        @pl.when(d > 0)
        def _():
            first_down(g).wait_send()

    def stencil(g, x, y0, level, rows):
        f = r[g, x + HALO, pl.ds(y0 + HALO, rows)]
        deep = jnp.dot(
            both_parts(f.reshape(rows * 8, NZ), 1), tz[...], preferred_element_type=F32
        )
        deep = (deep[:, :NZ] + deep[:, NZ:]).reshape(rows, 8, NZ)
        fs, images = [], []
        for part in range(0, rows, 8):
            line = r[g, x + HALO, pl.ds(y0 + part, 20)]
            f = line[HALO : HALO + 8]
            acc = deep[part : part + 8] + (potb[pl.ds(x * NY + y0 + part, 8)] + level[None]) * f
            for k in range(1, 7):
                pair = (
                    line[HALO + k : HALO + k + 8]
                    + line[HALO - k : HALO - k + 8]
                    + r[g, x + HALO + k, pl.ds(y0 + part + HALO, 8)]
                    + r[g, x + HALO - k, pl.ds(y0 + part + HALO, 8)]
                )
                acc = acc + (-0.5 * C[k]) * pair
            fs.append(f)
            images.append(acc)
        return fs, images

    def tree(parts):
        parts = [parts[j] for j in range(8)]
        while len(parts) > 1:
            parts = [a + b for a, b in zip(parts[::2], parts[1::2])]
        return parts[0]

    def place(i):
        per = NY // ROWS
        return i // per, pl.multiple_of((i % per) * ROWS, ROWS)

    none = jnp.zeros((8, NZ), F32)

    def level_of(g):
        rows = lax.broadcasted_iota(jnp.int32, (8, NZ), 0)
        value = none
        for j in range(8):
            value = jnp.where(rows == j, -1.5 * C[0] - lev[g * 8 + j], value)
        return value

    def main(k, g, between):
        level = level_of(g)
        coeff = tot[g, 0] * energy[...]
        coeff = jnp.where(lanes < SLOTS, coeff, pltpu.roll(coeff, SLOTS, 1))
        lhs[...] = both_parts(coeff, 0)

        def body(i, carry):
            rr, rw, acc = carry
            pl.when(i == BREAK)(between)
            x, y0 = place(i)
            fs, images = stencil(g, x, y0, level, ROWS)
            left = lhs[:, : 2 * SLOTS]
            for n, (f, image) in enumerate(zip(fs, images)):
                row = x * NY + y0 + n * 8
                right = jnp.concatenate([table[row + j] for j in range(8)], axis=1)
                v = jnp.dot(left, right, preferred_element_type=F32)
                v = v[:8] + v[8:]
                blocks = [image[j] + v[:, j * NZ : (j + 1) * NZ] for j in range(8)]
                for j in range(8):
                    w[k % 2, g, x, y0 + n * 8 + j] = blocks[j]
                rr = rr + tree(f * f)
                rw = rw + tree([f[j] * blocks[j] for j in range(8)])
                acc = project(blocks, row, acc)
            return rr, rw, acc

        rr, rw, acc = lax.fori_loop(
            0, SX * NY // ROWS, body, (none, none, jnp.zeros((16, 2 * SLOTS), F32))
        )
        send_sums(k, g, rr, rw)
        send_projections(k + 1, g, acc)
        send_halo(k, g)

    def last(g):
        level = level_of(g)

        def body(i, carry):
            rr, rw = carry
            x, y0 = place(i)
            for f, image in zip(*stencil(g, x, y0, level, ROWS)):
                rr, rw = rr + tree(f * f), rw + tree(f * image)
            return rr, rw

        rr, rw = lax.fori_loop(0, SX * NY // ROWS, body, (none, none))
        own = (lanes >= ATOM_DEV) & (lanes < 2 * ATOM_DEV)
        t = tot[g, 0]
        rw = rw + jnp.where(own, t * t * energy[...], 0.0)
        send_sums(3, g, rr, rw)

    def update(k, g):
        alpha, beta = take_sums(k - 1, g)
        t = gathered_projections(k, g)
        if k > 1:
            t = t + beta * tot[g, 1]
        tot[g, 1] = t
        tot[g, 0] = tot[g, 0] - alpha * t
        a, b = alpha[None], beta[None]

        def own(i, _):
            x = i // 4
            y0 = pl.multiple_of((i % 4) * 8, 8)
            step = w[(k - 1) % 2, g, x, pl.ds(y0, 8)]
            if k > 1:
                step = step + b * s[g, x + HALO, pl.ds(y0, 8)]
            if k < 3:
                s[g, x + HALO, pl.ds(y0, 8)] = step
            new = r[g, x + HALO, pl.ds(y0 + HALO, 8)] - a * step
            r[g, x + HALO, pl.ds(y0 + HALO, 8)] = new
            if k < 3:
                hist[k - 1, g, x, pl.ds(y0, 8)] = new
            return 0

        lax.fori_loop(0, SX * 4, own, 0)
        take_halo(k - 1, g)

        if k < 3:

            def side(i, _):
                x = i // 4
                y0 = pl.multiple_of((i % 4) * 8, 8)
                to = jnp.where(x < HALO, x, x + SX)
                step = hb[k - 1, g, x, pl.ds(y0, 8)]
                if k > 1:
                    step = step + b * s[g, to, pl.ds(y0, 8)]
                s[g, to, pl.ds(y0, 8)] = step
                r[g, to, pl.ds(y0 + HALO, 8)] = r[g, to, pl.ds(y0 + HALO, 8)] - a * step
                return 0

            lax.fori_loop(0, 2 * HALO * 4, side, 0)
        else:
            base = jnp.where(g == 0, 0, HALO + SX)
            other = HALO + SX - base

            def one_side(i, _):
                x = i // 4
                y0 = pl.multiple_of((i % 4) * 8, 8)
                step = hb2[g, x, pl.ds(y0, 8)] + b * s[g, base + x, pl.ds(y0, 8)]
                new = r[g, base + x, pl.ds(y0 + HALO, 8)] - a * step
                r[g, base + x, pl.ds(y0 + HALO, 8)] = new + new
                r[g, other + x, pl.ds(y0 + HALO, 8)] = jnp.zeros((8, 8, NZ), F32)
                return 0

            lax.fori_loop(0, HALO * 4, one_side, 0)

    def each(body):
        def run(g, _):
            body(g)
            return 0

        lax.fori_loop(0, 2, run, 0)

    def begin(i, acc):
        x = i // 4
        y0 = pl.multiple_of((i % 4) * 8, 8)
        row = pl.multiple_of(i * 8, 8)
        left = []
        for j in range(8):
            left.append(
                jnp.concatenate([both_parts(own_in[x, g, y0 + j], 0) for g in range(2)], axis=0)
            )
        right = []
        for j in range(8):
            right.append(table[row + j].astype(F32).T.astype(BF16))
            turned[pl.ds(pl.multiple_of((row + j) * NZ, NZ), NZ), :] = right[-1]
        return acc + jnp.dot(
            jnp.concatenate(left, axis=1),
            jnp.concatenate(right, axis=0),
            preferred_element_type=F32,
        )

    send_first(0)
    acc = lax.fori_loop(0, SX * NY // 8, begin, jnp.zeros((32, 2 * SLOTS), F32))
    send_projections(0, 0, acc[:16])
    send_projections(0, 1, acc[16:])
    send_first(1)

    def spread(i, _):
        rows = pot_in[pl.ds(pl.multiple_of(i * 8, 8), 8), :]
        for j in range(8):
            potb[i * 8 + j] = jnp.broadcast_to(rows[j : j + 1, :], (8, NZ))
        return 0

    lax.fori_loop(0, SX * NY // 8, spread, 0)

    def pass_on(k, g):
        forward_sums(k - 1 + g, 1 - g)

    def first(g):
        take_first(g)
        tot[g, 0] = gathered_projections(0, g)

        def between():
            @pl.when(g == 1)
            def _():
                pass_on(0, g)

        main(0, g, between)

    each(first)

    for k in (1, 2):

        def turn(g, k=k):
            update(k, g)
            main(k, g, lambda: pass_on(k, g))

        each(turn)
        each(lambda g, k=k: halo_sent(k - 1, g))

    each(first_sent)

    def closing(g):
        update(3, g)
        pass_on(3, g)
        last(g)

    each(closing)
    forward_sums(3, 1)
    each(lambda g: halo_sent(2, g))

    def finish(g):
        a3, b3 = take_sums(3, g)
        g3 = a3
        g2 = scal[g, 2] + b3 * g3
        g1 = scal[g, 1] + scal[g, 6] * g2
        g0 = scal[g, 0] + scal[g, 5] * g1

        def body(i, _):
            x = i // 4
            y0 = pl.multiple_of((i % 4) * 8, 8)
            value = (
                g0[None] * own_in[x, g, pl.ds(y0, 8)]
                + g1[None] * hist[0, g, x, pl.ds(y0, 8)]
                + g2[None] * hist[1, g, x, pl.ds(y0, 8)]
                + g3[None] * r[g, x + HALO, pl.ds(y0 + HALO, 8)]
            )
            x_out[x, g, pl.ds(y0, 8)] = value
            part = 4.0 * jnp.sum(value * orb[x, g, pl.ds(y0, 8)], axis=1)
            dens[x, pl.ds(y0, 8), :] = jnp.where(g == 0, part, dens[x, pl.ds(y0, 8), :] + part)
            return 0

        lax.fori_loop(0, SX * 4, body, 0)

    def clear_dens(i, _):
        dens[i] = jnp.zeros((NY, NZ), F32)
        return 0

    lax.fori_loop(0, SX, clear_dens, 0)
    each(finish)

    def rows_of(block):
        return pl.ds(pl.multiple_of(block * (NY // blocks_st), NY // blocks_st), NY // blocks_st)

    def block_copy(i, source):
        return pltpu.make_async_remote_copy(
            src_ref=dens.at[:, rows_of(other_block(i)), :],
            dst_ref=parts.at[source],
            send_sem=d_send.at[i],
            recv_sem=d_recv.at[i],
            device_id={"st": other_block(i)},
        )

    for i in range(1, blocks_st):
        block_copy(i, me).start()
    parts[me] = dens[:, rows_of(me), :]
    for i in range(1, blocks_st):
        block_copy(i, (me + blocks_st - i) % blocks_st).wait_recv()
    total = parts[0]
    for i in range(1, blocks_st):
        total = total + parts[i]
    dens_out[...] = total
    for i in range(1, blocks_st):
        block_copy(i, me).wait_send()


def solve(table, orb, pot, pert, lev, kb, tz, blocks_st):
    vmem = pl.BlockSpec(memory_space=pltpu.VMEM)
    dma = pltpu.SemaphoreType.DMA
    return pl.pallas_call(
        solve_kernel,
        out_shape=(
            jax.ShapeDtypeStruct((SX, 2, NY, 8, NZ), F32),
            jax.ShapeDtypeStruct((SX, NY // blocks_st, NZ), F32),
        ),
        in_specs=[vmem] * 4 + [pl.BlockSpec(memory_space=pltpu.SMEM)] * 2 + [vmem],
        out_specs=(vmem, vmem),
        scratch_shapes=[
            pltpu.VMEM((1, NZ), F32),
            pltpu.VMEM((SX, 2, NY, 8, NZ), F32),
            pltpu.VMEM((SX * NY * NZ, 2 * SLOTS), BF16),
            pltpu.VMEM((2, EXT, NYP, 8, NZ), F32),
            pltpu.VMEM((2, EXT, NY, 8, NZ), F32),
            pltpu.VMEM((2, 2, SX, NY, 8, NZ), F32),
            pltpu.VMEM((2, 2, 2 * HALO, NY, 8, NZ), F32),
            pltpu.VMEM((2, HALO, NY, 8, NZ), F32),
            pltpu.VMEM((2, 2, SX, NY, 8, NZ), F32),
            pltpu.VMEM((SX * NY, 8, NZ), F32),
            pltpu.VMEM((4, 2, PLANE, 8, NZ), F32),
            pltpu.VMEM((4, 2, DEPTH, 8, NZ), F32),
            pltpu.VMEM((4, 2, 4, 8, NZ), F32),
            pltpu.VMEM((4, 2, 2, 8, NZ), F32),
            pltpu.VMEM((4, 2, 8, NZ), F32),
            pltpu.VMEM((2, 12, 8, NZ), F32),
            pltpu.VMEM((2, 2, 8, NZ), F32),
            pltpu.VMEM((16, NZ), BF16),
            pltpu.VMEM((SX, NY, NZ), F32),
            pltpu.VMEM((blocks_st, SX, NY // blocks_st, NZ), F32),
            dma((4, 2, 2)),
            dma((4, 2, 2)),
            dma((2, PLANE)),
            dma((2, 2, PLANE)),
            dma((2, DEPTH)),
            dma((2, 2, DEPTH)),
            dma((2, 4)),
            dma((2, 2, 4)),
            dma((blocks_st,)),
            dma((blocks_st,)),
        ],
        compiler_params=pltpu.CompilerParams(
            collective_id=0, has_side_effects=True, vmem_limit_bytes=VMEM_MIB * 2**20
        ),
        name="bicg_solve",
    )(table, orb, pot, pert, lev, kb, tz)


def shards(orbitals, levels, potential, perturbation, projector, point_cell, point_atom, kb_energy):
    index = lax.axis_index("dom")
    orb = orbitals.reshape(2, 8, SX, NY, NZ).transpose(2, 0, 3, 1, 4)
    row = (point_cell >> 7) * SLOTS + point_atom - (index - 1) * ATOM_DEV
    place = jnp.where(point_atom >= 0, row * NZ + (point_cell & 127), UNUSED)
    table = build_table(projector, place)
    tz = jnp.asarray(depth_matrix())
    turned, density = solve(
        table, orb, potential.reshape(SX * NY, NZ), perturbation.reshape(SX * NY, NZ),
        levels, kb_energy, tz,
        lax.axis_size("st"),
    )
    response = turned.transpose(1, 3, 0, 2, 4).reshape(orbitals.shape)
    return response, density


def solution(mesh):
    in_specs = (
        P("st", "dom", None, None),
        P("st"),
        P("dom", None, None),
        P("dom", None, None),
        P("dom"),
        P("dom"),
        P("dom"),
        P(),
    )
    out_specs = (P("st", "dom", None, None), P("dom", "st", None))
    return jax.shard_map(shards, mesh=mesh, in_specs=in_specs, out_specs=out_specs, check_vma=False)
```

```python
import numpy as np
import jax
import jax.numpy as jnp
from jax import lax
from jax.experimental import pallas as pl
from jax.experimental.pallas import tpu as pltpu
from jax.sharding import PartitionSpec as P

ATOM_DEV = 16
SLOTS = 3 * ATOM_DEV
SX, NY, NZ = 8, 32, 128
HALO = 6
HALF = HALO // 2
EXT = SX + 2 * HALO
NYP = NY + 2 * HALO
N_DOM = 64
PLANE = 8
DEPTH = 8
C = (
    -5369.0 / 1800.0,
    12.0 / 7.0,
    -15.0 / 56.0,
    10.0 / 189.0,
    -1.0 / 112.0,
    2.0 / 1925.0,
    -1.0 / 16632.0,
)
F32 = jnp.float32
BF16 = jnp.bfloat16
UNROLL = 8
VMEM_MIB = 43
ROWS = 32
BREAK = 2
UNUSED = SX * NY * SLOTS * NZ


def depth_matrix():
    lag = np.abs(np.arange(NZ)[:, None] - np.arange(NZ)[None, :])
    band = np.zeros((NZ, NZ), np.float32)
    for k in range(1, 7):
        band[lag == k] = -0.5 * C[k]
    high = band.astype(jnp.bfloat16)
    low = (band - high.astype(np.float32)).astype(jnp.bfloat16)
    half = np.concatenate([high, low], axis=1)
    return np.concatenate([half, half], axis=0)


def both_parts(value, axis):
    high = value.astype(BF16).astype(F32)
    return jnp.concatenate([high, value - high], axis=axis).astype(BF16)


def table_kernel(place, value, orb, table, turned, dense, sems):
    moves = [
        pltpu.make_async_copy(orb.at[n], turned.at[:, n // 8, :, n % 8, :], sems.at[n])
        for n in range(16)
    ]
    for c in moves:
        c.start()
    slots = place.shape[0]

    def clear(i, _):
        dense[pl.ds(pl.multiple_of(i * 64, 64), 64), :] = jnp.zeros((64, NZ), F32)
        return 0

    lax.fori_loop(0, SX * NY * SLOTS // 64, clear, 0)

    def halve(_, ends):
        low, high = ends
        mid = (low + high) // 2
        used = place[jnp.minimum(mid, slots - 1)] < UNUSED
        go = low < high
        return (
            jnp.where(go & used, mid + 1, low),
            jnp.where(go & jnp.logical_not(used), mid, high),
        )

    used, _ = lax.fori_loop(0, 15, halve, (jnp.int32(0), jnp.int32(slots)))
    lanes = lax.broadcasted_iota(jnp.int32, (1, NZ), 1)

    def put(i, _):
        for u in range(UNROLL):
            where = place[i * UNROLL + u]
            pltpu.store(
                dense.at[pl.ds(where >> 7, 1), :],
                jnp.full((1, NZ), value[i * UNROLL + u], F32),
                mask=lanes == (jnp.full((1, NZ), where, jnp.int32) & 127),
            )
        return 0

    lax.fori_loop(0, (used + UNROLL - 1) // UNROLL, put, 0)

    def split(i, _):
        for j in range(4):
            row = i * 4 + j
            part = dense[pl.ds(pl.multiple_of(row * SLOTS, SLOTS), SLOTS), :]
            table[row] = both_parts(part, 0)
        return 0

    lax.fori_loop(0, SX * NY // 4, split, 0)
    for c in moves:
        c.wait()


def build_table(projector, place, orbitals):
    smem = pl.BlockSpec(memory_space=pltpu.SMEM)
    return pl.pallas_call(
        table_kernel,
        out_shape=(
            jax.ShapeDtypeStruct((SX * NY, 2 * SLOTS, NZ), BF16),
            jax.ShapeDtypeStruct((SX, 2, NY, 8, NZ), F32),
        ),
        in_specs=[smem, smem, pl.BlockSpec(memory_space=pl.ANY)],
        out_specs=(pl.BlockSpec(memory_space=pltpu.VMEM), pl.BlockSpec(memory_space=pltpu.VMEM)),
        scratch_shapes=[
            pltpu.VMEM((SX * NY * SLOTS + 8, NZ), F32),
            pltpu.SemaphoreType.DMA((16,)),
        ],
        compiler_params=pltpu.CompilerParams(vmem_limit_bytes=10 * 2**20),
        cost_estimate=pl.CostEstimate(flops=0, bytes_accessed=40 * 2**20, transcendentals=0),
        name="projector_table",
    )(place, projector, orbitals)


def solve_kernel(
    table, orb, pot_in, pert_in, lev, kb, tz,
    x_out, dens_out,
    energy, own_in, turned, r, s, w, hb, hb2, hist, potb, st1, st2, pj, msg, pmsg, scal, tot, lhs, dens, parts,
    h_send, h_recv, a_send, a_recv, b_send, b_recv, p_send, p_recv, d_send, d_recv,
):
    d = lax.axis_index("dom")
    zi = d // PLANE
    ji = d % PLANE
    inner = pl.ds(HALO, NY)

    zero = jnp.zeros((HALO, 8, NZ), F32)

    def clear(i, _):
        for g in range(2):
            r[g, i, pl.ds(0, HALO)] = zero
            r[g, i, pl.ds(HALO + NY, HALO)] = zero
        return 0

    lax.fori_loop(0, EXT, clear, 0)

    def start(i, _):
        x = i // 4
        y0 = pl.multiple_of((i % 4) * 8, 8)
        rows = pert_in[pl.ds(pl.multiple_of(i * 8, 8), 8), :]
        for j in range(8):
            row = jnp.broadcast_to(rows[j : j + 1, :], (8, NZ))
            for g in range(2):
                value = -row * orb[x, g, y0 + j]
                own_in[x, g, y0 + j] = value
                r[g, x + HALO, y0 + HALO + j] = value
        return 0

    lax.fori_loop(0, SX * NY // 8, start, 0)

    def clear_halo(base):
        plane = jnp.zeros((NY, 8, NZ), F32)
        far = jnp.where(base == 0, 0, SX + HALO)

        def one(i, _):
            for k in range(2):
                for g in range(2):
                    hb[k, g, base + i] = plane
            for g in range(2):
                hb2[g, i] = plane
                r[g, far + i, inner] = plane
            return 0

        lax.fori_loop(0, HALO, one, 0)

    @pl.when(d == 0)
    def _():
        clear_halo(0)

    @pl.when(d == N_DOM - 1)
    def _():
        clear_halo(HALO)

    for k in range(4):
        for g in range(2):
            pj[k, g] = jnp.zeros((4, 8, NZ), F32)

    near = ((-2, d >= 2), (-1, d >= 1), (1, d < N_DOM - 1), (2, d < N_DOM - 2))

    first_at, second_at = zi, ji

    def in_first(i):
        return ((zi + i) % DEPTH) * PLANE + ji

    def in_second(i):
        return zi * PLANE + (ji + i) % PLANE

    me = lax.axis_index("st")
    blocks_st = lax.axis_size("st")

    def other_block(i):
        return (me + i) % blocks_st

    barrier = pltpu.get_barrier_semaphore()
    count = jnp.int32(PLANE - 1 + DEPTH - 1 + blocks_st - 1)
    for i in range(1, blocks_st):
        pl.semaphore_signal(barrier, inc=1, device_id={"st": other_block(i)})
    for i in range(1, PLANE):
        pl.semaphore_signal(barrier, inc=1, device_id={"dom": in_first(i)})
    for i in range(1, DEPTH):
        pl.semaphore_signal(barrier, inc=1, device_id={"dom": in_second(i)})
    for step, there in near:
        count = count + there.astype(jnp.int32)

        @pl.when(there)
        def _(step=step):
            pl.semaphore_signal(barrier, inc=1, device_id={"dom": d + step})

    lanes = lax.broadcasted_iota(jnp.int32, (8, NZ), 1)
    line = jnp.zeros((1, NZ), F32)
    for j in range(SLOTS):
        atom = jnp.clip((d - 1) * ATOM_DEV + j, 0, kb.shape[0] - 1)
        line = jnp.where(lanes[:1] == j, kb[atom], line)
    energy[...] = line

    pl.semaphore_wait(barrier, count)

    def project(blocks, row, acc):
        left = jnp.concatenate([both_parts(b, 0) for b in blocks], axis=1)
        right = turned[pl.ds(pl.multiple_of(row * NZ, 8 * NZ), 8 * NZ), :]
        return acc + jnp.dot(left, right, preferred_element_type=F32)

    def near_copy(k, g, n):
        step = near[n][0]
        return pltpu.make_async_remote_copy(
            src_ref=pmsg.at[k, g],
            dst_ref=pj.at[k, g, 3 - n],
            send_sem=p_send.at[g, n],
            recv_sem=p_recv.at[k % 2, g, 3 - n],
            device_id={"dom": d + step},
        )

    def near_arrival(k, g, n):
        return pltpu.make_async_remote_copy(
            src_ref=pmsg.at[k, g],
            dst_ref=pj.at[k, g, n],
            send_sem=p_send.at[g, n],
            recv_sem=p_recv.at[k % 2, g, n],
            device_id={"dom": d + near[n][0]},
        )

    def send_projections(k, g, acc):
        part = acc[:8, :SLOTS] + acc[8:, :SLOTS] + acc[:8, SLOTS:] + acc[8:, SLOTS:]
        pmsg[k, g] = jnp.concatenate([part, jnp.zeros((8, NZ - SLOTS), F32)], axis=1)
        for n in range(4):

            @pl.when(near[n][1])
            def _(n=n):
                near_copy(k, g, n).start()

    def gathered_projections(k, g):
        for n in range(4):

            @pl.when(near[n][1])
            def _(n=n):
                near_arrival(k, g, n).wait_recv()
                near_copy(k, g, n).wait_send()

        total = pmsg[k, g]
        shifts = ((2 * ATOM_DEV, 0, 16), (ATOM_DEV, 0, 32), (-ATOM_DEV, 16, 48), (-2 * ATOM_DEV, 32, 48))
        for n, (back, low, high) in enumerate(shifts):
            moved = pltpu.roll(pj[k, g, n], (-back) % NZ, 1)
            total = total + jnp.where((lanes >= low) & (lanes < high), moved, 0.0)
        return total

    def first_copy(k, g, i):
        return pltpu.make_async_remote_copy(
            src_ref=msg.at[k, g, 0],
            dst_ref=st1.at[k, g, first_at],
            send_sem=a_send.at[g, i],
            recv_sem=a_recv.at[k % 2, g, i],
            device_id={"dom": in_first(i)},
        )

    def first_arrival(k, g, i):
        return pltpu.make_async_remote_copy(
            src_ref=msg.at[k, g, 0],
            dst_ref=st1.at[k, g, (first_at + PLANE - i) % PLANE],
            send_sem=a_send.at[g, i],
            recv_sem=a_recv.at[k % 2, g, i],
            device_id={"dom": in_first(i)},
        )

    def second_copy(k, g, i):
        return pltpu.make_async_remote_copy(
            src_ref=msg.at[k, g, 1],
            dst_ref=st2.at[k, g, second_at],
            send_sem=b_send.at[g, i],
            recv_sem=b_recv.at[k % 2, g, i],
            device_id={"dom": in_second(i)},
        )

    def second_arrival(k, g, i):
        return pltpu.make_async_remote_copy(
            src_ref=msg.at[k, g, 1],
            dst_ref=st2.at[k, g, (second_at + DEPTH - i) % DEPTH],
            send_sem=b_send.at[g, i],
            recv_sem=b_recv.at[k % 2, g, i],
            device_id={"dom": in_second(i)},
        )

    def send_sums(k, g, rr, rw):
        tile = jnp.where(
            lanes < 64, jnp.sum(rr, axis=1, keepdims=True), jnp.sum(rw, axis=1, keepdims=True)
        )
        msg[k, g, 0] = tile
        st1[k, g, first_at] = tile
        for i in range(1, PLANE):
            first_copy(k, g, i).start()

    def forward_sums(k, g):
        for i in range(1, PLANE):
            first_arrival(k, g, i).wait_recv()
            first_copy(k, g, i).wait_send()
        tile = st1[k, g, 0]
        for i in range(1, PLANE):
            tile = tile + st1[k, g, i]
        msg[k, g, 1] = tile
        st2[k, g, second_at] = tile
        for i in range(1, DEPTH):
            second_copy(k, g, i).start()

    def take_sums(k, g):
        for i in range(1, DEPTH):
            second_arrival(k, g, i).wait_recv()
            second_copy(k, g, i).wait_send()
        tile = st2[k, g, 0]
        for i in range(1, DEPTH):
            tile = tile + st2[k, g, i]
        rr = jnp.broadcast_to(tile[:, 0:1], (8, NZ))
        rw = jnp.broadcast_to(tile[:, 64:65], (8, NZ))
        scal[g, 8 + k] = rr
        if k == 0:
            alpha, beta = rr / rw, jnp.zeros_like(rr)
        else:
            beta = rr / scal[g, 7 + k]
            alpha = rr / (rw - beta * rr / scal[g, k - 1])
        scal[g, k] = alpha
        scal[g, 4 + k] = beta
        return alpha, beta

    def up_copy(k, g):
        planes = HALO if k < 2 else HALF
        dst = hb.at[k, g, pl.ds(0, HALO)] if k < 2 else hb2.at[g, pl.ds(0, HALF)]
        return pltpu.make_async_remote_copy(
            src_ref=w.at[k % 2, g, pl.ds(SX - planes, planes)],
            dst_ref=dst,
            send_sem=h_send.at[k, g, 0],
            recv_sem=h_recv.at[k, g, 0],
            device_id={"dom": d + 1},
        )

    def down_copy(k, g):
        planes = HALO if k < 2 else HALF
        dst = hb.at[k, g, pl.ds(HALO, HALO)] if k < 2 else hb2.at[g, pl.ds(HALF, HALF)]
        return pltpu.make_async_remote_copy(
            src_ref=w.at[k % 2, g, pl.ds(0, planes)],
            dst_ref=dst,
            send_sem=h_send.at[k, g, 1],
            recv_sem=h_recv.at[k, g, 1],
            device_id={"dom": d - 1},
        )

    def goes_up(k, g):
        return d < N_DOM - 1

    def goes_down(k, g):
        return d > 0

    def comes_up(k, g):
        return d > 0

    def comes_down(k, g):
        return d < N_DOM - 1

    def send_halo(k, g):
        @pl.when(goes_up(k, g))
        def _():
            up_copy(k, g).start()

        @pl.when(goes_down(k, g))
        def _():
            down_copy(k, g).start()

    def take_halo(k, g):
        @pl.when(comes_up(k, g))
        def _():
            up_copy(k, g).wait_recv()

        @pl.when(comes_down(k, g))
        def _():
            down_copy(k, g).wait_recv()

    def halo_sent(k, g):
        @pl.when(goes_up(k, g))
        def _():
            up_copy(k, g).wait_send()

        @pl.when(goes_down(k, g))
        def _():
            down_copy(k, g).wait_send()

    def first_up(g):
        return pltpu.make_async_remote_copy(
            src_ref=own_in.at[pl.ds(SX - HALO, HALO), g],
            dst_ref=r.at[g, pl.ds(0, HALO), inner],
            send_sem=h_send.at[3, g, 0],
            recv_sem=h_recv.at[3, g, 0],
            device_id={"dom": d + 1},
        )

    def first_down(g):
        return pltpu.make_async_remote_copy(
            src_ref=own_in.at[pl.ds(0, HALO), g],
            dst_ref=r.at[g, pl.ds(SX + HALO, HALO), inner],
            send_sem=h_send.at[3, g, 1],
            recv_sem=h_recv.at[3, g, 1],
            device_id={"dom": d - 1},
        )

    def send_first(g):
        @pl.when(d < N_DOM - 1)
        def _():
            first_up(g).start()

        @pl.when(d > 0)
        def _():
            first_down(g).start()

    def take_first(g):
        @pl.when(d > 0)
        def _():
            first_up(g).wait_recv()

        @pl.when(d < N_DOM - 1)
        def _():
            first_down(g).wait_recv()

    def first_sent(g):
        @pl.when(d < N_DOM - 1)
        def _():
            first_up(g).wait_send()

        @pl.when(d > 0)
        def _():
            first_down(g).wait_send()

    def stencil(g, x, y0, level, rows):
        f = r[g, x + HALO, pl.ds(y0 + HALO, rows)]
        deep = jnp.dot(
            both_parts(f.reshape(rows * 8, NZ), 1), tz[...], preferred_element_type=F32
        )
        deep = (deep[:, :NZ] + deep[:, NZ:]).reshape(rows, 8, NZ)
        fs, images = [], []
        for part in range(0, rows, 8):
            line = r[g, x + HALO, pl.ds(y0 + part, 20)]
            f = line[HALO : HALO + 8]
            acc = deep[part : part + 8] + (potb[pl.ds(x * NY + y0 + part, 8)] + level[None]) * f
            for k in range(1, 7):
                pair = (
                    line[HALO + k : HALO + k + 8]
                    + line[HALO - k : HALO - k + 8]
                    + r[g, x + HALO + k, pl.ds(y0 + part + HALO, 8)]
                    + r[g, x + HALO - k, pl.ds(y0 + part + HALO, 8)]
                )
                acc = acc + (-0.5 * C[k]) * pair
            fs.append(f)
            images.append(acc)
        return fs, images

    def tree(parts):
        parts = [parts[j] for j in range(8)]
        while len(parts) > 1:
            parts = [a + b for a, b in zip(parts[::2], parts[1::2])]
        return parts[0]

    def place(i):
        per = NY // ROWS
        return i // per, pl.multiple_of((i % per) * ROWS, ROWS)

    none = jnp.zeros((8, NZ), F32)

    def level_of(g):
        rows = lax.broadcasted_iota(jnp.int32, (8, NZ), 0)
        value = none
        for j in range(8):
            value = jnp.where(rows == j, -1.5 * C[0] - lev[g * 8 + j], value)
        return value

    def main(k, g, between):
        level = level_of(g)
        coeff = tot[g, 0] * energy[...]
        coeff = jnp.where(lanes < SLOTS, coeff, pltpu.roll(coeff, SLOTS, 1))
        lhs[...] = both_parts(coeff, 0)

        def body(i, carry):
            rr, rw = carry
            pl.when(i == BREAK)(between)
            x, y0 = place(i)
            fs, images = stencil(g, x, y0, level, ROWS)
            left = lhs[:, : 2 * SLOTS]
            for n, (f, image) in enumerate(zip(fs, images)):
                row = x * NY + y0 + n * 8
                right = jnp.concatenate([table[row + j] for j in range(8)], axis=1)
                v = jnp.dot(left, right, preferred_element_type=F32)
                v = v[:8] + v[8:]
                blocks = [image[j] + v[:, j * NZ : (j + 1) * NZ] for j in range(8)]
                for j in range(8):
                    w[k % 2, g, x, y0 + n * 8 + j] = blocks[j]
                rr = rr + tree(f * f)
                rw = rw + tree([f[j] * blocks[j] for j in range(8)])
            return rr, rw

        rr, rw = lax.fori_loop(0, SX * NY // ROWS, body, (none, none))
        send_sums(k, g, rr, rw)
        send_halo(k, g)

        def images(i, acc):
            x = i // 2
            y0 = pl.multiple_of((i % 2) * 16, 16)
            for n in range(2):
                blocks = [w[k % 2, g, x, y0 + n * 8 + j] for j in range(8)]
                acc = project(blocks, x * NY + y0 + n * 8, acc)
            return acc

        acc = lax.fori_loop(0, SX * NY // 16, images, jnp.zeros((16, 2 * SLOTS), F32))
        send_projections(k + 1, g, acc)

    def last(g):
        level = level_of(g)

        def body(i, carry):
            rr, rw = carry
            x, y0 = place(i)

            @pl.when(x == SX - HALF)
            def _():
                for j in range(HALF):
                    r[g, SX + HALO + j, inner] = jnp.zeros((NY, 8, NZ), F32)

            for f, image in zip(*stencil(g, x, y0, level, ROWS)):
                rr, rw = rr + tree(f * f), rw + tree(f * image)
            return rr, rw

        rr, rw = lax.fori_loop(0, SX * NY // ROWS, body, (none, none))
        own = (lanes >= ATOM_DEV) & (lanes < 2 * ATOM_DEV)
        t = tot[g, 0]
        rw = rw + jnp.where(own, t * t * energy[...], 0.0)
        send_sums(3, g, rr, rw)

    def update(k, g):
        alpha, beta = take_sums(k - 1, g)
        a, b = alpha[None], beta[None]

        def own(i, _):
            x = i // 4
            y0 = pl.multiple_of((i % 4) * 8, 8)
            step = w[(k - 1) % 2, g, x, pl.ds(y0, 8)]
            if k > 1:
                step = step + b * s[g, x + HALO, pl.ds(y0, 8)]
            if k < 3:
                s[g, x + HALO, pl.ds(y0, 8)] = step
            new = r[g, x + HALO, pl.ds(y0 + HALO, 8)] - a * step
            r[g, x + HALO, pl.ds(y0 + HALO, 8)] = new
            if k < 3:
                hist[k - 1, g, x, pl.ds(y0, 8)] = new
            return 0

        lax.fori_loop(0, SX * 4, own, 0)
        take_halo(k - 1, g)

        if k < 3:

            def side(i, _):
                x = i // 4
                y0 = pl.multiple_of((i % 4) * 8, 8)
                to = jnp.where(x < HALO, x, x + SX)
                step = hb[k - 1, g, x, pl.ds(y0, 8)]
                if k > 1:
                    step = step + b * s[g, to, pl.ds(y0, 8)]
                s[g, to, pl.ds(y0, 8)] = step
                r[g, to, pl.ds(y0 + HALO, 8)] = r[g, to, pl.ds(y0 + HALO, 8)] - a * step
                return 0

            lax.fori_loop(0, 2 * HALO * 4, side, 0)
        else:
            def near_side(i, _):
                x = i // 4
                y0 = pl.multiple_of((i % 4) * 8, 8)
                to = jnp.where(x < HALF, x + HALF, x + SX + HALO - HALF)
                step = hb2[g, x, pl.ds(y0, 8)] + b * s[g, to, pl.ds(y0, 8)]
                new = r[g, to, pl.ds(y0 + HALO, 8)] - a * step
                r[g, to, pl.ds(y0 + HALO, 8)] = new + new
                return 0

            lax.fori_loop(0, 2 * HALF * 4, near_side, 0)

            def far_side(i, _):
                plane = jnp.zeros((NY, 8, NZ), F32)
                r[g, i, inner] = plane
                r[g, EXT - 1 - i, inner] = plane
                return 0

            lax.fori_loop(0, HALF, far_side, 0)

    def update_projections(k, g):
        t = gathered_projections(k, g)
        if k > 1:
            t = t + scal[g, 3 + k] * tot[g, 1]
        tot[g, 1] = t
        tot[g, 0] = tot[g, 0] - scal[g, k - 1] * t

    def each(body):
        def run(g, _):
            body(g)
            return 0

        lax.fori_loop(0, 2, run, 0)

    def begin(i, acc):
        x = i // 4
        y0 = pl.multiple_of((i % 4) * 8, 8)
        row = pl.multiple_of(i * 8, 8)
        left = []
        for j in range(8):
            left.append(
                jnp.concatenate([both_parts(own_in[x, g, y0 + j], 0) for g in range(2)], axis=0)
            )
        right = []
        for j in range(8):
            right.append(table[row + j].astype(F32).T.astype(BF16))
            turned[pl.ds(pl.multiple_of((row + j) * NZ, NZ), NZ), :] = right[-1]
        return acc + jnp.dot(
            jnp.concatenate(left, axis=1),
            jnp.concatenate(right, axis=0),
            preferred_element_type=F32,
        )

    send_first(0)
    acc = lax.fori_loop(0, SX * NY // 8, begin, jnp.zeros((32, 2 * SLOTS), F32))
    send_projections(0, 0, acc[:16])
    send_projections(0, 1, acc[16:])
    send_first(1)

    def spread(i, _):
        rows = pot_in[pl.ds(pl.multiple_of(i * 8, 8), 8), :]
        for j in range(8):
            potb[i * 8 + j] = jnp.broadcast_to(rows[j : j + 1, :], (8, NZ))
        return 0

    lax.fori_loop(0, SX * NY // 8, spread, 0)

    def pass_on(k, g):
        forward_sums(k - 1 + g, 1 - g)

    def first(g):
        take_first(g)
        tot[g, 0] = gathered_projections(0, g)

        def between():
            @pl.when(g == 1)
            def _():
                pass_on(0, g)

        main(0, g, between)

    each(first)

    for k in (1, 2):

        def turn(g, k=k):
            update(k, g)
            update_projections(k, g)
            main(k, g, lambda: pass_on(k, g))

        each(turn)
        each(lambda g, k=k: halo_sent(k - 1, g))

    each(first_sent)

    def closing(g):
        update(3, g)
        update_projections(3, g)
        pass_on(3, g)
        last(g)

    each(closing)
    forward_sums(3, 1)
    each(lambda g: halo_sent(2, g))

    def finish(g):
        a3, b3 = take_sums(3, g)
        g3 = a3
        g2 = scal[g, 2] + b3 * g3
        g1 = scal[g, 1] + scal[g, 6] * g2
        g0 = scal[g, 0] + scal[g, 5] * g1

        def body(i, _):
            x = i // 4
            y0 = pl.multiple_of((i % 4) * 8, 8)
            value = (
                g0[None] * own_in[x, g, pl.ds(y0, 8)]
                + g1[None] * hist[0, g, x, pl.ds(y0, 8)]
                + g2[None] * hist[1, g, x, pl.ds(y0, 8)]
                + g3[None] * r[g, x + HALO, pl.ds(y0 + HALO, 8)]
            )
            x_out[x, g, pl.ds(y0, 8)] = value
            part = 4.0 * jnp.sum(value * orb[x, g, pl.ds(y0, 8)], axis=1)
            dens[x, pl.ds(y0, 8), :] = jnp.where(g == 0, part, dens[x, pl.ds(y0, 8), :] + part)
            return 0

        lax.fori_loop(0, SX * 4, body, 0)

    def clear_dens(i, _):
        dens[i] = jnp.zeros((NY, NZ), F32)
        return 0

    lax.fori_loop(0, SX, clear_dens, 0)
    each(finish)

    def rows_of(block):
        return pl.ds(pl.multiple_of(block * (NY // blocks_st), NY // blocks_st), NY // blocks_st)

    def block_copy(i, source):
        return pltpu.make_async_remote_copy(
            src_ref=dens.at[:, rows_of(other_block(i)), :],
            dst_ref=parts.at[source],
            send_sem=d_send.at[i],
            recv_sem=d_recv.at[i],
            device_id={"st": other_block(i)},
        )

    for i in range(1, blocks_st):
        block_copy(i, me).start()
    parts[me] = dens[:, rows_of(me), :]
    for i in range(1, blocks_st):
        block_copy(i, (me + blocks_st - i) % blocks_st).wait_recv()
    total = parts[0]
    for i in range(1, blocks_st):
        total = total + parts[i]
    dens_out[...] = total
    for i in range(1, blocks_st):
        block_copy(i, me).wait_send()


def solve(table, orb, pot, pert, lev, kb, tz, blocks_st):
    vmem = pl.BlockSpec(memory_space=pltpu.VMEM)
    dma = pltpu.SemaphoreType.DMA
    return pl.pallas_call(
        solve_kernel,
        out_shape=(
            jax.ShapeDtypeStruct((SX, 2, NY, 8, NZ), F32),
            jax.ShapeDtypeStruct((SX, NY // blocks_st, NZ), F32),
        ),
        in_specs=[vmem] * 4 + [pl.BlockSpec(memory_space=pltpu.SMEM)] * 2 + [vmem],
        out_specs=(vmem, vmem),
        scratch_shapes=[
            pltpu.VMEM((1, NZ), F32),
            pltpu.VMEM((SX, 2, NY, 8, NZ), F32),
            pltpu.VMEM((SX * NY * NZ, 2 * SLOTS), BF16),
            pltpu.VMEM((2, EXT, NYP, 8, NZ), F32),
            pltpu.VMEM((2, EXT, NY, 8, NZ), F32),
            pltpu.VMEM((2, 2, SX, NY, 8, NZ), F32),
            pltpu.VMEM((2, 2, 2 * HALO, NY, 8, NZ), F32),
            pltpu.VMEM((2, HALO, NY, 8, NZ), F32),
            pltpu.VMEM((2, 2, SX, NY, 8, NZ), F32),
            pltpu.VMEM((SX * NY, 8, NZ), F32),
            pltpu.VMEM((4, 2, PLANE, 8, NZ), F32),
            pltpu.VMEM((4, 2, DEPTH, 8, NZ), F32),
            pltpu.VMEM((4, 2, 4, 8, NZ), F32),
            pltpu.VMEM((4, 2, 2, 8, NZ), F32),
            pltpu.VMEM((4, 2, 8, NZ), F32),
            pltpu.VMEM((2, 12, 8, NZ), F32),
            pltpu.VMEM((2, 2, 8, NZ), F32),
            pltpu.VMEM((16, NZ), BF16),
            pltpu.VMEM((SX, NY, NZ), F32),
            pltpu.VMEM((blocks_st, SX, NY // blocks_st, NZ), F32),
            dma((4, 2, 2)),
            dma((4, 2, 2)),
            dma((2, PLANE)),
            dma((2, 2, PLANE)),
            dma((2, DEPTH)),
            dma((2, 2, DEPTH)),
            dma((2, 4)),
            dma((2, 2, 4)),
            dma((blocks_st,)),
            dma((blocks_st,)),
        ],
        compiler_params=pltpu.CompilerParams(
            collective_id=0, has_side_effects=True, vmem_limit_bytes=VMEM_MIB * 2**20
        ),
        name="bicg_solve",
    )(table, orb, pot, pert, lev, kb, tz)


def shards(orbitals, levels, potential, perturbation, projector, point_cell, point_atom, kb_energy):
    index = lax.axis_index("dom")
    row = (point_cell >> 7) * SLOTS + point_atom - (index - 1) * ATOM_DEV
    place = jnp.where(point_atom >= 0, row * NZ + (point_cell & 127), UNUSED)
    table, orb = build_table(projector, place, orbitals)
    tz = jnp.asarray(depth_matrix())
    turned, density = solve(
        table, orb, potential.reshape(SX * NY, NZ), perturbation.reshape(SX * NY, NZ),
        levels, kb_energy, tz,
        lax.axis_size("st"),
    )
    response = turned.transpose(1, 3, 0, 2, 4).reshape(orbitals.shape)
    return response, density


def solution(mesh):
    in_specs = (
        P("st", "dom", None, None),
        P("st"),
        P("dom", None, None),
        P("dom", None, None),
        P("dom"),
        P("dom"),
        P("dom"),
        P(),
    )
    out_specs = (P("st", "dom", None, None), P("dom", "st", None))
    return jax.shard_map(shards, mesh=mesh, in_specs=in_specs, out_specs=out_specs, check_vma=False)
```

```python
import numpy as np
import jax
import jax.numpy as jnp
from jax import lax
from jax.experimental import pallas as pl
from jax.experimental.pallas import tpu as pltpu
from jax.sharding import PartitionSpec as P

ATOM_DEV = 16
SLOTS = 3 * ATOM_DEV
SX, NY, NZ = 8, 32, 128
HALO = 6
HALF = HALO // 2
EXT = SX + 2 * HALO
NYP = NY + 2 * HALO
N_DOM = 64
PLANE = 8
DEPTH = 8
C = (
    -5369.0 / 1800.0,
    12.0 / 7.0,
    -15.0 / 56.0,
    10.0 / 189.0,
    -1.0 / 112.0,
    2.0 / 1925.0,
    -1.0 / 16632.0,
)
F32 = jnp.float32
BF16 = jnp.bfloat16
UNROLL = 16
VMEM_MIB = 43
ROWS = 32
BREAK = 2
UNUSED = SX * NY * SLOTS * NZ


def depth_matrix():
    lag = np.abs(np.arange(NZ)[:, None] - np.arange(NZ)[None, :])
    band = np.zeros((NZ, NZ), np.float32)
    for k in range(1, 7):
        band[lag == k] = -0.5 * C[k]
    high = band.astype(jnp.bfloat16)
    low = (band - high.astype(np.float32)).astype(jnp.bfloat16)
    half = np.concatenate([high, low], axis=1)
    return np.concatenate([half, half], axis=0)


def both_parts(value, axis):
    high = value.astype(BF16).astype(F32)
    return jnp.concatenate([high, value - high], axis=axis).astype(BF16)


def table_kernel(place, value, orb, table, turned, dense, sems):
    moves = [
        pltpu.make_async_copy(orb.at[n], turned.at[:, n // 8, :, n % 8, :], sems.at[n])
        for n in range(16)
    ]
    for c in moves:
        c.start()
    slots = place.shape[0]

    def clear(i, _):
        dense[pl.ds(pl.multiple_of(i * 64, 64), 64), :] = jnp.zeros((64, NZ), F32)
        return 0

    lax.fori_loop(0, SX * NY * SLOTS // 64, clear, 0)

    def halve(_, ends):
        low, high = ends
        mid = (low + high) // 2
        used = place[jnp.minimum(mid, slots - 1)] < UNUSED
        go = low < high
        return (
            jnp.where(go & used, mid + 1, low),
            jnp.where(go & jnp.logical_not(used), mid, high),
        )

    used, _ = lax.fori_loop(0, 15, halve, (jnp.int32(0), jnp.int32(slots)))
    lanes = lax.broadcasted_iota(jnp.int32, (1, NZ), 1)

    def put(i, _):
        for u in range(UNROLL):
            where = place[i * UNROLL + u]
            pltpu.store(
                dense.at[pl.ds(where >> 7, 1), :],
                jnp.full((1, NZ), value[i * UNROLL + u], F32),
                mask=lanes == (jnp.full((1, NZ), where, jnp.int32) & 127),
            )
        return 0

    lax.fori_loop(0, (used + UNROLL - 1) // UNROLL, put, 0)

    def split(i, _):
        for j in range(4):
            row = i * 4 + j
            part = dense[pl.ds(pl.multiple_of(row * SLOTS, SLOTS), SLOTS), :]
            table[row] = both_parts(part, 0)
        return 0

    lax.fori_loop(0, SX * NY // 4, split, 0)
    for c in moves:
        c.wait()


def build_table(projector, place, orbitals):
    smem = pl.BlockSpec(memory_space=pltpu.SMEM)
    return pl.pallas_call(
        table_kernel,
        out_shape=(
            jax.ShapeDtypeStruct((SX * NY, 2 * SLOTS, NZ), BF16),
            jax.ShapeDtypeStruct((SX, 2, NY, 8, NZ), F32),
        ),
        in_specs=[smem, smem, pl.BlockSpec(memory_space=pltpu.HBM)],
        out_specs=(pl.BlockSpec(memory_space=pltpu.VMEM), pl.BlockSpec(memory_space=pltpu.VMEM)),
        scratch_shapes=[
            pltpu.VMEM((SX * NY * SLOTS + 8, NZ), F32),
            pltpu.SemaphoreType.DMA((16,)),
        ],
        compiler_params=pltpu.CompilerParams(vmem_limit_bytes=10 * 2**20),
        cost_estimate=pl.CostEstimate(flops=0, bytes_accessed=40 * 2**20, transcendentals=0),
        name="projector_table",
    )(place, projector, orbitals)


def solve_kernel(
    table, orb, pot_in, pert_in, lev, kb, tz,
    x_out, dens_out,
    energy, own_in, turned, r, s, w, hb, hb2, hist, potb, st1, st2, pj, msg, pmsg, scal, tot, lhs, dens, parts,
    h_send, h_recv, a_send, a_recv, b_send, b_recv, p_send, p_recv, d_send, d_recv,
):
    d = lax.axis_index("dom")
    zi = d // PLANE
    ji = d % PLANE
    inner = pl.ds(HALO, NY)

    for k in range(4):
        for g in range(2):
            pj[k, g] = jnp.zeros((4, 8, NZ), F32)

    near = ((-2, d >= 2), (-1, d >= 1), (1, d < N_DOM - 1), (2, d < N_DOM - 2))

    first_at, second_at = zi, ji

    def in_first(i):
        return ((zi + i) % DEPTH) * PLANE + ji

    def in_second(i):
        return zi * PLANE + (ji + i) % PLANE

    me = lax.axis_index("st")
    blocks_st = lax.axis_size("st")

    def other_block(i):
        return (me + i) % blocks_st

    barrier = pltpu.get_barrier_semaphore()
    count = jnp.int32(PLANE - 1 + DEPTH - 1 + blocks_st - 1)
    for i in range(1, blocks_st):
        pl.semaphore_signal(barrier, inc=1, device_id={"st": other_block(i)})
    for i in range(1, PLANE):
        pl.semaphore_signal(barrier, inc=1, device_id={"dom": in_first(i)})
    for i in range(1, DEPTH):
        pl.semaphore_signal(barrier, inc=1, device_id={"dom": in_second(i)})
    for step, there in near:
        count = count + there.astype(jnp.int32)

        @pl.when(there)
        def _(step=step):
            pl.semaphore_signal(barrier, inc=1, device_id={"dom": d + step})

    zero = jnp.zeros((HALO, 8, NZ), F32)

    def clear(i, _):
        for g in range(2):
            r[g, i, pl.ds(0, HALO)] = zero
            r[g, i, pl.ds(HALO + NY, HALO)] = zero
        return 0

    lax.fori_loop(0, EXT, clear, 0)

    def start(i, _):
        x = i // 4
        y0 = pl.multiple_of((i % 4) * 8, 8)
        rows = pert_in[pl.ds(pl.multiple_of(i * 8, 8), 8), :]
        for j in range(8):
            row = jnp.broadcast_to(rows[j : j + 1, :], (8, NZ))
            for g in range(2):
                value = -row * orb[x, g, y0 + j]
                own_in[x, g, y0 + j] = value
                r[g, x + HALO, y0 + HALO + j] = value
        return 0

    lax.fori_loop(0, SX * NY // 8, start, 0)

    def clear_halo(base):
        plane = jnp.zeros((NY, 8, NZ), F32)
        far = jnp.where(base == 0, 0, SX + HALO)

        def one(i, _):
            for k in range(2):
                for g in range(2):
                    hb[k, g, base + i] = plane
            for g in range(2):
                hb2[g, i] = plane
                r[g, far + i, inner] = plane
            return 0

        lax.fori_loop(0, HALO, one, 0)

    @pl.when(d == 0)
    def _():
        clear_halo(0)

    @pl.when(d == N_DOM - 1)
    def _():
        clear_halo(HALO)

    lanes = lax.broadcasted_iota(jnp.int32, (8, NZ), 1)
    line = jnp.zeros((1, NZ), F32)
    for j in range(SLOTS):
        atom = jnp.clip((d - 1) * ATOM_DEV + j, 0, kb.shape[0] - 1)
        line = jnp.where(lanes[:1] == j, kb[atom], line)
    energy[...] = line

    pl.semaphore_wait(barrier, count)

    def project(blocks, row, acc):
        left = jnp.concatenate([both_parts(b, 0) for b in blocks], axis=1)
        right = turned[pl.ds(pl.multiple_of(row * NZ, 8 * NZ), 8 * NZ), :]
        return acc + jnp.dot(left, right, preferred_element_type=F32)

    def near_copy(k, g, n):
        step = near[n][0]
        return pltpu.make_async_remote_copy(
            src_ref=pmsg.at[k, g],
            dst_ref=pj.at[k, g, 3 - n],
            send_sem=p_send.at[g, n],
            recv_sem=p_recv.at[k % 2, g, 3 - n],
            device_id={"dom": d + step},
        )

    def near_arrival(k, g, n):
        return pltpu.make_async_remote_copy(
            src_ref=pmsg.at[k, g],
            dst_ref=pj.at[k, g, n],
            send_sem=p_send.at[g, n],
            recv_sem=p_recv.at[k % 2, g, n],
            device_id={"dom": d + near[n][0]},
        )

    def send_projections(k, g, acc):
        part = acc[:8, :SLOTS] + acc[8:, :SLOTS] + acc[:8, SLOTS:] + acc[8:, SLOTS:]
        pmsg[k, g] = jnp.concatenate([part, jnp.zeros((8, NZ - SLOTS), F32)], axis=1)
        for n in range(4):

            @pl.when(near[n][1])
            def _(n=n):
                near_copy(k, g, n).start()

    def gathered_projections(k, g):
        for n in range(4):

            @pl.when(near[n][1])
            def _(n=n):
                near_arrival(k, g, n).wait_recv()
                near_copy(k, g, n).wait_send()

        total = pmsg[k, g]
        shifts = ((2 * ATOM_DEV, 0, 16), (ATOM_DEV, 0, 32), (-ATOM_DEV, 16, 48), (-2 * ATOM_DEV, 32, 48))
        for n, (back, low, high) in enumerate(shifts):
            moved = pltpu.roll(pj[k, g, n], (-back) % NZ, 1)
            total = total + jnp.where((lanes >= low) & (lanes < high), moved, 0.0)
        return total

    def first_copy(k, g, i):
        return pltpu.make_async_remote_copy(
            src_ref=msg.at[k, g, 0],
            dst_ref=st1.at[k, g, first_at],
            send_sem=a_send.at[g, i],
            recv_sem=a_recv.at[k % 2, g, i],
            device_id={"dom": in_first(i)},
        )

    def first_arrival(k, g, i):
        return pltpu.make_async_remote_copy(
            src_ref=msg.at[k, g, 0],
            dst_ref=st1.at[k, g, (first_at + PLANE - i) % PLANE],
            send_sem=a_send.at[g, i],
            recv_sem=a_recv.at[k % 2, g, i],
            device_id={"dom": in_first(i)},
        )

    def second_copy(k, g, i):
        return pltpu.make_async_remote_copy(
            src_ref=msg.at[k, g, 1],
            dst_ref=st2.at[k, g, second_at],
            send_sem=b_send.at[g, i],
            recv_sem=b_recv.at[k % 2, g, i],
            device_id={"dom": in_second(i)},
        )

    def second_arrival(k, g, i):
        return pltpu.make_async_remote_copy(
            src_ref=msg.at[k, g, 1],
            dst_ref=st2.at[k, g, (second_at + DEPTH - i) % DEPTH],
            send_sem=b_send.at[g, i],
            recv_sem=b_recv.at[k % 2, g, i],
            device_id={"dom": in_second(i)},
        )

    def send_sums(k, g, rr, rw):
        tile = jnp.where(
            lanes < 64, jnp.sum(rr, axis=1, keepdims=True), jnp.sum(rw, axis=1, keepdims=True)
        )
        msg[k, g, 0] = tile
        st1[k, g, first_at] = tile
        for i in range(1, PLANE):
            first_copy(k, g, i).start()

    def forward_sums(k, g):
        for i in range(1, PLANE):
            first_arrival(k, g, i).wait_recv()
            first_copy(k, g, i).wait_send()
        tile = st1[k, g, 0]
        for i in range(1, PLANE):
            tile = tile + st1[k, g, i]
        msg[k, g, 1] = tile
        st2[k, g, second_at] = tile
        for i in range(1, DEPTH):
            second_copy(k, g, i).start()

    def take_sums(k, g):
        for i in range(1, DEPTH):
            second_arrival(k, g, i).wait_recv()
            second_copy(k, g, i).wait_send()
        tile = st2[k, g, 0]
        for i in range(1, DEPTH):
            tile = tile + st2[k, g, i]
        rr = jnp.broadcast_to(tile[:, 0:1], (8, NZ))
        rw = jnp.broadcast_to(tile[:, 64:65], (8, NZ))
        scal[g, 8 + k] = rr
        if k == 0:
            alpha, beta = rr / rw, jnp.zeros_like(rr)
        else:
            beta = rr / scal[g, 7 + k]
            alpha = rr / (rw - beta * rr / scal[g, k - 1])
        scal[g, k] = alpha
        scal[g, 4 + k] = beta
        return alpha, beta

    def up_copy(k, g):
        planes = HALO if k < 2 else HALF
        dst = hb.at[k, g, pl.ds(0, HALO)] if k < 2 else hb2.at[g, pl.ds(0, HALF)]
        return pltpu.make_async_remote_copy(
            src_ref=w.at[k % 2, g, pl.ds(SX - planes, planes)],
            dst_ref=dst,
            send_sem=h_send.at[k, g, 0],
            recv_sem=h_recv.at[k, g, 0],
            device_id={"dom": d + 1},
        )

    def down_copy(k, g):
        planes = HALO if k < 2 else HALF
        dst = hb.at[k, g, pl.ds(HALO, HALO)] if k < 2 else hb2.at[g, pl.ds(HALF, HALF)]
        return pltpu.make_async_remote_copy(
            src_ref=w.at[k % 2, g, pl.ds(0, planes)],
            dst_ref=dst,
            send_sem=h_send.at[k, g, 1],
            recv_sem=h_recv.at[k, g, 1],
            device_id={"dom": d - 1},
        )

    def goes_up(k, g):
        return d < N_DOM - 1

    def goes_down(k, g):
        return d > 0

    def comes_up(k, g):
        return d > 0

    def comes_down(k, g):
        return d < N_DOM - 1

    def send_halo(k, g):
        @pl.when(goes_up(k, g))
        def _():
            up_copy(k, g).start()

        @pl.when(goes_down(k, g))
        def _():
            down_copy(k, g).start()

    def take_halo(k, g):
        @pl.when(comes_up(k, g))
        def _():
            up_copy(k, g).wait_recv()

        @pl.when(comes_down(k, g))
        def _():
            down_copy(k, g).wait_recv()

    def halo_sent(k, g):
        @pl.when(goes_up(k, g))
        def _():
            up_copy(k, g).wait_send()

        @pl.when(goes_down(k, g))
        def _():
            down_copy(k, g).wait_send()

    def first_up(g):
        return pltpu.make_async_remote_copy(
            src_ref=own_in.at[pl.ds(SX - HALO, HALO), g],
            dst_ref=r.at[g, pl.ds(0, HALO), inner],
            send_sem=h_send.at[3, g, 0],
            recv_sem=h_recv.at[3, g, 0],
            device_id={"dom": d + 1},
        )

    def first_down(g):
        return pltpu.make_async_remote_copy(
            src_ref=own_in.at[pl.ds(0, HALO), g],
            dst_ref=r.at[g, pl.ds(SX + HALO, HALO), inner],
            send_sem=h_send.at[3, g, 1],
            recv_sem=h_recv.at[3, g, 1],
            device_id={"dom": d - 1},
        )

    def send_first(g):
        @pl.when(d < N_DOM - 1)
        def _():
            first_up(g).start()

        @pl.when(d > 0)
        def _():
            first_down(g).start()

    def take_first(g):
        @pl.when(d > 0)
        def _():
            first_up(g).wait_recv()

        @pl.when(d < N_DOM - 1)
        def _():
            first_down(g).wait_recv()

    def first_sent(g):
        @pl.when(d < N_DOM - 1)
        def _():
            first_up(g).wait_send()

        @pl.when(d > 0)
        def _():
            first_down(g).wait_send()

    def stencil(g, x, y0, level, rows):
        f = r[g, x + HALO, pl.ds(y0 + HALO, rows)]
        deep = jnp.dot(
            both_parts(f.reshape(rows * 8, NZ), 1), tz[...], preferred_element_type=F32
        )
        deep = (deep[:, :NZ] + deep[:, NZ:]).reshape(rows, 8, NZ)
        fs, images = [], []
        for part in range(0, rows, 8):
            line = r[g, x + HALO, pl.ds(y0 + part, 20)]
            f = line[HALO : HALO + 8]
            acc = deep[part : part + 8] + (potb[pl.ds(x * NY + y0 + part, 8)] + level[None]) * f
            for k in range(1, 7):
                pair = (
                    line[HALO + k : HALO + k + 8]
                    + line[HALO - k : HALO - k + 8]
                    + r[g, x + HALO + k, pl.ds(y0 + part + HALO, 8)]
                    + r[g, x + HALO - k, pl.ds(y0 + part + HALO, 8)]
                )
                acc = acc + (-0.5 * C[k]) * pair
            fs.append(f)
            images.append(acc)
        return fs, images

    def tree(parts):
        parts = [parts[j] for j in range(8)]
        while len(parts) > 1:
            parts = [a + b for a, b in zip(parts[::2], parts[1::2])]
        return parts[0]

    def place(i):
        per = NY // ROWS
        return i // per, pl.multiple_of((i % per) * ROWS, ROWS)

    none = jnp.zeros((8, NZ), F32)

    def level_of(g):
        rows = lax.broadcasted_iota(jnp.int32, (8, NZ), 0)
        value = none
        for j in range(8):
            value = jnp.where(rows == j, -1.5 * C[0] - lev[g * 8 + j], value)
        return value

    def main(k, g, between):
        level = level_of(g)
        coeff = tot[g, 0] * energy[...]
        coeff = jnp.where(lanes < SLOTS, coeff, pltpu.roll(coeff, SLOTS, 1))
        lhs[...] = both_parts(coeff, 0)

        def body(i, carry):
            rr, rw = carry
            pl.when(i == BREAK)(between)
            x, y0 = place(i)
            fs, images = stencil(g, x, y0, level, ROWS)
            left = lhs[:, : 2 * SLOTS]
            for n, (f, image) in enumerate(zip(fs, images)):
                row = x * NY + y0 + n * 8
                right = jnp.concatenate([table[row + j] for j in range(8)], axis=1)
                v = jnp.dot(left, right, preferred_element_type=F32)
                v = v[:8] + v[8:]
                blocks = [image[j] + v[:, j * NZ : (j + 1) * NZ] for j in range(8)]
                for j in range(8):
                    w[k % 2, g, x, y0 + n * 8 + j] = blocks[j]
                rr = rr + tree(f * f)
                rw = rw + tree([f[j] * blocks[j] for j in range(8)])
            return rr, rw

        rr, rw = lax.fori_loop(0, SX * NY // ROWS, body, (none, none))
        send_sums(k, g, rr, rw)
        send_halo(k, g)

        def images(i, acc):
            x = i // 2
            y0 = pl.multiple_of((i % 2) * 16, 16)
            for n in range(2):
                blocks = [w[k % 2, g, x, y0 + n * 8 + j] for j in range(8)]
                acc = project(blocks, x * NY + y0 + n * 8, acc)
            return acc

        acc = lax.fori_loop(0, SX * NY // 16, images, jnp.zeros((16, 2 * SLOTS), F32))
        send_projections(k + 1, g, acc)

    def last(g):
        level = level_of(g)

        def body(i, carry):
            rr, rw = carry
            x, y0 = place(i)

            @pl.when(x == SX - HALF)
            def _():
                for j in range(HALF):
                    r[g, SX + HALO + j, inner] = jnp.zeros((NY, 8, NZ), F32)

            for f, image in zip(*stencil(g, x, y0, level, ROWS)):
                rr, rw = rr + tree(f * f), rw + tree(f * image)
            return rr, rw

        rr, rw = lax.fori_loop(0, SX * NY // ROWS, body, (none, none))
        own = (lanes >= ATOM_DEV) & (lanes < 2 * ATOM_DEV)
        t = tot[g, 0]
        rw = rw + jnp.where(own, t * t * energy[...], 0.0)
        send_sums(3, g, rr, rw)

    def update(k, g):
        alpha, beta = take_sums(k - 1, g)
        a, b = alpha[None], beta[None]

        def own(i, _):
            x = i // 4
            y0 = pl.multiple_of((i % 4) * 8, 8)
            step = w[(k - 1) % 2, g, x, pl.ds(y0, 8)]
            if k > 1:
                step = step + b * s[g, x + HALO, pl.ds(y0, 8)]
            if k < 3:
                s[g, x + HALO, pl.ds(y0, 8)] = step
            new = r[g, x + HALO, pl.ds(y0 + HALO, 8)] - a * step
            r[g, x + HALO, pl.ds(y0 + HALO, 8)] = new
            if k < 3:
                hist[k - 1, g, x, pl.ds(y0, 8)] = new
            return 0

        lax.fori_loop(0, SX * 4, own, 0)
        take_halo(k - 1, g)

        if k < 3:

            def side(i, _):
                x = i // 4
                y0 = pl.multiple_of((i % 4) * 8, 8)
                to = jnp.where(x < HALO, x, x + SX)
                step = hb[k - 1, g, x, pl.ds(y0, 8)]
                if k > 1:
                    step = step + b * s[g, to, pl.ds(y0, 8)]
                s[g, to, pl.ds(y0, 8)] = step
                r[g, to, pl.ds(y0 + HALO, 8)] = r[g, to, pl.ds(y0 + HALO, 8)] - a * step
                return 0

            lax.fori_loop(0, 2 * HALO * 4, side, 0)
        else:
            def near_side(i, _):
                x = i // 4
                y0 = pl.multiple_of((i % 4) * 8, 8)
                to = jnp.where(x < HALF, x + HALF, x + SX + HALO - HALF)
                step = hb2[g, x, pl.ds(y0, 8)] + b * s[g, to, pl.ds(y0, 8)]
                new = r[g, to, pl.ds(y0 + HALO, 8)] - a * step
                r[g, to, pl.ds(y0 + HALO, 8)] = new + new
                return 0

            lax.fori_loop(0, 2 * HALF * 4, near_side, 0)

            def far_side(i, _):
                plane = jnp.zeros((NY, 8, NZ), F32)
                r[g, i, inner] = plane
                r[g, EXT - 1 - i, inner] = plane
                return 0

            lax.fori_loop(0, HALF, far_side, 0)

    def update_projections(k, g):
        t = gathered_projections(k, g)
        if k > 1:
            t = t + scal[g, 3 + k] * tot[g, 1]
        tot[g, 1] = t
        tot[g, 0] = tot[g, 0] - scal[g, k - 1] * t

    def each(body):
        def run(g, _):
            body(g)
            return 0

        lax.fori_loop(0, 2, run, 0)

    def begin(i, acc):
        x = i // 4
        y0 = pl.multiple_of((i % 4) * 8, 8)
        row = pl.multiple_of(i * 8, 8)
        left = []
        for j in range(8):
            left.append(
                jnp.concatenate([both_parts(own_in[x, g, y0 + j], 0) for g in range(2)], axis=0)
            )
        right = []
        for j in range(8):
            right.append(table[row + j].astype(F32).T.astype(BF16))
            turned[pl.ds(pl.multiple_of((row + j) * NZ, NZ), NZ), :] = right[-1]
        return acc + jnp.dot(
            jnp.concatenate(left, axis=1),
            jnp.concatenate(right, axis=0),
            preferred_element_type=F32,
        )

    send_first(0)
    acc = lax.fori_loop(0, SX * NY // 8, begin, jnp.zeros((32, 2 * SLOTS), F32))
    send_projections(0, 0, acc[:16])
    send_projections(0, 1, acc[16:])
    send_first(1)

    def spread(i, _):
        rows = pot_in[pl.ds(pl.multiple_of(i * 8, 8), 8), :]
        for j in range(8):
            potb[i * 8 + j] = jnp.broadcast_to(rows[j : j + 1, :], (8, NZ))
        return 0

    lax.fori_loop(0, SX * NY // 8, spread, 0)

    def pass_on(k, g):
        forward_sums(k - 1 + g, 1 - g)

    def first(g):
        take_first(g)
        tot[g, 0] = gathered_projections(0, g)

        def between():
            @pl.when(g == 1)
            def _():
                pass_on(0, g)

        main(0, g, between)

    each(first)

    for k in (1, 2):

        def turn(g, k=k):
            update(k, g)
            update_projections(k, g)
            main(k, g, lambda: pass_on(k, g))

        each(turn)
        each(lambda g, k=k: halo_sent(k - 1, g))

    each(first_sent)

    def closing(g):
        update(3, g)
        update_projections(3, g)
        pass_on(3, g)
        last(g)

    each(closing)
    forward_sums(3, 1)
    each(lambda g: halo_sent(2, g))

    def finish(g):
        a3, b3 = take_sums(3, g)
        g3 = a3
        g2 = scal[g, 2] + b3 * g3
        g1 = scal[g, 1] + scal[g, 6] * g2
        g0 = scal[g, 0] + scal[g, 5] * g1

        def body(i, _):
            x = i // 4
            y0 = pl.multiple_of((i % 4) * 8, 8)
            value = (
                g0[None] * own_in[x, g, pl.ds(y0, 8)]
                + g1[None] * hist[0, g, x, pl.ds(y0, 8)]
                + g2[None] * hist[1, g, x, pl.ds(y0, 8)]
                + g3[None] * r[g, x + HALO, pl.ds(y0 + HALO, 8)]
            )
            x_out[x, g, pl.ds(y0, 8)] = value
            part = 4.0 * jnp.sum(value * orb[x, g, pl.ds(y0, 8)], axis=1)
            dens[x, pl.ds(y0, 8), :] = jnp.where(g == 0, part, dens[x, pl.ds(y0, 8), :] + part)
            return 0

        lax.fori_loop(0, SX * 4, body, 0)

    def clear_dens(i, _):
        dens[i] = jnp.zeros((NY, NZ), F32)
        return 0

    lax.fori_loop(0, SX, clear_dens, 0)
    each(finish)

    def rows_of(block):
        return pl.ds(pl.multiple_of(block * (NY // blocks_st), NY // blocks_st), NY // blocks_st)

    def block_copy(i, source):
        return pltpu.make_async_remote_copy(
            src_ref=dens.at[:, rows_of(other_block(i)), :],
            dst_ref=parts.at[source],
            send_sem=d_send.at[i],
            recv_sem=d_recv.at[i],
            device_id={"st": other_block(i)},
        )

    for i in range(1, blocks_st):
        block_copy(i, me).start()
    parts[me] = dens[:, rows_of(me), :]
    for i in range(1, blocks_st):
        block_copy(i, (me + blocks_st - i) % blocks_st).wait_recv()
    total = parts[0]
    for i in range(1, blocks_st):
        total = total + parts[i]
    dens_out[...] = total
    for i in range(1, blocks_st):
        block_copy(i, me).wait_send()


def solve(table, orb, pot, pert, lev, kb, tz, blocks_st):
    vmem = pl.BlockSpec(memory_space=pltpu.VMEM)
    dma = pltpu.SemaphoreType.DMA
    return pl.pallas_call(
        solve_kernel,
        out_shape=(
            jax.ShapeDtypeStruct((SX, 2, NY, 8, NZ), F32),
            jax.ShapeDtypeStruct((SX, NY // blocks_st, NZ), F32),
        ),
        in_specs=[vmem] * 4 + [pl.BlockSpec(memory_space=pltpu.SMEM)] * 2 + [vmem],
        out_specs=(vmem, vmem),
        scratch_shapes=[
            pltpu.VMEM((1, NZ), F32),
            pltpu.VMEM((SX, 2, NY, 8, NZ), F32),
            pltpu.VMEM((SX * NY * NZ, 2 * SLOTS), BF16),
            pltpu.VMEM((2, EXT, NYP, 8, NZ), F32),
            pltpu.VMEM((2, EXT, NY, 8, NZ), F32),
            pltpu.VMEM((2, 2, SX, NY, 8, NZ), F32),
            pltpu.VMEM((2, 2, 2 * HALO, NY, 8, NZ), F32),
            pltpu.VMEM((2, HALO, NY, 8, NZ), F32),
            pltpu.VMEM((2, 2, SX, NY, 8, NZ), F32),
            pltpu.VMEM((SX * NY, 8, NZ), F32),
            pltpu.VMEM((4, 2, PLANE, 8, NZ), F32),
            pltpu.VMEM((4, 2, DEPTH, 8, NZ), F32),
            pltpu.VMEM((4, 2, 4, 8, NZ), F32),
            pltpu.VMEM((4, 2, 2, 8, NZ), F32),
            pltpu.VMEM((4, 2, 8, NZ), F32),
            pltpu.VMEM((2, 12, 8, NZ), F32),
            pltpu.VMEM((2, 2, 8, NZ), F32),
            pltpu.VMEM((16, NZ), BF16),
            pltpu.VMEM((SX, NY, NZ), F32),
            pltpu.VMEM((blocks_st, SX, NY // blocks_st, NZ), F32),
            dma((4, 2, 2)),
            dma((4, 2, 2)),
            dma((2, PLANE)),
            dma((2, 2, PLANE)),
            dma((2, DEPTH)),
            dma((2, 2, DEPTH)),
            dma((2, 4)),
            dma((2, 2, 4)),
            dma((blocks_st,)),
            dma((blocks_st,)),
        ],
        compiler_params=pltpu.CompilerParams(
            collective_id=0, has_side_effects=True, vmem_limit_bytes=VMEM_MIB * 2**20
        ),
        name="bicg_solve",
    )(table, orb, pot, pert, lev, kb, tz)


def shards(orbitals, levels, potential, perturbation, projector, point_cell, point_atom, kb_energy):
    index = lax.axis_index("dom")
    row = (point_cell >> 7) * SLOTS + point_atom - (index - 1) * ATOM_DEV
    place = jnp.where(point_atom >= 0, row * NZ + (point_cell & 127), UNUSED)
    table, orb = build_table(projector, place, orbitals)
    tz = jnp.asarray(depth_matrix())
    turned, density = solve(
        table, orb, potential.reshape(SX * NY, NZ), perturbation.reshape(SX * NY, NZ),
        levels, kb_energy, tz,
        lax.axis_size("st"),
    )
    response = turned.transpose(1, 3, 0, 2, 4).reshape(orbitals.shape)
    return response, density


def solution(mesh):
    in_specs = (
        P("st", "dom", None, None),
        P("st"),
        P("dom", None, None),
        P("dom", None, None),
        P("dom"),
        P("dom"),
        P("dom"),
        P(),
    )
    out_specs = (P("st", "dom", None, None), P("dom", "st", None))
    return jax.shard_map(shards, mesh=mesh, in_specs=in_specs, out_specs=out_specs, check_vma=False)
```

```python
import numpy as np
import jax
import jax.numpy as jnp
from jax import lax
from jax.experimental import pallas as pl
from jax.experimental.pallas import tpu as pltpu
from jax.sharding import PartitionSpec as P

ATOM_DEV = 16
SLOTS = 3 * ATOM_DEV
SX, NY, NZ = 8, 32, 128
HALO = 6
HALF = HALO // 2
EXT = SX + 2 * HALO
NYP = NY + 2 * HALO
N_DOM = 64
PLANE = 8
DEPTH = 8
C = (
    -5369.0 / 1800.0,
    12.0 / 7.0,
    -15.0 / 56.0,
    10.0 / 189.0,
    -1.0 / 112.0,
    2.0 / 1925.0,
    -1.0 / 16632.0,
)
F32 = jnp.float32
BF16 = jnp.bfloat16
UNROLL = 32
VMEM_MIB = 43
ROWS = 32
BREAK = 2
UNUSED = SX * NY * SLOTS * NZ


def depth_matrix():
    lag = np.abs(np.arange(NZ)[:, None] - np.arange(NZ)[None, :])
    band = np.zeros((NZ, NZ), np.float32)
    for k in range(1, 7):
        band[lag == k] = -0.5 * C[k]
    high = band.astype(jnp.bfloat16)
    low = (band - high.astype(np.float32)).astype(jnp.bfloat16)
    half = np.concatenate([high, low], axis=1)
    return np.concatenate([half, half], axis=0)


def both_parts(value, axis):
    high = value.astype(BF16).astype(F32)
    return jnp.concatenate([high, value - high], axis=axis).astype(BF16)


def table_kernel(place, value, orb, table, turned, dense, sems):
    moves = [
        pltpu.make_async_copy(orb.at[n], turned.at[:, n // 8, :, n % 8, :], sems.at[n])
        for n in range(16)
    ]
    for c in moves:
        c.start()
    slots = place.shape[0]

    def clear(i, _):
        dense[pl.ds(pl.multiple_of(i * 64, 64), 64), :] = jnp.zeros((64, NZ), F32)
        return 0

    lax.fori_loop(0, SX * NY * SLOTS // 64, clear, 0)

    def halve(_, ends):
        low, high = ends
        mid = (low + high) // 2
        used = place[jnp.minimum(mid, slots - 1)] < UNUSED
        go = low < high
        return (
            jnp.where(go & used, mid + 1, low),
            jnp.where(go & jnp.logical_not(used), mid, high),
        )

    used, _ = lax.fori_loop(0, 15, halve, (jnp.int32(0), jnp.int32(slots)))
    lanes = lax.broadcasted_iota(jnp.int32, (1, NZ), 1)

    def put(i, _):
        for u in range(UNROLL):
            where = place[i * UNROLL + u]
            pltpu.store(
                dense.at[pl.ds(where >> 7, 1), :],
                jnp.full((1, NZ), value[i * UNROLL + u], F32),
                mask=lanes == (jnp.full((1, NZ), where, jnp.int32) & 127),
            )
        return 0

    lax.fori_loop(0, (used + UNROLL - 1) // UNROLL, put, 0)

    def split(i, _):
        for j in range(4):
            row = i * 4 + j
            part = dense[pl.ds(pl.multiple_of(row * SLOTS, SLOTS), SLOTS), :]
            table[row] = both_parts(part, 0)
        return 0

    lax.fori_loop(0, SX * NY // 4, split, 0)
    for c in moves:
        c.wait()


def build_table(projector, place, orbitals):
    smem = pl.BlockSpec(memory_space=pltpu.SMEM)
    return pl.pallas_call(
        table_kernel,
        out_shape=(
            jax.ShapeDtypeStruct((SX * NY, 2 * SLOTS, NZ), BF16),
            jax.ShapeDtypeStruct((SX, 2, NY, 8, NZ), F32),
        ),
        in_specs=[smem, smem, pl.BlockSpec(memory_space=pltpu.HBM)],
        out_specs=(pl.BlockSpec(memory_space=pltpu.VMEM), pl.BlockSpec(memory_space=pltpu.VMEM)),
        scratch_shapes=[
            pltpu.VMEM((SX * NY * SLOTS + 8, NZ), F32),
            pltpu.SemaphoreType.DMA((16,)),
        ],
        compiler_params=pltpu.CompilerParams(vmem_limit_bytes=10 * 2**20),
        cost_estimate=pl.CostEstimate(flops=0, bytes_accessed=40 * 2**20, transcendentals=0),
        name="projector_table",
    )(place, projector, orbitals)


def solve_kernel(
    table, orb, pot_in, pert_in, lev, kb, tz,
    x_out, dens_out,
    energy, own_in, turned, r, s, w, hb, hb2, hist, potb, st1, st2, pj, msg, pmsg, scal, tot, lhs, dens, parts,
    h_send, h_recv, a_send, a_recv, b_send, b_recv, p_send, p_recv, d_send, d_recv,
):
    d = lax.axis_index("dom")
    zi = d // PLANE
    ji = d % PLANE
    inner = pl.ds(HALO, NY)

    for k in range(4):
        for g in range(2):
            pj[k, g] = jnp.zeros((4, 8, NZ), F32)

    near = ((-2, d >= 2), (-1, d >= 1), (1, d < N_DOM - 1), (2, d < N_DOM - 2))

    first_at, second_at = zi, ji

    def in_first(i):
        return ((zi + i) % DEPTH) * PLANE + ji

    def in_second(i):
        return zi * PLANE + (ji + i) % PLANE

    me = lax.axis_index("st")
    blocks_st = lax.axis_size("st")

    def other_block(i):
        return (me + i) % blocks_st

    barrier = pltpu.get_barrier_semaphore()
    count = jnp.int32(PLANE - 1 + DEPTH - 1 + blocks_st - 1)
    for i in range(1, blocks_st):
        pl.semaphore_signal(barrier, inc=1, device_id={"st": other_block(i)})
    for i in range(1, PLANE):
        pl.semaphore_signal(barrier, inc=1, device_id={"dom": in_first(i)})
    for i in range(1, DEPTH):
        pl.semaphore_signal(barrier, inc=1, device_id={"dom": in_second(i)})
    for step, there in near:
        count = count + there.astype(jnp.int32)

        @pl.when(there)
        def _(step=step):
            pl.semaphore_signal(barrier, inc=1, device_id={"dom": d + step})

    zero = jnp.zeros((HALO, 8, NZ), F32)

    def clear(i, _):
        for g in range(2):
            r[g, i, pl.ds(0, HALO)] = zero
            r[g, i, pl.ds(HALO + NY, HALO)] = zero
        return 0

    lax.fori_loop(0, EXT, clear, 0)

    def start(i, _):
        x = i // 4
        y0 = pl.multiple_of((i % 4) * 8, 8)
        rows = pert_in[pl.ds(pl.multiple_of(i * 8, 8), 8), :]
        for j in range(8):
            row = jnp.broadcast_to(rows[j : j + 1, :], (8, NZ))
            for g in range(2):
                value = -row * orb[x, g, y0 + j]
                own_in[x, g, y0 + j] = value
                r[g, x + HALO, y0 + HALO + j] = value
        return 0

    lax.fori_loop(0, SX * NY // 8, start, 0)

    def clear_halo(base):
        plane = jnp.zeros((NY, 8, NZ), F32)
        far = jnp.where(base == 0, 0, SX + HALO)

        def one(i, _):
            for k in range(2):
                for g in range(2):
                    hb[k, g, base + i] = plane
            for g in range(2):
                hb2[g, i] = plane
                r[g, far + i, inner] = plane
            return 0

        lax.fori_loop(0, HALO, one, 0)

    @pl.when(d == 0)
    def _():
        clear_halo(0)

    @pl.when(d == N_DOM - 1)
    def _():
        clear_halo(HALO)

    lanes = lax.broadcasted_iota(jnp.int32, (8, NZ), 1)
    line = jnp.zeros((1, NZ), F32)
    for j in range(SLOTS):
        atom = jnp.clip((d - 1) * ATOM_DEV + j, 0, kb.shape[0] - 1)
        line = jnp.where(lanes[:1] == j, kb[atom], line)
    energy[...] = line

    pl.semaphore_wait(barrier, count)

    def project(blocks, row, acc):
        left = jnp.concatenate([both_parts(b, 0) for b in blocks], axis=1)
        right = turned[pl.ds(pl.multiple_of(row * NZ, 8 * NZ), 8 * NZ), :]
        return acc + jnp.dot(left, right, preferred_element_type=F32)

    def near_copy(k, g, n):
        step = near[n][0]
        return pltpu.make_async_remote_copy(
            src_ref=pmsg.at[k, g],
            dst_ref=pj.at[k, g, 3 - n],
            send_sem=p_send.at[g, n],
            recv_sem=p_recv.at[k % 2, g, 3 - n],
            device_id={"dom": d + step},
        )

    def near_arrival(k, g, n):
        return pltpu.make_async_remote_copy(
            src_ref=pmsg.at[k, g],
            dst_ref=pj.at[k, g, n],
            send_sem=p_send.at[g, n],
            recv_sem=p_recv.at[k % 2, g, n],
            device_id={"dom": d + near[n][0]},
        )

    def send_projections(k, g, acc):
        part = acc[:8, :SLOTS] + acc[8:, :SLOTS] + acc[:8, SLOTS:] + acc[8:, SLOTS:]
        pmsg[k, g] = jnp.concatenate([part, jnp.zeros((8, NZ - SLOTS), F32)], axis=1)
        for n in range(4):

            @pl.when(near[n][1])
            def _(n=n):
                near_copy(k, g, n).start()

    def gathered_projections(k, g):
        for n in range(4):

            @pl.when(near[n][1])
            def _(n=n):
                near_arrival(k, g, n).wait_recv()
                near_copy(k, g, n).wait_send()

        total = pmsg[k, g]
        shifts = ((2 * ATOM_DEV, 0, 16), (ATOM_DEV, 0, 32), (-ATOM_DEV, 16, 48), (-2 * ATOM_DEV, 32, 48))
        for n, (back, low, high) in enumerate(shifts):
            moved = pltpu.roll(pj[k, g, n], (-back) % NZ, 1)
            total = total + jnp.where((lanes >= low) & (lanes < high), moved, 0.0)
        return total

    def first_copy(k, g, i):
        return pltpu.make_async_remote_copy(
            src_ref=msg.at[k, g, 0],
            dst_ref=st1.at[k, g, first_at],
            send_sem=a_send.at[g, i],
            recv_sem=a_recv.at[k % 2, g, i],
            device_id={"dom": in_first(i)},
        )

    def first_arrival(k, g, i):
        return pltpu.make_async_remote_copy(
            src_ref=msg.at[k, g, 0],
            dst_ref=st1.at[k, g, (first_at + PLANE - i) % PLANE],
            send_sem=a_send.at[g, i],
            recv_sem=a_recv.at[k % 2, g, i],
            device_id={"dom": in_first(i)},
        )

    def second_copy(k, g, i):
        return pltpu.make_async_remote_copy(
            src_ref=msg.at[k, g, 1],
            dst_ref=st2.at[k, g, second_at],
            send_sem=b_send.at[g, i],
            recv_sem=b_recv.at[k % 2, g, i],
            device_id={"dom": in_second(i)},
        )

    def second_arrival(k, g, i):
        return pltpu.make_async_remote_copy(
            src_ref=msg.at[k, g, 1],
            dst_ref=st2.at[k, g, (second_at + DEPTH - i) % DEPTH],
            send_sem=b_send.at[g, i],
            recv_sem=b_recv.at[k % 2, g, i],
            device_id={"dom": in_second(i)},
        )

    def send_sums(k, g, rr, rw):
        tile = jnp.where(
            lanes < 64, jnp.sum(rr, axis=1, keepdims=True), jnp.sum(rw, axis=1, keepdims=True)
        )
        msg[k, g, 0] = tile
        st1[k, g, first_at] = tile
        for i in range(1, PLANE):
            first_copy(k, g, i).start()

    def forward_sums(k, g):
        for i in range(1, PLANE):
            first_arrival(k, g, i).wait_recv()
            first_copy(k, g, i).wait_send()
        tile = st1[k, g, 0]
        for i in range(1, PLANE):
            tile = tile + st1[k, g, i]
        msg[k, g, 1] = tile
        st2[k, g, second_at] = tile
        for i in range(1, DEPTH):
            second_copy(k, g, i).start()

    def take_sums(k, g):
        for i in range(1, DEPTH):
            second_arrival(k, g, i).wait_recv()
            second_copy(k, g, i).wait_send()
        tile = st2[k, g, 0]
        for i in range(1, DEPTH):
            tile = tile + st2[k, g, i]
        rr = jnp.broadcast_to(tile[:, 0:1], (8, NZ))
        rw = jnp.broadcast_to(tile[:, 64:65], (8, NZ))
        scal[g, 8 + k] = rr
        if k == 0:
            alpha, beta = rr / rw, jnp.zeros_like(rr)
        else:
            beta = rr / scal[g, 7 + k]
            alpha = rr / (rw - beta * rr / scal[g, k - 1])
        scal[g, k] = alpha
        scal[g, 4 + k] = beta
        return alpha, beta

    def up_copy(k, g):
        planes = HALO if k < 2 else HALF
        dst = hb.at[k, g, pl.ds(0, HALO)] if k < 2 else hb2.at[g, pl.ds(0, HALF)]
        return pltpu.make_async_remote_copy(
            src_ref=w.at[k % 2, g, pl.ds(SX - planes, planes)],
            dst_ref=dst,
            send_sem=h_send.at[k, g, 0],
            recv_sem=h_recv.at[k, g, 0],
            device_id={"dom": d + 1},
        )

    def down_copy(k, g):
        planes = HALO if k < 2 else HALF
        dst = hb.at[k, g, pl.ds(HALO, HALO)] if k < 2 else hb2.at[g, pl.ds(HALF, HALF)]
        return pltpu.make_async_remote_copy(
            src_ref=w.at[k % 2, g, pl.ds(0, planes)],
            dst_ref=dst,
            send_sem=h_send.at[k, g, 1],
            recv_sem=h_recv.at[k, g, 1],
            device_id={"dom": d - 1},
        )

    def goes_up(k, g):
        return d < N_DOM - 1

    def goes_down(k, g):
        return d > 0

    def comes_up(k, g):
        return d > 0

    def comes_down(k, g):
        return d < N_DOM - 1

    def send_halo(k, g):
        @pl.when(goes_up(k, g))
        def _():
            up_copy(k, g).start()

        @pl.when(goes_down(k, g))
        def _():
            down_copy(k, g).start()

    def take_halo(k, g):
        @pl.when(comes_up(k, g))
        def _():
            up_copy(k, g).wait_recv()

        @pl.when(comes_down(k, g))
        def _():
            down_copy(k, g).wait_recv()

    def halo_sent(k, g):
        @pl.when(goes_up(k, g))
        def _():
            up_copy(k, g).wait_send()

        @pl.when(goes_down(k, g))
        def _():
            down_copy(k, g).wait_send()

    def first_up(g):
        return pltpu.make_async_remote_copy(
            src_ref=own_in.at[pl.ds(SX - HALO, HALO), g],
            dst_ref=r.at[g, pl.ds(0, HALO), inner],
            send_sem=h_send.at[3, g, 0],
            recv_sem=h_recv.at[3, g, 0],
            device_id={"dom": d + 1},
        )

    def first_down(g):
        return pltpu.make_async_remote_copy(
            src_ref=own_in.at[pl.ds(0, HALO), g],
            dst_ref=r.at[g, pl.ds(SX + HALO, HALO), inner],
            send_sem=h_send.at[3, g, 1],
            recv_sem=h_recv.at[3, g, 1],
            device_id={"dom": d - 1},
        )

    def send_first(g):
        @pl.when(d < N_DOM - 1)
        def _():
            first_up(g).start()

        @pl.when(d > 0)
        def _():
            first_down(g).start()

    def take_first(g):
        @pl.when(d > 0)
        def _():
            first_up(g).wait_recv()

        @pl.when(d < N_DOM - 1)
        def _():
            first_down(g).wait_recv()

    def first_sent(g):
        @pl.when(d < N_DOM - 1)
        def _():
            first_up(g).wait_send()

        @pl.when(d > 0)
        def _():
            first_down(g).wait_send()

    def stencil(g, x, y0, level, rows):
        f = r[g, x + HALO, pl.ds(y0 + HALO, rows)]
        deep = jnp.dot(
            both_parts(f.reshape(rows * 8, NZ), 1), tz[...], preferred_element_type=F32
        )
        deep = (deep[:, :NZ] + deep[:, NZ:]).reshape(rows, 8, NZ)
        fs, images = [], []
        for part in range(0, rows, 8):
            line = r[g, x + HALO, pl.ds(y0 + part, 20)]
            f = line[HALO : HALO + 8]
            acc = deep[part : part + 8] + (potb[pl.ds(x * NY + y0 + part, 8)] + level[None]) * f
            for k in range(1, 7):
                pair = (
                    line[HALO + k : HALO + k + 8]
                    + line[HALO - k : HALO - k + 8]
                    + r[g, x + HALO + k, pl.ds(y0 + part + HALO, 8)]
                    + r[g, x + HALO - k, pl.ds(y0 + part + HALO, 8)]
                )
                acc = acc + (-0.5 * C[k]) * pair
            fs.append(f)
            images.append(acc)
        return fs, images

    def tree(parts):
        parts = [parts[j] for j in range(8)]
        while len(parts) > 1:
            parts = [a + b for a, b in zip(parts[::2], parts[1::2])]
        return parts[0]

    def place(i):
        per = NY // ROWS
        return i // per, pl.multiple_of((i % per) * ROWS, ROWS)

    none = jnp.zeros((8, NZ), F32)

    def level_of(g):
        rows = lax.broadcasted_iota(jnp.int32, (8, NZ), 0)
        value = none
        for j in range(8):
            value = jnp.where(rows == j, -1.5 * C[0] - lev[g * 8 + j], value)
        return value

    def main(k, g, between):
        level = level_of(g)
        coeff = tot[g, 0] * energy[...]
        coeff = jnp.where(lanes < SLOTS, coeff, pltpu.roll(coeff, SLOTS, 1))
        lhs[...] = both_parts(coeff, 0)

        def body(i, carry):
            rr, rw = carry
            pl.when(i == BREAK)(between)
            x, y0 = place(i)
            fs, images = stencil(g, x, y0, level, ROWS)
            left = lhs[:, : 2 * SLOTS]
            for n, (f, image) in enumerate(zip(fs, images)):
                row = x * NY + y0 + n * 8
                right = jnp.concatenate([table[row + j] for j in range(8)], axis=1)
                v = jnp.dot(left, right, preferred_element_type=F32)
                v = v[:8] + v[8:]
                blocks = [image[j] + v[:, j * NZ : (j + 1) * NZ] for j in range(8)]
                for j in range(8):
                    w[k % 2, g, x, y0 + n * 8 + j] = blocks[j]
                rr = rr + tree(f * f)
                rw = rw + tree([f[j] * blocks[j] for j in range(8)])
            return rr, rw

        rr, rw = lax.fori_loop(0, SX * NY // ROWS, body, (none, none))
        send_sums(k, g, rr, rw)
        send_halo(k, g)

        def images(i, acc):
            for n in range(4):
                blocks = [w[k % 2, g, i, n * 8 + j] for j in range(8)]
                acc = project(blocks, i * NY + n * 8, acc)
            return acc

        acc = lax.fori_loop(0, SX, images, jnp.zeros((16, 2 * SLOTS), F32))
        send_projections(k + 1, g, acc)

    def last(g):
        level = level_of(g)

        def body(i, carry):
            rr, rw = carry
            x, y0 = place(i)

            @pl.when(x == SX - HALF)
            def _():
                for j in range(HALF):
                    r[g, SX + HALO + j, inner] = jnp.zeros((NY, 8, NZ), F32)

            for f, image in zip(*stencil(g, x, y0, level, ROWS)):
                rr, rw = rr + tree(f * f), rw + tree(f * image)
            return rr, rw

        rr, rw = lax.fori_loop(0, SX * NY // ROWS, body, (none, none))
        own = (lanes >= ATOM_DEV) & (lanes < 2 * ATOM_DEV)
        t = tot[g, 0]
        rw = rw + jnp.where(own, t * t * energy[...], 0.0)
        send_sums(3, g, rr, rw)

    def update(k, g):
        alpha, beta = take_sums(k - 1, g)
        a, b = alpha[None], beta[None]

        def own(i, _):
            x = i // 4
            y0 = pl.multiple_of((i % 4) * 8, 8)
            step = w[(k - 1) % 2, g, x, pl.ds(y0, 8)]
            if k > 1:
                step = step + b * s[g, x + HALO, pl.ds(y0, 8)]
            if k < 3:
                s[g, x + HALO, pl.ds(y0, 8)] = step
            new = r[g, x + HALO, pl.ds(y0 + HALO, 8)] - a * step
            r[g, x + HALO, pl.ds(y0 + HALO, 8)] = new
            if k < 3:
                hist[k - 1, g, x, pl.ds(y0, 8)] = new
            return 0

        lax.fori_loop(0, SX * 4, own, 0)
        take_halo(k - 1, g)

        if k < 3:

            def side(i, _):
                x = i // 4
                y0 = pl.multiple_of((i % 4) * 8, 8)
                to = jnp.where(x < HALO, x, x + SX)
                step = hb[k - 1, g, x, pl.ds(y0, 8)]
                if k > 1:
                    step = step + b * s[g, to, pl.ds(y0, 8)]
                s[g, to, pl.ds(y0, 8)] = step
                r[g, to, pl.ds(y0 + HALO, 8)] = r[g, to, pl.ds(y0 + HALO, 8)] - a * step
                return 0

            lax.fori_loop(0, 2 * HALO * 4, side, 0)
        else:
            def near_side(i, _):
                x = i // 4
                y0 = pl.multiple_of((i % 4) * 8, 8)
                to = jnp.where(x < HALF, x + HALF, x + SX + HALO - HALF)
                step = hb2[g, x, pl.ds(y0, 8)] + b * s[g, to, pl.ds(y0, 8)]
                new = r[g, to, pl.ds(y0 + HALO, 8)] - a * step
                r[g, to, pl.ds(y0 + HALO, 8)] = new + new
                return 0

            lax.fori_loop(0, 2 * HALF * 4, near_side, 0)

            def far_side(i, _):
                plane = jnp.zeros((NY, 8, NZ), F32)
                r[g, i, inner] = plane
                r[g, EXT - 1 - i, inner] = plane
                return 0

            lax.fori_loop(0, HALF, far_side, 0)

    def update_projections(k, g):
        t = gathered_projections(k, g)
        if k > 1:
            t = t + scal[g, 3 + k] * tot[g, 1]
        tot[g, 1] = t
        tot[g, 0] = tot[g, 0] - scal[g, k - 1] * t

    def each(body):
        def run(g, _):
            body(g)
            return 0

        lax.fori_loop(0, 2, run, 0)

    def begin(i, acc):
        x = i // 4
        y0 = pl.multiple_of((i % 4) * 8, 8)
        row = pl.multiple_of(i * 8, 8)
        left = []
        for j in range(8):
            left.append(
                jnp.concatenate([both_parts(own_in[x, g, y0 + j], 0) for g in range(2)], axis=0)
            )
        right = []
        for j in range(8):
            right.append(table[row + j].astype(F32).T.astype(BF16))
            turned[pl.ds(pl.multiple_of((row + j) * NZ, NZ), NZ), :] = right[-1]
        return acc + jnp.dot(
            jnp.concatenate(left, axis=1),
            jnp.concatenate(right, axis=0),
            preferred_element_type=F32,
        )

    send_first(0)
    acc = lax.fori_loop(0, SX * NY // 8, begin, jnp.zeros((32, 2 * SLOTS), F32))
    send_projections(0, 0, acc[:16])
    send_projections(0, 1, acc[16:])
    send_first(1)

    def spread(i, _):
        rows = pot_in[pl.ds(pl.multiple_of(i * 8, 8), 8), :]
        for j in range(8):
            potb[i * 8 + j] = jnp.broadcast_to(rows[j : j + 1, :], (8, NZ))
        return 0

    lax.fori_loop(0, SX * NY // 8, spread, 0)

    def pass_on(k, g):
        forward_sums(k - 1 + g, 1 - g)

    def first(g):
        take_first(g)
        tot[g, 0] = gathered_projections(0, g)

        def between():
            @pl.when(g == 1)
            def _():
                pass_on(0, g)

        main(0, g, between)

    each(first)

    for k in (1, 2):

        def turn(g, k=k):
            update(k, g)
            update_projections(k, g)
            main(k, g, lambda: pass_on(k, g))

        each(turn)
        each(lambda g, k=k: halo_sent(k - 1, g))

    each(first_sent)

    def closing(g):
        update(3, g)
        update_projections(3, g)
        pass_on(3, g)
        last(g)

    each(closing)
    forward_sums(3, 1)
    each(lambda g: halo_sent(2, g))

    def finish(g):
        a3, b3 = take_sums(3, g)
        g3 = a3
        g2 = scal[g, 2] + b3 * g3
        g1 = scal[g, 1] + scal[g, 6] * g2
        g0 = scal[g, 0] + scal[g, 5] * g1

        def body(i, _):
            x = i // 4
            y0 = pl.multiple_of((i % 4) * 8, 8)
            value = (
                g0[None] * own_in[x, g, pl.ds(y0, 8)]
                + g1[None] * hist[0, g, x, pl.ds(y0, 8)]
                + g2[None] * hist[1, g, x, pl.ds(y0, 8)]
                + g3[None] * r[g, x + HALO, pl.ds(y0 + HALO, 8)]
            )
            x_out[x, g, pl.ds(y0, 8)] = value
            part = 4.0 * jnp.sum(value * orb[x, g, pl.ds(y0, 8)], axis=1)
            dens[x, pl.ds(y0, 8), :] = jnp.where(g == 0, part, dens[x, pl.ds(y0, 8), :] + part)
            return 0

        lax.fori_loop(0, SX * 4, body, 0)

    def clear_dens(i, _):
        dens[i] = jnp.zeros((NY, NZ), F32)
        return 0

    lax.fori_loop(0, SX, clear_dens, 0)
    each(finish)

    def rows_of(block):
        return pl.ds(pl.multiple_of(block * (NY // blocks_st), NY // blocks_st), NY // blocks_st)

    def block_copy(i, source):
        return pltpu.make_async_remote_copy(
            src_ref=dens.at[:, rows_of(other_block(i)), :],
            dst_ref=parts.at[source],
            send_sem=d_send.at[i],
            recv_sem=d_recv.at[i],
            device_id={"st": other_block(i)},
        )

    for i in range(1, blocks_st):
        block_copy(i, me).start()
    parts[me] = dens[:, rows_of(me), :]
    for i in range(1, blocks_st):
        block_copy(i, (me + blocks_st - i) % blocks_st).wait_recv()
    total = parts[0]
    for i in range(1, blocks_st):
        total = total + parts[i]
    dens_out[...] = total
    for i in range(1, blocks_st):
        block_copy(i, me).wait_send()


def solve(table, orb, pot, pert, lev, kb, tz, blocks_st):
    vmem = pl.BlockSpec(memory_space=pltpu.VMEM)
    dma = pltpu.SemaphoreType.DMA
    return pl.pallas_call(
        solve_kernel,
        out_shape=(
            jax.ShapeDtypeStruct((SX, 2, NY, 8, NZ), F32),
            jax.ShapeDtypeStruct((SX, NY // blocks_st, NZ), F32),
        ),
        in_specs=[vmem] * 4 + [pl.BlockSpec(memory_space=pltpu.SMEM)] * 2 + [vmem],
        out_specs=(vmem, vmem),
        scratch_shapes=[
            pltpu.VMEM((1, NZ), F32),
            pltpu.VMEM((SX, 2, NY, 8, NZ), F32),
            pltpu.VMEM((SX * NY * NZ, 2 * SLOTS), BF16),
            pltpu.VMEM((2, EXT, NYP, 8, NZ), F32),
            pltpu.VMEM((2, EXT, NY, 8, NZ), F32),
            pltpu.VMEM((2, 2, SX, NY, 8, NZ), F32),
            pltpu.VMEM((2, 2, 2 * HALO, NY, 8, NZ), F32),
            pltpu.VMEM((2, HALO, NY, 8, NZ), F32),
            pltpu.VMEM((2, 2, SX, NY, 8, NZ), F32),
            pltpu.VMEM((SX * NY, 8, NZ), F32),
            pltpu.VMEM((4, 2, PLANE, 8, NZ), F32),
            pltpu.VMEM((4, 2, DEPTH, 8, NZ), F32),
            pltpu.VMEM((4, 2, 4, 8, NZ), F32),
            pltpu.VMEM((4, 2, 2, 8, NZ), F32),
            pltpu.VMEM((4, 2, 8, NZ), F32),
            pltpu.VMEM((2, 12, 8, NZ), F32),
            pltpu.VMEM((2, 2, 8, NZ), F32),
            pltpu.VMEM((16, NZ), BF16),
            pltpu.VMEM((SX, NY, NZ), F32),
            pltpu.VMEM((blocks_st, SX, NY // blocks_st, NZ), F32),
            dma((4, 2, 2)),
            dma((4, 2, 2)),
            dma((2, PLANE)),
            dma((2, 2, PLANE)),
            dma((2, DEPTH)),
            dma((2, 2, DEPTH)),
            dma((2, 4)),
            dma((2, 2, 4)),
            dma((blocks_st,)),
            dma((blocks_st,)),
        ],
        compiler_params=pltpu.CompilerParams(
            collective_id=0, has_side_effects=True, vmem_limit_bytes=VMEM_MIB * 2**20
        ),
        name="bicg_solve",
    )(table, orb, pot, pert, lev, kb, tz)


def shards(orbitals, levels, potential, perturbation, projector, point_cell, point_atom, kb_energy):
    index = lax.axis_index("dom")
    row = (point_cell >> 7) * SLOTS + point_atom - (index - 1) * ATOM_DEV
    place = jnp.where(point_atom >= 0, row * NZ + (point_cell & 127), UNUSED)
    table, orb = build_table(projector, place, orbitals)
    tz = jnp.asarray(depth_matrix())
    turned, density = solve(
        table, orb, potential.reshape(SX * NY, NZ), perturbation.reshape(SX * NY, NZ),
        levels, kb_energy, tz,
        lax.axis_size("st"),
    )
    response = turned.transpose(1, 3, 0, 2, 4).reshape(orbitals.shape)
    return response, density


def solution(mesh):
    in_specs = (
        P("st", "dom", None, None),
        P("st"),
        P("dom", None, None),
        P("dom", None, None),
        P("dom"),
        P("dom"),
        P("dom"),
        P(),
    )
    out_specs = (P("st", "dom", None, None), P("dom", "st", None))
    return jax.shard_map(shards, mesh=mesh, in_specs=in_specs, out_specs=out_specs, check_vma=False)
```
